256 devices in a mesh: seq: 8 (over y, x_lo), tp: 32 (over z, x_hi, core).
Axes of the slice: x: 4 (x_hi: 2, x_lo: 2; x = x_hi * 2 + x_lo), y: 4, z: 8, core: 2. Of those that a mesh axis runs over, the one named last changes fastest.
Arguments:
- projected: bfloat16 [3, 8192, 8192], P(None, 'seq', 'tp'), may hold values from -6 to 6
- short_filter: float32 [3, 3, 8192], P(None, None, 'tp'), may hold values from -2.5 to 2.5
- residue: float32 [512, 16], P('tp'), may hold values from -1.5 to 1.5
- rate: float32 [512, 16], P('tp'), may hold values from 0 to 1, as said below
- out_weight: bfloat16 [8192, 8192], P('tp'), may hold values from -0.0625 to 0.0625
Outputs:
- output: bfloat16 [8192, 8192], P(('seq', 'tp'))
The draws below stay inside these ranges and needn't reach their ends.
Inputs may be any that keep to these rules, and one draw needn't show every extreme that they name: Every rate is positive.
All inputs are finite; a program needn't handle non-finite values.
Results may differ from the reference program's by a relative error of at most 0.02.
Values may be sent and summed in bfloat16 or wider, within the bound.
No kernel may reach another device: no remote copies, remote signals or barrier semaphores. Data moves between devices by JAX's collectives and lax.ppermute only.
A program may use at most 128 MiB of HBM per device.

```python
import jax
import jax.numpy as jnp
from jax import lax

D = 8192
GROUP = 16
MODES = 16
SEQ_LEN = 8192
GROUPS = 512


def draw_rate(key, part):
    lowest = jnp.log(0.02 / SEQ_LEN)
    highest = jnp.log(1.0 / 30.0)
    spread = jax.random.uniform(key, (GROUPS, MODES), jnp.float32)
    logged = lowest + spread * (highest - lowest)
    return jnp.exp(logged).astype(jnp.float32)


def levels(own_key, shape, shards, least, high):
    def one(dim, blocks):
        heights = jax.random.uniform(jax.random.fold_in(jax.random.fold_in(own_key, 6), dim), (blocks,), jnp.float32, least / len(shards), high / len(shards))
        return jnp.repeat(jnp.exp(heights), shape[dim] // blocks).reshape((-1,) + (1,) * (len(shape) - dim - 1))

    loudness = one(*shards[0])
    for cut in shards[1:]:
        loudness = loudness * one(*cut)
    return loudness


def centred(rng, shape, deviation, bound, shards=(), kind=jnp.bfloat16):
    entries = jax.random.normal(rng, shape, jnp.float32) * deviation
    if len(shards) > 0:
        entries = levels(rng, shape, shards, -0.22, 0.18) * entries
    return jnp.clip(entries, min=-bound, max=bound).astype(kind)


def setup_inputs(seed: int = 0) -> dict:
    seeds = jax.random.split(jax.random.key(seed), 6)
    projected = centred(seeds[0], (3, SEQ_LEN, D), 1.0, 6.0, ((1, 8), (2, 32)))
    short_filter = centred(seeds[1], (3, 3, D), 0.5, 2.5, ((2, 32),), jnp.float32)
    residue = centred(seeds[2], (GROUPS, MODES), 0.25, 1.5, ((0, 32),), jnp.float32)
    rate = draw_rate(jax.random.fold_in(seeds[5], 71), 0)
    out_weight = centred(seeds[4], (D, D), D ** -0.5, 0.0625, ((0, 32),))
    return dict(projected=projected, short_filter=short_filter, residue=residue, rate=rate, out_weight=out_weight)


def filter_tables(rate, residue, block_len):
    mode_weight = residue * jnp.sqrt(-jnp.expm1(-2.0 * rate))
    offsets = lax.iota(jnp.int32, block_len)
    lag_float = offsets.astype(jnp.float32)
    powers = jnp.exp(-rate[None, :, :] * lag_float[:, None, None])
    kernel = jnp.einsum('tgn,gn->gt', powers, mode_weight, precision=lax.Precision.HIGHEST)
    lagged = offsets[:, None] - offsets[None, :]
    clipped = jnp.clip(lagged, 0, block_len - 1).astype(jnp.int32)
    toeplitz = jnp.where(lagged[None] >= 0, kernel[:, clipped], jnp.float32(0.0))
    decay_into = jnp.exp(-rate[None, :, :] * (lag_float[:, None, None] + 1.0)) * mode_weight[None]
    decay_out = jnp.exp(-rate[None, :, :] * (block_len - 1.0 - lag_float)[:, None, None])
    block_power = jnp.exp(-rate * block_len)
    return (toeplitz, decay_into, decay_out, block_power)

def causal_conv(signal, tables, state_start):
    toeplitz, decay_into, decay_out, block_power = tables
    block_len = toeplitz.shape[1]
    row_count, group_count, group_width = signal.shape
    segments = signal.reshape(row_count // block_len, block_len, group_count, group_width)

    def advance(state_in, segment):
        within = jnp.einsum('gts,sgi->tgi', toeplitz, segment, precision=lax.Precision.HIGHEST)
        carried = jnp.einsum('tgn,gni->tgi', decay_into, state_in, precision=lax.Precision.HIGHEST)
        state_next = block_power[:, :, None] * state_in + jnp.einsum('tgn,tgi->gni', decay_out, segment, precision=lax.Precision.HIGHEST)
        return (state_next, within + carried)
    state_end, outputs = lax.scan(advance, state_start, segments)
    return (outputs.reshape(row_count, group_count, group_width), state_end)

def featurize(projected, short_filter):
    values = projected.astype(jnp.float32)
    length = values.shape[1]
    padded = jnp.concatenate([jnp.zeros((3, 2, values.shape[2]), jnp.float32), values], axis=1)
    return short_filter[:, 0, None, :] * padded[:, 2:] + short_filter[:, 1, None, :] * padded[:, 1:length + 1] + short_filter[:, 2, None, :] * padded[:, 0:length]

def reference(projected, short_filter, residue, rate, out_weight):
    featured = featurize(projected, short_filter)
    signal = featured[1] * featured[2]
    length = signal.shape[0]
    tables = filter_tables(rate, residue, min(256, length))
    grouped = signal.reshape(length, GROUPS, GROUP)
    conv = causal_conv(grouped, tables, jnp.zeros((GROUPS, MODES, GROUP), jnp.float32))[0]
    mixed = (featured[0] * conv.reshape(length, D)).astype(jnp.bfloat16)
    return jnp.dot(mixed, out_weight, preferred_element_type=jnp.float32).astype(jnp.bfloat16)
```

```python
import jax
import jax.numpy as jnp
from jax import lax
from jax.experimental import pallas as pl
from jax.experimental.pallas import tpu as pltpu
from jax.sharding import Mesh, PartitionSpec as P

GROUP = 16
MODES = 16
CHUNK = 128
LANES = 128
BF = jnp.bfloat16
F32 = jnp.float32
VM = pl.BlockSpec(memory_space=pltpu.VMEM)
SM = pl.BlockSpec(memory_space=pltpu.SMEM)


def iota(shape, dim):
    return lax.broadcasted_iota(jnp.int32, shape, dim)


def spread(state):
    width = state.shape[1]
    groups = width // GROUP
    tall = jnp.concatenate([state] * groups, axis=0)
    shape = (groups * MODES, width)
    own = iota(shape, 0) // MODES == iota(shape, 1) // GROUP
    return jnp.where(own, tall, 0.0).astype(BF)


def conv_kernel(p_ref, halo_ref, sf_ref, rcol_ref, wcol_ref, rrow_ref, wrow_ref, rt_ref,
                y_ref, q_ref, end_ref, din_ref, table, masked):
    rows, channels = p_ref.shape[1], p_ref.shape[2]
    halves = channels // LANES
    per_half = LANES // GROUP
    groups = channels // GROUP
    rcol = rcol_ref[...]
    wcol = wcol_ref[...]
    lane = iota((groups * MODES, CHUNK), 1)
    back = jnp.where(lane == 0, 0, CHUNK - lane).astype(F32)
    taps = (wcol * jnp.exp(-rcol * back)).reshape(groups, MODES, CHUNK).sum(axis=1)
    leave = jnp.exp(-rcol * (CHUNK - 1 - lane).astype(F32)).astype(BF)
    causal = iota((CHUNK, CHUNK), 0) >= iota((CHUNK, CHUNK), 1)
    for g in range(groups):
        wide = jnp.broadcast_to(taps[g : g + 1, :], (CHUNK, CHUNK))
        turned = pltpu.roll(wide, 0, 1, stride=1, stride_axis=0)
        table[0:CHUNK, g * CHUNK : (g + 1) * CHUNK] = jnp.where(causal, turned, 0.0).astype(BF)
        table[CHUNK : CHUNK + MODES, g * CHUNK : (g + 1) * CHUNK] = leave[g * MODES : (g + 1) * MODES]
    steps = (iota((CHUNK, groups * MODES), 0) + 1).astype(F32)
    din = (wrow_ref[...] * jnp.exp(-rrow_ref[...] * steps)).astype(BF)
    din_ref[...] = din
    power = jnp.exp(-rt_ref[...] * float(CHUNK))
    group_lane = iota((CHUNK, LANES), 1) // GROUP

    def featured(i, q):
        cur = p_ref[i, q * CHUNK : (q + 1) * CHUNK, :].astype(F32)
        if q == 0:
            before = halo_ref[i].astype(F32)
        else:
            before = p_ref[i, q * CHUNK - 16 : q * CHUNK, :].astype(F32)
        ext = jnp.concatenate([before, cur], axis=0)
        skip = before.shape[0]
        one = pltpu.roll(ext, 1, 0)[skip:]
        two = pltpu.roll(ext, 2, 0)[skip:]
        return sf_ref[i, 0:1, :] * cur + sf_ref[i, 1:2, :] * one + sf_ref[i, 2:3, :] * two

    state = jnp.zeros((MODES, channels), F32)
    for pair in range(rows // (2 * CHUNK)):
        for j in range(2):
            q = 2 * pair + j
            q_ref[q * CHUNK : (q + 1) * CHUNK, :] = featured(0, q)
            signal = (featured(1, q) * featured(2, q)).astype(BF)
            for h in range(halves):
                part = signal[:, h * LANES : (h + 1) * LANES]
                for g in range(per_half):
                    masked[h, g * CHUNK : (g + 1) * CHUNK, j * LANES : (j + 1) * LANES] = jnp.where(
                        group_lane == g, part, jnp.zeros_like(part)
                    )
        span = per_half * CHUNK
        made = [
            jnp.dot(table[:, h * span : (h + 1) * span], masked[h], preferred_element_type=F32)
            for h in range(halves)
        ]
        for j in range(2):
            q = 2 * pair + j
            full = jnp.concatenate([m[:, j * LANES : (j + 1) * LANES] for m in made], axis=1)
            within = full[:CHUNK]
            if q > 0:
                within = within + jnp.dot(din, spread(state), preferred_element_type=F32)
            y_ref[q * CHUNK : (q + 1) * CHUNK, :] = within
            state = power * state + full[CHUNK:]
    end_ref[...] = state


def mix_kernel(at_ref, ends_ref, rt_ref, din_ref, y_ref, q_ref, mixed_ref):
    rows = y_ref.shape[0]
    here = at_ref[0]
    block_power = jnp.exp(-rt_ref[...] * float(rows))
    state = jnp.zeros(rt_ref.shape, F32)
    for j in range(ends_ref.shape[0]):
        state = jnp.where(j < here, block_power * state + ends_ref[j], state)
    power = jnp.exp(-rt_ref[...] * float(CHUNK))
    din = din_ref[...]
    for q in range(rows // CHUNK):
        span = slice(q * CHUNK, (q + 1) * CHUNK)
        carried = jnp.dot(din, spread(state), preferred_element_type=F32)
        mixed_ref[span, :] = (q_ref[span, :] * (y_ref[span, :] + carried)).astype(BF)
        state = power * state


def product_kernel(at_ref, a0, a1, a2, a3, w0, w1, m1, r1, r2, r3, m2, c_ref, wx):
    y, mine = at_ref[1], at_ref[2]
    piece = m1.shape[1]
    tail = m2.shape[1]

    @pl.when(pl.program_id(0) == 0)
    def _():
        for k, ref in enumerate((m1, r1, r2, r3)):
            start = pl.multiple_of(lax.rem(y - k + 4, 4) * piece, 16)
            for s in range(2):
                wx[s, pl.ds(start, piece), :] = ref[s]
        for s in range(2):
            wx[s, 4 * piece : 4 * piece + tail, :] = m2[s]

    tile = 512
    for n in range(c_ref.shape[1] // tile):
        cols = slice(n * tile, (n + 1) * tile)
        total = jnp.dot(a0[...], w0[:, cols], preferred_element_type=F32)
        total += jnp.dot(a1[...], w1[:, cols], preferred_element_type=F32)
        total += jnp.dot(a2[...], wx[0, :, cols], preferred_element_type=F32)
        total += jnp.dot(a3[...], wx[1, :, cols], preferred_element_type=F32)
        total = total.astype(BF)
        for b in range(total.shape[0] // 32):
            high, low = b // 4, b % 4
            place = pl.multiple_of((high * 4 + jnp.bitwise_xor(low, mine)) * 32, 32)
            c_ref[pl.ds(place, 32), cols] = total[b * 32 : (b + 1) * 32]


def join_kernel(at_ref, p0, p1, p2, p3, out_ref):
    mine = at_ref[2]
    width = p0.shape[1]
    for k, ref in enumerate((p0, p1, p2, p3)):
        place = pl.multiple_of(jnp.bitwise_xor(mine, k) * width, width)
        out_ref[:, pl.ds(place, width)] = ref[...]


def other_core(value):
    return lax.ppermute(value, "c", [(0, 1), (1, 0)])


def local(projected, short_filter, residue, rate, out_weight):
    rows, channels = projected.shape[1], projected.shape[2]
    groups = rate.shape[0]
    width = out_weight.shape[1] // 4
    y, xh, core = lax.axis_index("y"), lax.axis_index("xh"), lax.axis_index("c")
    seq = lax.axis_index(("y", "xl"))
    at = jnp.stack([seq, y, xh * 2 + core]).astype(jnp.int32)

    halo = lax.ppermute(projected[:, rows - 8 :, :], ("y", "xl"), [(i, i + 1) for i in range(7)])

    def columns(h, k):
        return lax.dynamic_slice(out_weight, (0, (h * 2 + k) * width), (channels, width))

    w_mine = columns(xh, core)
    o_mine = columns(1 - xh, core)
    o_other = other_core(columns(1 - xh, 1 - core))
    w_other = other_core(columns(xh, 1 - core))
    piece = 48
    mirror = [(0, 3), (3, 0), (1, 2), (2, 1)]

    def rows_of(start, size):
        return jnp.stack([lax.dynamic_slice(v, (start, 0), (size, width)) for v in (o_mine, o_other)])

    m1 = lax.ppermute(rows_of(y * piece, piece), ("xl", "xh"), mirror)
    m2 = lax.ppermute(rows_of(4 * piece, channels - 4 * piece), ("xl", "xh"), mirror)
    r1, r2, r3 = (lax.ppermute(m1, "y", [(i, (i + k) % 4) for i in range(4)]) for k in (1, 2, 3))

    weight = residue * jnp.sqrt(-jnp.expm1(-2.0 * rate))
    rt = jnp.repeat(rate.T, GROUP, axis=1)
    flat = groups * MODES
    conv, query, end, din = pl.pallas_call(
        conv_kernel,
        out_shape=(
            jax.ShapeDtypeStruct((rows, channels), F32),
            jax.ShapeDtypeStruct((rows, channels), F32),
            jax.ShapeDtypeStruct((MODES, channels), F32),
            jax.ShapeDtypeStruct((CHUNK, flat), BF),
        ),
        in_specs=[VM] * 8,
        out_specs=(VM, VM, VM, VM),
        scratch_shapes=[
            pltpu.VMEM((CHUNK + MODES, groups * CHUNK), BF),
            pltpu.VMEM((channels // LANES, LANES // GROUP * CHUNK, 2 * LANES), BF),
        ],
        cost_estimate=pl.CostEstimate(flops=2 * 10**9, bytes_accessed=4 * 2**20, transcendentals=10**5),
        name="conv",
    )(
        projected, halo, short_filter,
        rate.reshape(flat, 1), weight.reshape(flat, 1), rate.reshape(1, flat), weight.reshape(1, flat), rt,
    )
    ends = lax.all_to_all(jnp.broadcast_to(end[None], (8,) + end.shape), ("y", "xl"), 0, 0, tiled=True)
    mixed = pl.pallas_call(
        mix_kernel,
        out_shape=jax.ShapeDtypeStruct((rows, channels), BF),
        in_specs=[SM] + [VM] * 5,
        out_specs=VM,
        cost_estimate=pl.CostEstimate(flops=2 * 10**8, bytes_accessed=3 * 2**20, transcendentals=10**4),
        name="mix",
    )(at, ends, rt, din, conv, query)

    a_far = lax.ppermute(mixed, "xh", [(0, 1), (1, 0)])
    a_other = other_core(mixed)
    a_far_other = other_core(a_far)

    block = 256
    a_spec = pl.BlockSpec((block, channels), lambda i: (i, 0))

    def whole(shape):
        return pl.BlockSpec(shape, lambda i: (0,) * len(shape))

    partial = pl.pallas_call(
        product_kernel,
        out_shape=jax.ShapeDtypeStruct((rows, width), BF),
        grid=(rows // block,),
        in_specs=[SM] + [a_spec] * 4 + [whole((channels, width))] * 2 + [whole(m1.shape)] * 4 + [whole(m2.shape)],
        out_specs=pl.BlockSpec((block, width), lambda i: (i, 0)),
        scratch_shapes=[pltpu.VMEM((2, channels, width), BF)],
        cost_estimate=pl.CostEstimate(flops=4 * 10**9, bytes_accessed=10 * 2**20, transcendentals=0),
        name="product",
    )(at, mixed, a_other, a_far, a_far_other, w_mine, w_other, m1, r1, r2, r3, m2)

    summed = lax.psum_scatter(partial, "z", scatter_dimension=0, tiled=True)
    size = summed.shape[0] // 4

    def traded(k):
        pairs = [(i, i ^ k) for i in range(4)]
        return lax.ppermute(summed[k * size : (k + 1) * size], ("xh", "c"), pairs)

    return pl.pallas_call(
        join_kernel,
        out_shape=jax.ShapeDtypeStruct((size, 4 * width), BF),
        in_specs=[SM] + [VM] * 4,
        out_specs=VM,
        name="join",
    )(at, summed[:size], traded(1), traded(2), traded(3))


def solution(mesh):
    fine = Mesh(mesh.devices.reshape(4, 2, 8, 2, 2), ("y", "xl", "z", "xh", "c"))
    seq, tp = ("y", "xl"), ("z", "xh", "c")
    placed = (P(None, seq, tp), P(None, None, tp), P(tp, None), P(tp, None), P(tp, None))
    return jax.shard_map(local, mesh=fine, in_specs=placed, out_specs=P(seq + tp, None), check_vma=False)
```

```python
import jax
import jax.numpy as jnp
from jax import lax
from jax.experimental import pallas as pl
from jax.experimental.pallas import tpu as pltpu
from jax.sharding import Mesh, PartitionSpec as P

GROUP = 16
MODES = 16
CHUNK = 128
LANES = 128
BF = jnp.bfloat16
F32 = jnp.float32
VM = pl.BlockSpec(memory_space=pltpu.VMEM)
SM = pl.BlockSpec(memory_space=pltpu.SMEM)


def iota(shape, dim):
    return lax.broadcasted_iota(jnp.int32, shape, dim)


def spread(state):
    width = state.shape[1]
    groups = width // GROUP
    tall = jnp.concatenate([state] * groups, axis=0)
    shape = (groups * MODES, width)
    own = iota(shape, 0) // MODES == iota(shape, 1) // GROUP
    return jnp.where(own, tall, 0.0).astype(BF)


def one_hot(rows, columns, row_size, column_size):
    shape = (rows, columns)
    return (iota(shape, 0) // row_size == iota(shape, 1) // column_size).astype(F32)


def exact_dot(a, b, dims):
    return lax.dot_general(a, b, (dims, ((), ())), precision=lax.Precision.HIGHEST, preferred_element_type=F32)


def by_channel(table, channels):
    return exact_dot(table, one_hot(table.shape[0], channels, 1, GROUP), ((0,), (0,)))


def by_row(table):
    flat = table.shape[0] * MODES
    wide = exact_dot(one_hot(flat, table.shape[0], MODES, 1), table, ((1,), (0,)))
    keep = iota((flat, MODES), 0) % MODES == iota((flat, MODES), 1)
    return jnp.where(keep, wide, 0.0).sum(axis=1, keepdims=True)


def by_lane(table):
    flat = table.shape[0] * MODES
    wide = exact_dot(table, one_hot(table.shape[0], flat, 1, MODES), ((0,), (0,)))
    keep = iota((MODES, flat), 1) % MODES == iota((MODES, flat), 0)
    return jnp.where(keep, wide, 0.0).sum(axis=0, keepdims=True)


def tapped(taps, cur, before):
    ext = jnp.concatenate([before, cur], axis=0)
    skip = before.shape[0]
    one = pltpu.roll(ext, 1, 0)[skip:]
    two = pltpu.roll(ext, 2, 0)[skip:]
    return taps[0:1, :] * cur + taps[1:2, :] * one + taps[2:3, :] * two


def state_kernel(k_ref, v_ref, halo_ref, sf_ref, rate_ref, x_ref, end_ref, rt_ref, tail, total, power):
    step = pl.program_id(0)
    rows, channels = k_ref.shape

    @pl.when(step == 0)
    def _():
        rt = by_channel(rate_ref[...], channels)
        rt_ref[...] = rt
        total[...] = jnp.zeros_like(total)
        for n in range(MODES):
            power[n] = jnp.broadcast_to(jnp.exp(-8.0 * rt[n : n + 1, :]), (8, channels))
        for i in range(2):
            tail[i] = halo_ref[i + 1].astype(F32)

    featured = []
    for i, ref in enumerate((k_ref, v_ref)):
        cur = ref[...].astype(F32)
        featured.append(tapped(sf_ref[i + 1], cur, tail[i]))
        tail[i] = cur[rows - 8 :]
    signal = featured[0] * featured[1]
    x_ref[...] = signal.astype(BF)
    for h in range(channels // LANES):
        lanes = slice(h * LANES, (h + 1) * LANES)
        for first in range(0, MODES, 8):
            sums = [total[n, :, lanes] for n in range(first, first + 8)]
            powers = [power[n, :, lanes] for n in range(first, first + 8)]
            for b in range(rows // 8):
                block = signal[b * 8 : (b + 1) * 8, lanes]
                sums = [s * w + block for s, w in zip(sums, powers)]
            for n in range(8):
                total[first + n, :, lanes] = sums[n]

    @pl.when(step == pl.num_programs(0) - 1)
    def _():
        rt = rt_ref[...]
        ahead = (7 - iota((8, channels), 0)).astype(F32)
        end = jnp.concatenate(
            [
                (total[n] * jnp.exp(-ahead * rt[n : n + 1, :])).sum(axis=0, keepdims=True)
                for n in range(MODES)
            ],
            axis=0,
        )
        for j in range(end_ref.shape[0]):
            end_ref[j] = end


def conv_kernel(p_ref, x_ref, halo_ref, sf_ref, rate_ref, weight_ref, rt_ref,
                y_ref, q_ref, din_ref, table, masked):
    rows, channels = x_ref.shape
    halves = channels // LANES
    per_half = LANES // GROUP
    groups = channels // GROUP
    rate, weight = rate_ref[...], weight_ref[...]
    rcol = by_row(rate)
    wcol = by_row(weight)
    lane = iota((groups * MODES, CHUNK), 1)
    back = jnp.where(lane == 0, 0, CHUNK - lane).astype(F32)
    taps = (wcol * jnp.exp(-rcol * back)).reshape(groups, MODES, CHUNK).sum(axis=1)
    leave = jnp.exp(-rcol * (CHUNK - 1 - lane).astype(F32)).astype(BF)
    causal = iota((CHUNK, CHUNK), 0) >= iota((CHUNK, CHUNK), 1)
    for g in range(groups):
        wide = jnp.broadcast_to(taps[g : g + 1, :], (CHUNK, CHUNK))
        turned = pltpu.roll(wide, 0, 1, stride=1, stride_axis=0)
        table[0:CHUNK, g * CHUNK : (g + 1) * CHUNK] = jnp.where(causal, turned, 0.0).astype(BF)
        table[CHUNK : CHUNK + MODES, g * CHUNK : (g + 1) * CHUNK] = leave[g * MODES : (g + 1) * MODES]
    steps = (iota((CHUNK, groups * MODES), 0) + 1).astype(F32)
    din = (by_lane(weight) * jnp.exp(-by_lane(rate) * steps)).astype(BF)
    din_ref[...] = din
    power = jnp.exp(-rt_ref[...] * float(CHUNK))
    group_lane = iota((CHUNK, LANES), 1) // GROUP

    state = jnp.zeros((MODES, channels), F32)
    for pair in range(rows // (2 * CHUNK)):
        for j in range(2):
            q = 2 * pair + j
            span = slice(q * CHUNK, (q + 1) * CHUNK)
            before = halo_ref[0] if q == 0 else p_ref[q * CHUNK - 16 : q * CHUNK, :]
            q_ref[span, :] = tapped(sf_ref[0], p_ref[span, :].astype(F32), before.astype(F32))
            for h in range(halves):
                part = x_ref[span, h * LANES : (h + 1) * LANES]
                for g in range(per_half):
                    masked[h, g * CHUNK : (g + 1) * CHUNK, j * LANES : (j + 1) * LANES] = jnp.where(
                        group_lane == g, part, jnp.zeros_like(part)
                    )
        depth = per_half * CHUNK
        made = [
            jnp.dot(table[:, h * depth : (h + 1) * depth], masked[h], preferred_element_type=F32)
            for h in range(halves)
        ]
        for j in range(2):
            q = 2 * pair + j
            full = jnp.concatenate([m[:, j * LANES : (j + 1) * LANES] for m in made], axis=1)
            within = full[:CHUNK]
            if q > 0:
                within = within + jnp.dot(din, spread(state), preferred_element_type=F32)
            y_ref[q * CHUNK : (q + 1) * CHUNK, :] = within
            state = power * state + full[CHUNK:]


def mix_kernel(at_ref, ends_ref, rt_ref, din_ref, y_ref, q_ref, mixed_ref):
    rows = y_ref.shape[0]
    here = at_ref[0]
    block_power = jnp.exp(-rt_ref[...] * float(rows))
    state = jnp.zeros(rt_ref.shape, F32)
    for j in range(ends_ref.shape[0]):
        state = jnp.where(j < here, block_power * state + ends_ref[j], state)
    power = jnp.exp(-rt_ref[...] * float(CHUNK))
    din = din_ref[...]
    for q in range(rows // CHUNK):
        span = slice(q * CHUNK, (q + 1) * CHUNK)
        carried = jnp.dot(din, spread(state), preferred_element_type=F32)
        mixed_ref[span, :] = (q_ref[span, :] * (y_ref[span, :] + carried)).astype(BF)
        state = power * state


def product_kernel(at_ref, a0, a1, a2, a3, w0, w1, m1, r1, r2, r3, m2, c_ref, left, right):
    y, mine = at_ref[1], at_ref[2]
    depth = w0.shape[0]
    piece, tail = m1.shape[1], m2.shape[1]

    @pl.when(pl.program_id(0) == 0)
    def _():
        for k, ref in enumerate((a0, a1, a2, a3)):
            left[:, k * depth : (k + 1) * depth] = ref[...]

    right[0:depth] = w0[...]
    right[depth : 2 * depth] = w1[...]
    for s in range(2):
        base = (2 + s) * depth
        for k, ref in enumerate((m1, r1, r2, r3)):
            start = pl.multiple_of(base + lax.rem(y - k + 4, 4) * piece, 16)
            right[pl.ds(start, piece), :] = ref[s]
        right[base + 4 * piece : base + 4 * piece + tail, :] = m2[s]
    block = 256
    for m in range(left.shape[0] // block):
        total = jnp.dot(left[m * block : (m + 1) * block, :], right[...], preferred_element_type=F32).astype(BF)
        for b in range(block // 32):
            high, low = m * (block // 128) + b // 4, b % 4
            place = pl.multiple_of((high * 4 + jnp.bitwise_xor(low, mine)) * 32, 32)
            c_ref[pl.ds(place, 32), :] = total[b * 32 : (b + 1) * 32]


def join_kernel(at_ref, p0, p1, p2, p3, out_ref):
    mine = at_ref[2]
    width = p0.shape[1]
    for k, ref in enumerate((p0, p1, p2, p3)):
        place = pl.multiple_of(jnp.bitwise_xor(mine, k) * width, width)
        out_ref[:, pl.ds(place, width)] = ref[...]


def other_core(value):
    return lax.ppermute(value, "c", [(0, 1), (1, 0)])


def local(projected, short_filter, residue, rate, out_weight):
    rows, channels = projected.shape[1], projected.shape[2]
    groups = rate.shape[0]
    width = out_weight.shape[1] // 4
    y, xh, core = lax.axis_index("y"), lax.axis_index("xh"), lax.axis_index("c")
    seq = lax.axis_index(("y", "xl"))
    at = jnp.stack([seq, y, xh * 2 + core]).astype(jnp.int32)

    halo = lax.ppermute(projected[:, rows - 8 :, :], ("y", "xl"), [(i, i + 1) for i in range(7)])

    def columns(h, k):
        return lax.dynamic_slice(out_weight, (0, (h * 2 + k) * width), (channels, width))

    w_mine = columns(xh, core)
    o_mine = columns(1 - xh, core)
    o_other = other_core(columns(1 - xh, 1 - core))
    w_other = other_core(columns(xh, 1 - core))
    piece = 48
    mirror = [(0, 3), (3, 0), (1, 2), (2, 1)]

    def rows_of(start, size):
        return jnp.stack([lax.dynamic_slice(v, (start, 0), (size, width)) for v in (o_mine, o_other)])

    m1 = lax.ppermute(rows_of(y * piece, piece), ("xl", "xh"), mirror)
    m2 = lax.ppermute(rows_of(4 * piece, channels - 4 * piece), ("xl", "xh"), mirror)

    weight = residue * jnp.sqrt(-jnp.expm1(-2.0 * rate))
    flat = groups * MODES
    span = 256
    once = {"pipeline_mode": pl.Buffered(1)}

    def whole(shape):
        return pl.BlockSpec(shape, lambda i: (0,) * len(shape))

    def third(k):
        return pl.BlockSpec((None, span, channels), lambda i: (k, i, 0))

    signal, end, rt = pl.pallas_call(
        state_kernel,
        out_shape=(
            pltpu.HBM((rows, channels), BF),
            jax.ShapeDtypeStruct((8, MODES, channels), F32),
            jax.ShapeDtypeStruct((MODES, channels), F32),
        ),
        grid=(rows // span,),
        in_specs=[third(1), third(2), whole(halo.shape), whole(short_filter.shape), whole(rate.shape)],
        out_specs=(
            pl.BlockSpec((span, channels), lambda i: (i, 0)),
            whole((8, MODES, channels)),
            whole((MODES, channels)),
        ),
        scratch_shapes=[
            pltpu.VMEM((2, 8, channels), F32),
            pltpu.VMEM((MODES, 8, channels), F32),
            pltpu.VMEM((MODES, 8, channels), F32),
        ],
        compiler_params=pltpu.CompilerParams(vmem_limit_bytes=12 * 2**20),
        cost_estimate=pl.CostEstimate(flops=2 * 10**7, bytes_accessed=6 * 2**20, transcendentals=10**4),
        name="state",
    )(projected, projected, halo, short_filter, rate)
    ends = lax.all_to_all(end, ("y", "xl"), 0, 0, tiled=True)
    conv, query, din = pl.pallas_call(
        conv_kernel,
        out_shape=(
            pltpu.HBM((rows, channels), F32),
            pltpu.HBM((rows, channels), F32),
            jax.ShapeDtypeStruct((CHUNK, flat), BF),
        ),
        grid=(1,),
        in_specs=[
            pl.BlockSpec((None, rows, channels), lambda i: (0, 0, 0)),
            whole((rows, channels)), whole(halo.shape), whole(short_filter.shape),
            whole(rate.shape), whole(rate.shape), whole(rt.shape),
        ],
        out_specs=(whole((rows, channels)), whole((rows, channels)), whole((CHUNK, flat))),
        scratch_shapes=[
            pltpu.VMEM((CHUNK + MODES, groups * CHUNK), BF),
            pltpu.VMEM((channels // LANES, LANES // GROUP * CHUNK, 2 * LANES), BF),
        ],
        compiler_params=pltpu.CompilerParams(vmem_limit_bytes=20 * 2**20),
        cost_estimate=pl.CostEstimate(flops=4 * 10**9, bytes_accessed=12 * 2**20, transcendentals=10**5),
        name="conv",
    )(projected, signal, halo, short_filter, rate, weight, rt)
    ends, m1 = lax.optimization_barrier((ends, m1))
    mixed = pl.pallas_call(
        mix_kernel,
        out_shape=jax.ShapeDtypeStruct((rows, channels), BF),
        in_specs=[SM] + [VM] * 5,
        out_specs=VM,
        compiler_params=pltpu.CompilerParams(vmem_limit_bytes=12 * 2**20),
        cost_estimate=pl.CostEstimate(flops=2 * 10**8, bytes_accessed=5 * 2**20, transcendentals=10**4),
        name="mix",
    )(at, ends, rt, din, conv, query)

    r1, r2, r3 = (lax.ppermute(m1, "y", [(i, (i + k) % 4) for i in range(4)]) for k in (1, 2, 3))
    a_far = lax.ppermute(mixed, "xh", [(0, 1), (1, 0)])
    a_other = other_core(mixed)
    a_far, m2, r1, r2, r3 = lax.optimization_barrier((a_far, m2, r1, r2, r3))
    a_far_other = other_core(a_far)

    tile = 512

    def strip(shape):
        return pl.BlockSpec(shape[:-1] + (tile,), lambda i: (0,) * (len(shape) - 1) + (i,))

    partial = pl.pallas_call(
        product_kernel,
        out_shape=pltpu.HBM((rows, width), BF),
        grid=(width // tile,),
        in_specs=[SM]
        + [pl.BlockSpec((rows, channels), lambda i: (0, 0), **once)] * 4
        + [strip((channels, width))] * 2
        + [strip(m1.shape)] * 4
        + [strip(m2.shape)],
        out_specs=strip((rows, width)),
        scratch_shapes=[pltpu.VMEM((rows, 4 * channels), BF), pltpu.VMEM((4 * channels, tile), BF)],
        compiler_params=pltpu.CompilerParams(vmem_limit_bytes=28 * 2**20),
        cost_estimate=pl.CostEstimate(flops=4 * 10**9, bytes_accessed=10 * 2**20, transcendentals=0),
        name="product",
    )(at, mixed, a_other, a_far, a_far_other, w_mine, w_other, m1, r1, r2, r3, m2)

    summed = lax.psum_scatter(partial, "z", scatter_dimension=0, tiled=True)
    size = summed.shape[0] // 4

    def traded(k):
        pairs = [(i, i ^ k) for i in range(4)]
        return lax.ppermute(summed[k * size : (k + 1) * size], ("xh", "c"), pairs)

    return pl.pallas_call(
        join_kernel,
        out_shape=jax.ShapeDtypeStruct((size, 4 * width), BF),
        in_specs=[SM] + [VM] * 4,
        out_specs=VM,
        compiler_params=pltpu.CompilerParams(vmem_limit_bytes=4 * 2**20),
        name="join",
    )(at, summed[:size], traded(1), traded(2), traded(3))


def solution(mesh):
    fine = Mesh(mesh.devices.reshape(4, 2, 8, 2, 2), ("y", "xl", "z", "xh", "c"))
    seq, tp = ("y", "xl"), ("z", "xh", "c")
    placed = (P(None, seq, tp), P(None, None, tp), P(tp, None), P(tp, None), P(tp, None))
    return jax.shard_map(local, mesh=fine, in_specs=placed, out_specs=P(seq + tp, None), check_vma=False)
```

```python
import jax
import jax.numpy as jnp
from jax import lax
from jax.experimental import pallas as pl
from jax.experimental.pallas import tpu as pltpu
from jax.sharding import Mesh, PartitionSpec as P

GROUP = 16
MODES = 16
CHUNK = 128
LANES = 128
BF = jnp.bfloat16
F32 = jnp.float32
VM = pl.BlockSpec(memory_space=pltpu.VMEM)
SM = pl.BlockSpec(memory_space=pltpu.SMEM)


def iota(shape, dim):
    return lax.broadcasted_iota(jnp.int32, shape, dim)


def spread(state):
    width = state.shape[1]
    groups = width // GROUP
    tall = jnp.concatenate([state] * groups, axis=0)
    shape = (groups * MODES, width)
    own = iota(shape, 0) // MODES == iota(shape, 1) // GROUP
    return jnp.where(own, tall, 0.0).astype(BF)


def one_hot(rows, columns, row_size, column_size):
    shape = (rows, columns)
    return (iota(shape, 0) // row_size == iota(shape, 1) // column_size).astype(F32)


def exact_dot(a, b, dims):
    return lax.dot_general(a, b, (dims, ((), ())), precision=lax.Precision.HIGHEST, preferred_element_type=F32)


def by_channel(table, channels):
    return exact_dot(table, one_hot(table.shape[0], channels, 1, GROUP), ((0,), (0,)))


def by_row(table):
    flat = table.shape[0] * MODES
    wide = exact_dot(one_hot(flat, table.shape[0], MODES, 1), table, ((1,), (0,)))
    keep = iota((flat, MODES), 0) % MODES == iota((flat, MODES), 1)
    return jnp.where(keep, wide, 0.0).sum(axis=1, keepdims=True)


def by_lane(table):
    flat = table.shape[0] * MODES
    wide = exact_dot(table, one_hot(table.shape[0], flat, 1, MODES), ((0,), (0,)))
    keep = iota((MODES, flat), 1) % MODES == iota((MODES, flat), 0)
    return jnp.where(keep, wide, 0.0).sum(axis=0, keepdims=True)


def tapped(taps, cur, before):
    ext = jnp.concatenate([before, cur], axis=0)
    skip = before.shape[0]
    one = pltpu.roll(ext, 1, 0)[skip:]
    two = pltpu.roll(ext, 2, 0)[skip:]
    return taps[0:1, :] * cur + taps[1:2, :] * one + taps[2:3, :] * two


def state_kernel(k_ref, v_ref, halo_ref, sf_ref, rate_ref, x_ref, end_ref, rt_ref, tail, total, power):
    step = pl.program_id(0)
    rows, channels = k_ref.shape

    @pl.when(step == 0)
    def _():
        rt = by_channel(rate_ref[...], channels)
        rt_ref[...] = rt
        total[...] = jnp.zeros_like(total)
        for n in range(MODES):
            power[n] = jnp.broadcast_to(jnp.exp(-8.0 * rt[n : n + 1, :]), (8, channels))
        for i in range(2):
            tail[i] = halo_ref[i + 1].astype(F32)

    featured = []
    for i, ref in enumerate((k_ref, v_ref)):
        cur = ref[...].astype(F32)
        featured.append(tapped(sf_ref[i + 1], cur, tail[i]))
        tail[i] = cur[rows - 8 :]
    signal = featured[0] * featured[1]
    x_ref[...] = signal.astype(BF)
    for h in range(channels // LANES):
        lanes = slice(h * LANES, (h + 1) * LANES)
        for first in range(0, MODES, 8):
            sums = [total[n, :, lanes] for n in range(first, first + 8)]
            powers = [power[n, :, lanes] for n in range(first, first + 8)]
            for b in range(rows // 8):
                block = signal[b * 8 : (b + 1) * 8, lanes]
                sums = [s * w + block for s, w in zip(sums, powers)]
            for n in range(8):
                total[first + n, :, lanes] = sums[n]

    @pl.when(step == pl.num_programs(0) - 1)
    def _():
        rt = rt_ref[...]
        ahead = (7 - iota((8, channels), 0)).astype(F32)
        end = jnp.concatenate(
            [
                (total[n] * jnp.exp(-ahead * rt[n : n + 1, :])).sum(axis=0, keepdims=True)
                for n in range(MODES)
            ],
            axis=0,
        )
        for j in range(end_ref.shape[0]):
            end_ref[j] = end


def conv_kernel(p_ref, x_ref, halo_ref, sf_ref, rate_ref, weight_ref, rt_ref,
                y_ref, q_ref, din_ref, table, masked):
    rows, channels = x_ref.shape
    halves = channels // LANES
    per_half = LANES // GROUP
    groups = channels // GROUP
    rate, weight = rate_ref[...], weight_ref[...]
    rcol = by_row(rate)
    wcol = by_row(weight)
    lane = iota((groups * MODES, CHUNK), 1)
    back = jnp.where(lane == 0, 0, CHUNK - lane).astype(F32)
    taps = (wcol * jnp.exp(-rcol * back)).reshape(groups, MODES, CHUNK).sum(axis=1)
    leave = jnp.exp(-rcol * (CHUNK - 1 - lane).astype(F32)).astype(BF)
    causal = iota((CHUNK, CHUNK), 0) >= iota((CHUNK, CHUNK), 1)
    for g in range(groups):
        wide = jnp.broadcast_to(taps[g : g + 1, :], (CHUNK, CHUNK))
        turned = pltpu.roll(wide, 0, 1, stride=1, stride_axis=0)
        table[0:CHUNK, g * CHUNK : (g + 1) * CHUNK] = jnp.where(causal, turned, 0.0).astype(BF)
        table[CHUNK : CHUNK + MODES, g * CHUNK : (g + 1) * CHUNK] = leave[g * MODES : (g + 1) * MODES]
    steps = (iota((CHUNK, groups * MODES), 0) + 1).astype(F32)
    din = (by_lane(weight) * jnp.exp(-by_lane(rate) * steps)).astype(BF)
    din_ref[...] = din
    power = jnp.exp(-rt_ref[...] * float(CHUNK))
    group_lane = iota((CHUNK, LANES), 1) // GROUP

    state = jnp.zeros((MODES, channels), F32)
    for pair in range(rows // (2 * CHUNK)):
        for j in range(2):
            q = 2 * pair + j
            span = slice(q * CHUNK, (q + 1) * CHUNK)
            before = halo_ref[0] if q == 0 else p_ref[q * CHUNK - 16 : q * CHUNK, :]
            q_ref[span, :] = tapped(sf_ref[0], p_ref[span, :].astype(F32), before.astype(F32))
            for h in range(halves):
                part = x_ref[span, h * LANES : (h + 1) * LANES]
                for g in range(per_half):
                    masked[h, g * CHUNK : (g + 1) * CHUNK, j * LANES : (j + 1) * LANES] = jnp.where(
                        group_lane == g, part, jnp.zeros_like(part)
                    )
        depth = per_half * CHUNK
        made = [
            jnp.dot(table[:, h * depth : (h + 1) * depth], masked[h], preferred_element_type=F32)
            for h in range(halves)
        ]
        for j in range(2):
            q = 2 * pair + j
            full = jnp.concatenate([m[:, j * LANES : (j + 1) * LANES] for m in made], axis=1)
            within = full[:CHUNK]
            if q > 0:
                within = within + jnp.dot(din, spread(state), preferred_element_type=F32)
            y_ref[q * CHUNK : (q + 1) * CHUNK, :] = within
            state = power * state + full[CHUNK:]


def mix_kernel(at_ref, ends_ref, rt_ref, din_ref, y_ref, q_ref, mixed_ref, carried_state):
    rows = y_ref.shape[0]
    rt = rt_ref[...]

    @pl.when(pl.program_id(0) == 0)
    def _():
        here = at_ref[0]
        block_power = jnp.exp(-rt * float(rows * pl.num_programs(0)))
        state = jnp.zeros(rt.shape, F32)
        for j in range(ends_ref.shape[0]):
            state = jnp.where(j < here, block_power * state + ends_ref[j], state)
        carried_state[...] = state

    state = carried_state[...]
    power = jnp.exp(-rt * float(CHUNK))
    din = din_ref[...]
    for q in range(rows // CHUNK):
        span = slice(q * CHUNK, (q + 1) * CHUNK)
        carried = jnp.dot(din, spread(state), preferred_element_type=F32)
        mixed_ref[span, :] = (q_ref[span, :] * (y_ref[span, :] + carried)).astype(BF)
        state = power * state
    carried_state[...] = state


def product_kernel(at_ref, a0, a1, a2, a3, w0, w1, m1, r1, r2, r3, m2, f1, c_ref, left, right):
    y, mine = at_ref[1], at_ref[2]
    depth = w0.shape[0]
    piece, tail = m1.shape[0], m2.shape[0]

    @pl.when(pl.program_id(0) == 0)
    def _():
        for k, ref in enumerate((a0, a1, a2, a3)):
            left[:, k * depth : (k + 1) * depth] = ref[...]

    right[0:depth] = w0[...]
    right[depth : 2 * depth] = w1[...]
    for k, ref in enumerate((m1, r1, r2, r3)):
        shift = lax.rem(y - k + 4, 4) * piece
        start = pl.multiple_of(2 * depth + shift, 16)
        right[pl.ds(start, piece), :] = ref[...]
        start = pl.multiple_of(3 * depth + shift, 16)
        right[pl.ds(start, piece), :] = f1[k * piece : (k + 1) * piece]
    right[3 * depth - tail : 3 * depth] = m2[...]
    right[4 * depth - tail : 4 * depth] = f1[4 * piece :]
    block = 256
    for m in range(left.shape[0] // block):
        total = jnp.dot(left[m * block : (m + 1) * block, :], right[...], preferred_element_type=F32).astype(BF)
        for b in range(block // 32):
            high, low = m * (block // 128) + b // 4, b % 4
            place = pl.multiple_of((high * 4 + jnp.bitwise_xor(low, mine)) * 32, 32)
            c_ref[pl.ds(place, 32), :] = total[b * 32 : (b + 1) * 32]


def join_kernel(at_ref, p0, p1, p2, p3, out_ref):
    mine = at_ref[2]
    width = p0.shape[1]
    for k, ref in enumerate((p0, p1, p2, p3)):
        place = pl.multiple_of(jnp.bitwise_xor(mine, k) * width, width)
        out_ref[:, pl.ds(place, width)] = ref[...]


def other_core(value):
    return lax.ppermute(value, "c", [(0, 1), (1, 0)])


def local(projected, short_filter, residue, rate, out_weight):
    rows, channels = projected.shape[1], projected.shape[2]
    groups = rate.shape[0]
    width = out_weight.shape[1] // 4
    y, xh, core = lax.axis_index("y"), lax.axis_index("xh"), lax.axis_index("c")
    seq = lax.axis_index(("y", "xl"))
    at = jnp.stack([seq, y, xh * 2 + core, core]).astype(jnp.int32)

    halo = lax.ppermute(projected[:, rows - 8 :, :], ("y", "xl"), [(i, i + 1) for i in range(7)])

    piece = 48
    half = 2 * width
    mirror = [(0, 3), (3, 0), (1, 2), (2, 1)]

    def weight_rows(start, size):
        return lax.dynamic_slice(out_weight, (start, (1 - xh) * half), (size, half))

    m1 = lax.ppermute(weight_rows(y * piece, piece), ("xl", "xh"), mirror)
    m2 = lax.ppermute(weight_rows(4 * piece, channels - 4 * piece), ("xl", "xh"), mirror)
    w_other = other_core(lax.dynamic_slice(out_weight, (0, (xh * 2 + 1 - core) * width), (channels, width)))

    weight = residue * jnp.sqrt(-jnp.expm1(-2.0 * rate))
    flat = groups * MODES
    span = 256
    once = {"pipeline_mode": pl.Buffered(1)}

    def whole(shape):
        return pl.BlockSpec(shape, lambda i: (0,) * len(shape))

    def third(k):
        return pl.BlockSpec((None, span, channels), lambda i: (k, i, 0))

    signal, end, rt = pl.pallas_call(
        state_kernel,
        out_shape=(
            pltpu.HBM((rows, channels), BF),
            jax.ShapeDtypeStruct((8, MODES, channels), F32),
            jax.ShapeDtypeStruct((MODES, channels), F32),
        ),
        grid=(rows // span,),
        in_specs=[third(1), third(2), whole(halo.shape), whole(short_filter.shape), whole(rate.shape)],
        out_specs=(
            pl.BlockSpec((span, channels), lambda i: (i, 0)),
            whole((8, MODES, channels)),
            whole((MODES, channels)),
        ),
        scratch_shapes=[
            pltpu.VMEM((2, 8, channels), F32),
            pltpu.VMEM((MODES, 8, channels), F32),
            pltpu.VMEM((MODES, 8, channels), F32),
        ],
        compiler_params=pltpu.CompilerParams(vmem_limit_bytes=12 * 2**20),
        cost_estimate=pl.CostEstimate(flops=2 * 10**7, bytes_accessed=6 * 2**20, transcendentals=10**4),
        name="state",
    )(projected, projected, halo, short_filter, rate)
    signal, m1 = lax.optimization_barrier((signal, m1))
    ends = lax.all_to_all(end, ("y", "xl"), 0, 0, tiled=True)
    conv, query, din = pl.pallas_call(
        conv_kernel,
        out_shape=(
            pltpu.HBM((rows, channels), F32),
            pltpu.HBM((rows, channels), F32),
            jax.ShapeDtypeStruct((CHUNK, flat), BF),
        ),
        grid=(1,),
        in_specs=[
            pl.BlockSpec((None, rows, channels), lambda i: (0, 0, 0)),
            whole((rows, channels)), whole(halo.shape), whole(short_filter.shape),
            whole(rate.shape), whole(rate.shape), whole(rt.shape),
        ],
        out_specs=(whole((rows, channels)), whole((rows, channels)), whole((CHUNK, flat))),
        scratch_shapes=[
            pltpu.VMEM((CHUNK + MODES, groups * CHUNK), BF),
            pltpu.VMEM((channels // LANES, LANES // GROUP * CHUNK, 2 * LANES), BF),
        ],
        cost_estimate=pl.CostEstimate(flops=4 * 10**9, bytes_accessed=12 * 2**20, transcendentals=10**5),
        name="conv",
    )(projected, signal, halo, short_filter, rate, weight, rt)
    r1, r2, r3 = (lax.ppermute(m1, "y", [(i, (i + k) % 4) for i in range(4)]) for k in (1, 2, 3))
    ends, r1, r3, m2 = lax.optimization_barrier((ends, r1, r3, m2))
    mixed = pl.pallas_call(
        mix_kernel,
        out_shape=jax.ShapeDtypeStruct((rows, channels), BF),
        grid=(rows // span,),
        in_specs=[
            SM, whole(ends.shape), whole(rt.shape), whole(din.shape),
            pl.BlockSpec((span, channels), lambda i: (i, 0)),
            pl.BlockSpec((span, channels), lambda i: (i, 0)),
        ],
        out_specs=pl.BlockSpec((span, channels), lambda i: (i, 0)),
        scratch_shapes=[pltpu.VMEM((MODES, channels), F32)],
        cost_estimate=pl.CostEstimate(flops=2 * 10**8, bytes_accessed=5 * 2**20, transcendentals=10**4),
        name="mix",
    )(at, ends, rt, din, conv, query)

    a_far = lax.ppermute(mixed, "xh", [(0, 1), (1, 0)])
    a_other = other_core(mixed)
    a_far_other = other_core(a_far)
    given = jnp.concatenate(
        [lax.dynamic_slice(v, (0, (1 - core) * width), (v.shape[0], width)) for v in (m1, r1, r2, r3, m2)], axis=0
    )
    f_other = other_core(given)

    tile = 512
    strips = width // tile

    def strip(shape):
        return pl.BlockSpec(shape[:-1] + (tile,), lambda i, at_ref: (0, i))

    def half_strip(shape):
        return pl.BlockSpec(shape[:-1] + (tile,), lambda i, at_ref: (0, at_ref[3] * strips + i))

    partial = pl.pallas_call(
        product_kernel,
        out_shape=pltpu.HBM((rows, width), BF),
        grid_spec=pltpu.PrefetchScalarGridSpec(
            num_scalar_prefetch=1,
            grid=(strips,),
            in_specs=[pl.BlockSpec((rows, channels), lambda i, at_ref: (0, 0), **once)] * 4
            + [pl.BlockSpec((channels, tile), lambda i, at_ref: (0, at_ref[2] * strips + i)), strip(w_other.shape)]
            + [half_strip(m1.shape)] * 4
            + [half_strip(m2.shape), strip(f_other.shape)],
            out_specs=strip((rows, width)),
            scratch_shapes=[pltpu.VMEM((rows, 4 * channels), BF), pltpu.VMEM((4 * channels, tile), BF)],
        ),
        compiler_params=pltpu.CompilerParams(vmem_limit_bytes=28 * 2**20),
        cost_estimate=pl.CostEstimate(flops=4 * 10**9, bytes_accessed=10 * 2**20, transcendentals=0),
        name="product",
    )(at, mixed, a_other, a_far, a_far_other, pltpu.with_memory_space_constraint(out_weight, pltpu.HBM), w_other, m1, r1, r2, r3, m2, f_other)

    summed = lax.psum_scatter(partial, "z", scatter_dimension=0, tiled=True)
    size = summed.shape[0] // 4

    def traded(k):
        pairs = [(i, i ^ k) for i in range(4)]
        return lax.ppermute(summed[k * size : (k + 1) * size], ("xh", "c"), pairs)

    return pl.pallas_call(
        join_kernel,
        out_shape=jax.ShapeDtypeStruct((size, 4 * width), BF),
        in_specs=[SM] + [VM] * 4,
        out_specs=VM,
        compiler_params=pltpu.CompilerParams(vmem_limit_bytes=4 * 2**20),
        name="join",
    )(at, summed[:size], traded(1), traded(2), traded(3))


def solution(mesh):
    fine = Mesh(mesh.devices.reshape(4, 2, 8, 2, 2), ("y", "xl", "z", "xh", "c"))
    seq, tp = ("y", "xl"), ("z", "xh", "c")
    placed = (P(None, seq, tp), P(None, None, tp), P(tp, None), P(tp, None), P(tp, None))
    return jax.shard_map(local, mesh=fine, in_specs=placed, out_specs=P(seq + tp, None), check_vma=False)
```

```python
import jax
import jax.numpy as jnp
from jax import lax
from jax.experimental import pallas as pl
from jax.experimental.pallas import tpu as pltpu
from jax.sharding import Mesh, PartitionSpec as P

GROUP = 16
MODES = 16
CHUNK = 128
LANES = 128
BF = jnp.bfloat16
F32 = jnp.float32
VM = pl.BlockSpec(memory_space=pltpu.VMEM)
SM = pl.BlockSpec(memory_space=pltpu.SMEM)


def iota(shape, dim):
    return lax.broadcasted_iota(jnp.int32, shape, dim)


def spread(state):
    width = state.shape[1]
    groups = width // GROUP
    tall = jnp.concatenate([state] * groups, axis=0)
    shape = (groups * MODES, width)
    own = iota(shape, 0) // MODES == iota(shape, 1) // GROUP
    return jnp.where(own, tall, 0.0).astype(BF)


def one_hot(rows, columns, row_size, column_size):
    shape = (rows, columns)
    return (iota(shape, 0) // row_size == iota(shape, 1) // column_size).astype(F32)


def exact_dot(a, b, dims):
    return lax.dot_general(a, b, (dims, ((), ())), precision=lax.Precision.HIGHEST, preferred_element_type=F32)


def by_channel(table, channels):
    return exact_dot(table, one_hot(table.shape[0], channels, 1, GROUP), ((0,), (0,)))


def by_row(table):
    flat = table.shape[0] * MODES
    wide = exact_dot(one_hot(flat, table.shape[0], MODES, 1), table, ((1,), (0,)))
    keep = iota((flat, MODES), 0) % MODES == iota((flat, MODES), 1)
    return jnp.where(keep, wide, 0.0).sum(axis=1, keepdims=True)


def by_lane(table):
    flat = table.shape[0] * MODES
    wide = exact_dot(table, one_hot(table.shape[0], flat, 1, MODES), ((0,), (0,)))
    keep = iota((MODES, flat), 1) % MODES == iota((MODES, flat), 0)
    return jnp.where(keep, wide, 0.0).sum(axis=0, keepdims=True)


def tapped(taps, cur, before):
    ext = jnp.concatenate([before, cur], axis=0)
    skip = before.shape[0]
    one = pltpu.roll(ext, 1, 0)[skip:]
    two = pltpu.roll(ext, 2, 0)[skip:]
    return taps[0:1, :] * cur + taps[1:2, :] * one + taps[2:3, :] * two


def state_kernel(k_ref, v_ref, halo_ref, sf_ref, rate_ref, x_ref, end_ref, rt_ref, tail, total, power):
    step = pl.program_id(0)
    rows, channels = k_ref.shape

    @pl.when(step == 0)
    def _():
        rt = by_channel(rate_ref[...], channels)
        rt_ref[...] = rt
        total[...] = jnp.zeros_like(total)
        for n in range(MODES):
            power[n] = jnp.broadcast_to(jnp.exp(-8.0 * rt[n : n + 1, :]), (8, channels))
        for i in range(2):
            tail[i] = halo_ref[i + 1].astype(F32)

    featured = []
    for i, ref in enumerate((k_ref, v_ref)):
        cur = ref[...].astype(F32)
        featured.append(tapped(sf_ref[i + 1], cur, tail[i]))
        tail[i] = cur[rows - 8 :]
    signal = featured[0] * featured[1]
    x_ref[...] = signal.astype(BF)
    for h in range(channels // LANES):
        lanes = slice(h * LANES, (h + 1) * LANES)
        for first in range(0, MODES, 8):
            sums = [total[n, :, lanes] for n in range(first, first + 8)]
            powers = [power[n, :, lanes] for n in range(first, first + 8)]
            for b in range(rows // 8):
                block = signal[b * 8 : (b + 1) * 8, lanes]
                sums = [s * w + block for s, w in zip(sums, powers)]
            for n in range(8):
                total[first + n, :, lanes] = sums[n]

    @pl.when(step == pl.num_programs(0) - 1)
    def _():
        rt = rt_ref[...]
        ahead = (7 - iota((8, channels), 0)).astype(F32)
        end = jnp.concatenate(
            [
                (total[n] * jnp.exp(-ahead * rt[n : n + 1, :])).sum(axis=0, keepdims=True)
                for n in range(MODES)
            ],
            axis=0,
        )
        for j in range(end_ref.shape[0]):
            end_ref[j] = end


def conv_kernel(p_ref, x_ref, halo_ref, sf_ref, rate_ref, weight_ref, rt_ref,
                y_ref, q_ref, din_ref, table, masked):
    rows, channels = x_ref.shape
    halves = channels // LANES
    per_half = LANES // GROUP
    groups = channels // GROUP
    rate, weight = rate_ref[...], weight_ref[...]
    rcol = by_row(rate)
    wcol = by_row(weight)
    lane = iota((groups * MODES, CHUNK), 1)
    back = jnp.where(lane == 0, 0, CHUNK - lane).astype(F32)
    taps = (wcol * jnp.exp(-rcol * back)).reshape(groups, MODES, CHUNK).sum(axis=1)
    leave = jnp.exp(-rcol * (CHUNK - 1 - lane).astype(F32)).astype(BF)
    causal = iota((CHUNK, CHUNK), 0) >= iota((CHUNK, CHUNK), 1)
    for g in range(groups):
        wide = jnp.broadcast_to(taps[g : g + 1, :], (CHUNK, CHUNK))
        turned = pltpu.roll(wide, 0, 1, stride=1, stride_axis=0)
        table[0:CHUNK, g * CHUNK : (g + 1) * CHUNK] = jnp.where(causal, turned, 0.0).astype(BF)
        table[CHUNK : CHUNK + MODES, g * CHUNK : (g + 1) * CHUNK] = leave[g * MODES : (g + 1) * MODES]
    steps = (iota((CHUNK, groups * MODES), 0) + 1).astype(F32)
    din = (by_lane(weight) * jnp.exp(-by_lane(rate) * steps)).astype(BF)
    din_ref[...] = din
    power = jnp.exp(-rt_ref[...] * float(CHUNK))
    group_lane = iota((CHUNK, LANES), 1) // GROUP

    state = jnp.zeros((MODES, channels), F32)
    for pair in range(rows // (2 * CHUNK)):
        for j in range(2):
            q = 2 * pair + j
            span = slice(q * CHUNK, (q + 1) * CHUNK)
            before = halo_ref[0] if q == 0 else p_ref[q * CHUNK - 16 : q * CHUNK, :]
            q_ref[span, :] = tapped(sf_ref[0], p_ref[span, :].astype(F32), before.astype(F32)).astype(BF)
            for h in range(halves):
                part = x_ref[span, h * LANES : (h + 1) * LANES]
                for g in range(per_half):
                    masked[h, g * CHUNK : (g + 1) * CHUNK, j * LANES : (j + 1) * LANES] = jnp.where(
                        group_lane == g, part, jnp.zeros_like(part)
                    )
        depth = per_half * CHUNK
        made = [
            jnp.dot(table[:, h * depth : (h + 1) * depth], masked[h], preferred_element_type=F32)
            for h in range(halves)
        ]
        for j in range(2):
            q = 2 * pair + j
            full = jnp.concatenate([m[:, j * LANES : (j + 1) * LANES] for m in made], axis=1)
            within = full[:CHUNK]
            if q > 0:
                within = within + jnp.dot(din, spread(state), preferred_element_type=F32)
            y_ref[q * CHUNK : (q + 1) * CHUNK, :] = within.astype(BF)
            state = power * state + full[CHUNK:]


def mix_kernel(at_ref, ends_ref, rt_ref, din_ref, y_ref, q_ref, mixed_ref):
    rows = y_ref.shape[0]
    here = at_ref[0]
    rt = rt_ref[...]
    block_power = jnp.exp(-rt * float(rows))
    state = jnp.zeros(rt.shape, F32)
    for j in range(ends_ref.shape[0]):
        state = jnp.where(j < here, block_power * state + ends_ref[j], state)
    power = jnp.exp(-rt * float(CHUNK))
    din = din_ref[...]
    for q in range(rows // CHUNK):
        span = slice(q * CHUNK, (q + 1) * CHUNK)
        carried = jnp.dot(din, spread(state), preferred_element_type=F32)
        mixed_ref[span, :] = (q_ref[span, :].astype(F32) * (y_ref[span, :].astype(F32) + carried)).astype(BF)
        state = power * state


def product_kernel(at_ref, a0, a1, a2, a3, w0, w1, m1, r1, r2, r3, m2, f1, c_ref, left, right):
    y, mine = at_ref[1], at_ref[2]
    depth = w0.shape[0]
    piece, tail = m1.shape[0], m2.shape[0]

    @pl.when(pl.program_id(0) == 0)
    def _():
        for k, ref in enumerate((a0, a1, a2, a3)):
            left[:, k * depth : (k + 1) * depth] = ref[...]

    right[0:depth] = w0[...]
    right[depth : 2 * depth] = w1[...]
    for k, ref in enumerate((m1, r1, r2, r3)):
        shift = lax.rem(y - k + 4, 4) * piece
        start = pl.multiple_of(2 * depth + shift, 16)
        right[pl.ds(start, piece), :] = ref[...]
        start = pl.multiple_of(3 * depth + shift, 16)
        right[pl.ds(start, piece), :] = f1[k * piece : (k + 1) * piece]
    right[3 * depth - tail : 3 * depth] = m2[...]
    right[4 * depth - tail : 4 * depth] = f1[4 * piece :]
    block = 256
    for m in range(left.shape[0] // block):
        total = jnp.dot(left[m * block : (m + 1) * block, :], right[...], preferred_element_type=F32).astype(BF)
        for b in range(block // 32):
            high, low = m * (block // 128) + b // 4, b % 4
            place = pl.multiple_of((high * 4 + jnp.bitwise_xor(low, mine)) * 32, 32)
            c_ref[pl.ds(place, 32), :] = total[b * 32 : (b + 1) * 32]


def join_kernel(at_ref, p0, p1, p2, p3, out_ref):
    mine = at_ref[2]
    width = p0.shape[1]
    for k, ref in enumerate((p0, p1, p2, p3)):
        place = pl.multiple_of(jnp.bitwise_xor(mine, k) * width, width)
        out_ref[:, pl.ds(place, width)] = ref[...]


def other_core(value):
    return lax.ppermute(value, "c", [(0, 1), (1, 0)])


def local(projected, short_filter, residue, rate, out_weight):
    rows, channels = projected.shape[1], projected.shape[2]
    groups = rate.shape[0]
    width = out_weight.shape[1] // 4
    y, xh, core = lax.axis_index("y"), lax.axis_index("xh"), lax.axis_index("c")
    seq = lax.axis_index(("y", "xl"))
    halo = lax.ppermute(projected[:, rows - 8 :, :], ("y", "xl"), [(i, i + 1) for i in range(7)])

    piece = 48
    half = 2 * width
    mirror = [(0, 3), (3, 0), (1, 2), (2, 1)]

    def mirrored_rows(start, size, xh):
        rows_there = lax.dynamic_slice(out_weight, (start, (1 - xh) * half), (size, half))
        return lax.ppermute(rows_there, ("xl", "xh"), mirror)

    m1 = mirrored_rows(y * piece, piece, xh)

    flat = groups * MODES
    span = 256
    once = {"pipeline_mode": pl.Buffered(1)}

    def whole(shape):
        return pl.BlockSpec(shape, lambda i: (0,) * len(shape))

    def third(k):
        return pl.BlockSpec((None, span, channels), lambda i: (k, i, 0))

    signal, end, rt = pl.pallas_call(
        state_kernel,
        out_shape=(
            jax.ShapeDtypeStruct((rows, channels), BF),
            jax.ShapeDtypeStruct((8, MODES, channels), F32),
            jax.ShapeDtypeStruct((MODES, channels), F32),
        ),
        grid=(rows // span,),
        in_specs=[third(1), third(2), whole(halo.shape), whole(short_filter.shape), whole(rate.shape)],
        out_specs=(
            pl.BlockSpec((span, channels), lambda i: (i, 0)),
            whole((8, MODES, channels)),
            whole((MODES, channels)),
        ),
        scratch_shapes=[
            pltpu.VMEM((2, 8, channels), F32),
            pltpu.VMEM((MODES, 8, channels), F32),
            pltpu.VMEM((MODES, 8, channels), F32),
        ],
        compiler_params=pltpu.CompilerParams(vmem_limit_bytes=12 * 2**20),
        cost_estimate=pl.CostEstimate(flops=10**6, bytes_accessed=2**16, transcendentals=0),
        name="state",
    )(projected, projected, halo, short_filter, rate)
    end, xh_late, core_late, residue_late = lax.optimization_barrier((end, xh, core, residue))
    at = jnp.stack([seq, y, xh_late * 2 + core_late, core_late]).astype(jnp.int32)
    m2 = mirrored_rows(4 * piece, channels - 4 * piece, xh_late)
    w_other = other_core(
        lax.dynamic_slice(out_weight, (0, (xh_late * 2 + 1 - core_late) * width), (channels, width))
    )
    weight = residue_late * jnp.sqrt(-jnp.expm1(-2.0 * rate))
    ends = lax.all_to_all(end, ("y", "xl"), 0, 0, tiled=True)
    conv, query, din = pl.pallas_call(
        conv_kernel,
        out_shape=(
            jax.ShapeDtypeStruct((rows, channels), BF),
            jax.ShapeDtypeStruct((rows, channels), BF),
            jax.ShapeDtypeStruct((CHUNK, flat), BF),
        ),
        grid=(1,),
        in_specs=[
            pl.BlockSpec((None, rows, channels), lambda i: (0, 0, 0)),
            whole((rows, channels)), whole(halo.shape), whole(short_filter.shape),
            whole(rate.shape), whole(rate.shape), whole(rt.shape),
        ],
        out_specs=(whole((rows, channels)), whole((rows, channels)), whole((CHUNK, flat))),
        scratch_shapes=[
            pltpu.VMEM((CHUNK + MODES, groups * CHUNK), BF),
            pltpu.VMEM((channels // LANES, LANES // GROUP * CHUNK, 2 * LANES), BF),
        ],
        compiler_params=pltpu.CompilerParams(vmem_limit_bytes=16 * 2**20),
        cost_estimate=pl.CostEstimate(flops=10**6, bytes_accessed=2**16, transcendentals=0),
        name="conv",
    )(projected, signal, halo, short_filter, rate, weight, rt)
    r1, r2, r3 = (lax.ppermute(m1, "y", [(i, (i + k) % 4) for i in range(4)]) for k in (1, 2, 3))
    ends, r1, r3 = lax.optimization_barrier((ends, r1, r3))
    mixed = pl.pallas_call(
        mix_kernel,
        out_shape=jax.ShapeDtypeStruct((rows, channels), BF),
        in_specs=[SM] + [VM] * 5,
        out_specs=VM,
        compiler_params=pltpu.CompilerParams(vmem_limit_bytes=10 * 2**20),
        cost_estimate=pl.CostEstimate(flops=10**6, bytes_accessed=2**16, transcendentals=0),
        name="mix",
    )(at, ends, rt, din, conv, query)

    a_far = lax.ppermute(mixed, "xh", [(0, 1), (1, 0)])
    a_other = other_core(mixed)
    a_far_other = other_core(a_far)
    given = jnp.concatenate(
        [lax.dynamic_slice(v, (0, (1 - core) * width), (v.shape[0], width)) for v in (m1, r1, r2, r3, m2)], axis=0
    )
    f_other = other_core(given)

    tile = 512
    strips = width // tile

    def strip(shape):
        return pl.BlockSpec(shape[:-1] + (tile,), lambda i, at_ref: (0, i))

    def half_strip(shape):
        return pl.BlockSpec(shape[:-1] + (tile,), lambda i, at_ref: (0, at_ref[3] * strips + i))

    partial = pl.pallas_call(
        product_kernel,
        out_shape=pltpu.HBM((rows, width), BF),
        grid_spec=pltpu.PrefetchScalarGridSpec(
            num_scalar_prefetch=1,
            grid=(strips,),
            in_specs=[pl.BlockSpec((rows, channels), lambda i, at_ref: (0, 0), **once)] * 4
            + [pl.BlockSpec((channels, tile), lambda i, at_ref: (0, at_ref[2] * strips + i)), strip(w_other.shape)]
            + [half_strip(m1.shape)] * 4
            + [half_strip(m2.shape), strip(f_other.shape)],
            out_specs=strip((rows, width)),
            scratch_shapes=[pltpu.VMEM((rows, 4 * channels), BF), pltpu.VMEM((4 * channels, tile), BF)],
        ),
        compiler_params=pltpu.CompilerParams(vmem_limit_bytes=28 * 2**20),
        cost_estimate=pl.CostEstimate(flops=4 * 10**9, bytes_accessed=10 * 2**20, transcendentals=0),
        name="product",
    )(at, mixed, a_other, a_far, a_far_other, pltpu.with_memory_space_constraint(out_weight, pltpu.HBM), w_other, m1, r1, r2, r3, m2, f_other)

    summed = lax.psum_scatter(partial, "z", scatter_dimension=0, tiled=True)
    size = summed.shape[0] // 4

    def traded(k):
        pairs = [(i, i ^ k) for i in range(4)]
        return lax.ppermute(summed[k * size : (k + 1) * size], ("xh", "c"), pairs)

    return pl.pallas_call(
        join_kernel,
        out_shape=jax.ShapeDtypeStruct((size, 4 * width), BF),
        in_specs=[SM] + [VM] * 4,
        out_specs=VM,
        compiler_params=pltpu.CompilerParams(vmem_limit_bytes=4 * 2**20),
        name="join",
    )(at, summed[:size], traded(1), traded(2), traded(3))


def solution(mesh):
    fine = Mesh(mesh.devices.reshape(4, 2, 8, 2, 2), ("y", "xl", "z", "xh", "c"))
    seq, tp = ("y", "xl"), ("z", "xh", "c")
    placed = (P(None, seq, tp), P(None, None, tp), P(tp, None), P(tp, None), P(tp, None))
    return jax.shard_map(local, mesh=fine, in_specs=placed, out_specs=P(seq + tp, None), check_vma=False)
```

```python
import jax
import jax.numpy as jnp
from jax import lax
from jax.experimental import pallas as pl
from jax.experimental.pallas import tpu as pltpu
from jax.sharding import Mesh, PartitionSpec as P

GROUP = 16
MODES = 16
CHUNK = 128
LANES = 128
BF = jnp.bfloat16
F32 = jnp.float32
VM = pl.BlockSpec(memory_space=pltpu.VMEM)
SM = pl.BlockSpec(memory_space=pltpu.SMEM)


def iota(shape, dim):
    return lax.broadcasted_iota(jnp.int32, shape, dim)


def spread(state):
    width = state.shape[1]
    groups = width // GROUP
    tall = jnp.concatenate([state] * groups, axis=0)
    shape = (groups * MODES, width)
    own = iota(shape, 0) // MODES == iota(shape, 1) // GROUP
    return jnp.where(own, tall, 0.0).astype(BF)


def one_hot(rows, columns, row_size, column_size):
    shape = (rows, columns)
    return (iota(shape, 0) // row_size == iota(shape, 1) // column_size).astype(F32)


def exact_dot(a, b, dims):
    return lax.dot_general(a, b, (dims, ((), ())), precision=lax.Precision.HIGHEST, preferred_element_type=F32)


def by_channel(table, channels):
    return exact_dot(table, one_hot(table.shape[0], channels, 1, GROUP), ((0,), (0,)))


def by_row(table):
    flat = table.shape[0] * MODES
    wide = exact_dot(one_hot(flat, table.shape[0], MODES, 1), table, ((1,), (0,)))
    keep = iota((flat, MODES), 0) % MODES == iota((flat, MODES), 1)
    return jnp.where(keep, wide, 0.0).sum(axis=1, keepdims=True)


def by_lane(table):
    flat = table.shape[0] * MODES
    wide = exact_dot(table, one_hot(table.shape[0], flat, 1, MODES), ((0,), (0,)))
    keep = iota((MODES, flat), 1) % MODES == iota((MODES, flat), 0)
    return jnp.where(keep, wide, 0.0).sum(axis=0, keepdims=True)


def tapped(taps, cur, before):
    ext = jnp.concatenate([before, cur], axis=0)
    skip = before.shape[0]
    one = pltpu.roll(ext, 1, 0)[skip:]
    two = pltpu.roll(ext, 2, 0)[skip:]
    return taps[0:1, :] * cur + taps[1:2, :] * one + taps[2:3, :] * two


def state_kernel(k_ref, v_ref, halo_ref, sf_ref, rate_ref, x_ref, end_ref, rt_ref, tail, total, power):
    step = pl.program_id(0)
    rows, channels = k_ref.shape

    @pl.when(step == 0)
    def _():
        rt = by_channel(rate_ref[...], channels)
        rt_ref[...] = rt
        total[...] = jnp.zeros_like(total)
        for n in range(MODES):
            power[n] = jnp.broadcast_to(jnp.exp(-8.0 * rt[n : n + 1, :]), (8, channels))
        for i in range(2):
            tail[i] = halo_ref[i + 1].astype(F32)

    featured = []
    for i, ref in enumerate((k_ref, v_ref)):
        cur = ref[...].astype(F32)
        featured.append(tapped(sf_ref[i + 1], cur, tail[i]))
        tail[i] = cur[rows - 8 :]
    signal = featured[0] * featured[1]
    x_ref[...] = signal.astype(BF)
    for h in range(channels // LANES):
        lanes = slice(h * LANES, (h + 1) * LANES)
        for first in range(0, MODES, 8):
            sums = [total[n, :, lanes] for n in range(first, first + 8)]
            powers = [power[n, :, lanes] for n in range(first, first + 8)]
            for b in range(rows // 8):
                block = signal[b * 8 : (b + 1) * 8, lanes]
                sums = [s * w + block for s, w in zip(sums, powers)]
            for n in range(8):
                total[first + n, :, lanes] = sums[n]

    @pl.when(step == pl.num_programs(0) - 1)
    def _():
        rt = rt_ref[...]
        ahead = (7 - iota((8, channels), 0)).astype(F32)
        end = jnp.concatenate(
            [
                (total[n] * jnp.exp(-ahead * rt[n : n + 1, :])).sum(axis=0, keepdims=True)
                for n in range(MODES)
            ],
            axis=0,
        )
        for j in range(end_ref.shape[0]):
            end_ref[j] = end


def conv_kernel(p_ref, x_ref, halo_ref, sf_ref, rate_ref, weight_ref, rt_ref,
                y_ref, q_ref, din_ref, table, masked):
    rows, channels = x_ref.shape
    halves = channels // LANES
    per_half = LANES // GROUP
    groups = channels // GROUP
    rate, weight = rate_ref[...], weight_ref[...]
    rcol = by_row(rate)
    wcol = by_row(weight)
    lane = iota((groups * MODES, CHUNK), 1)
    back = jnp.where(lane == 0, 0, CHUNK - lane).astype(F32)
    taps = (wcol * jnp.exp(-rcol * back)).reshape(groups, MODES, CHUNK).sum(axis=1)
    leave = jnp.exp(-rcol * (CHUNK - 1 - lane).astype(F32)).astype(BF)
    causal = iota((CHUNK, CHUNK), 0) >= iota((CHUNK, CHUNK), 1)
    for g in range(groups):
        wide = jnp.broadcast_to(taps[g : g + 1, :], (CHUNK, CHUNK))
        turned = pltpu.roll(wide, 0, 1, stride=1, stride_axis=0)
        table[0:CHUNK, g * CHUNK : (g + 1) * CHUNK] = jnp.where(causal, turned, 0.0).astype(BF)
        table[CHUNK : CHUNK + MODES, g * CHUNK : (g + 1) * CHUNK] = leave[g * MODES : (g + 1) * MODES]
    steps = (iota((CHUNK, groups * MODES), 0) + 1).astype(F32)
    din = (by_lane(weight) * jnp.exp(-by_lane(rate) * steps)).astype(BF)
    din_ref[...] = din
    power = jnp.exp(-rt_ref[...] * float(CHUNK))
    group_lane = iota((CHUNK, LANES), 1) // GROUP

    state = jnp.zeros((MODES, channels), F32)
    for pair in range(rows // (2 * CHUNK)):
        for j in range(2):
            q = 2 * pair + j
            span = slice(q * CHUNK, (q + 1) * CHUNK)
            before = halo_ref[0] if q == 0 else p_ref[q * CHUNK - 16 : q * CHUNK, :]
            q_ref[span, :] = tapped(sf_ref[0], p_ref[span, :].astype(F32), before.astype(F32)).astype(BF)
            for h in range(halves):
                part = x_ref[span, h * LANES : (h + 1) * LANES]
                for g in range(per_half):
                    masked[h, g * CHUNK : (g + 1) * CHUNK, j * LANES : (j + 1) * LANES] = jnp.where(
                        group_lane == g, part, jnp.zeros_like(part)
                    )
        depth = per_half * CHUNK
        made = [
            jnp.dot(table[:, h * depth : (h + 1) * depth], masked[h], preferred_element_type=F32)
            for h in range(halves)
        ]
        for j in range(2):
            q = 2 * pair + j
            full = jnp.concatenate([m[:, j * LANES : (j + 1) * LANES] for m in made], axis=1)
            within = full[:CHUNK]
            if q > 0:
                within = within + jnp.dot(din, spread(state), preferred_element_type=F32)
            y_ref[q * CHUNK : (q + 1) * CHUNK, :] = within.astype(BF)
            state = power * state + full[CHUNK:]


def mix_kernel(at_ref, ends_ref, rt_ref, din_ref, y_ref, q_ref, mixed_ref):
    rows = y_ref.shape[0]
    here = at_ref[0]
    rt = rt_ref[...]
    block_power = jnp.exp(-rt * float(rows))
    state = jnp.zeros(rt.shape, F32)
    for j in range(ends_ref.shape[0]):
        state = jnp.where(j < here, block_power * state + ends_ref[j], state)
    power = jnp.exp(-rt * float(CHUNK))
    din = din_ref[...]
    for q in range(rows // CHUNK):
        span = slice(q * CHUNK, (q + 1) * CHUNK)
        carried = jnp.dot(din, spread(state), preferred_element_type=F32)
        mixed_ref[span, :] = (q_ref[span, :].astype(F32) * (y_ref[span, :].astype(F32) + carried)).astype(BF)
        state = power * state


def product_kernel(at_ref, a0, a1, a2, a3, w0, w1, f0, f1, f2, g0, g1, g2, c_ref, left, right):
    parity, mine = at_ref[1], at_ref[2]
    depth = w0.shape[0]
    size, quarter = f0.shape[0], f1.shape[0]

    @pl.when(pl.program_id(0) == 0)
    def _():
        for k, ref in enumerate((a0, a1, a2, a3)):
            left[:, k * depth : (k + 1) * depth] = ref[...]

    right[0:depth] = w0[...]
    right[depth : 2 * depth] = w1[...]
    for s, refs in enumerate(((f0, f1, f2), (g0, g1, g2))):
        base = (2 + s) * depth
        near = pl.multiple_of(base + parity * size, 64)
        far = pl.multiple_of(base + (1 - parity) * size, 64)
        right[pl.ds(near, size), :] = refs[0][...]
        right[pl.ds(far, quarter), :] = refs[1][...]
        right[pl.ds(pl.multiple_of(far + quarter, 64), quarter), :] = refs[2][...]
    block = 256
    for m in range(left.shape[0] // block):
        total = jnp.dot(left[m * block : (m + 1) * block, :], right[...], preferred_element_type=F32).astype(BF)
        for b in range(block // 32):
            high, low = m * (block // 128) + b // 4, b % 4
            place = pl.multiple_of((high * 4 + jnp.bitwise_xor(low, mine)) * 32, 32)
            c_ref[pl.ds(place, 32), :] = total[b * 32 : (b + 1) * 32]


def join_kernel(at_ref, p0, p1, p2, p3, out_ref):
    mine = at_ref[2]
    width = p0.shape[1]
    for k, ref in enumerate((p0, p1, p2, p3)):
        place = pl.multiple_of(jnp.bitwise_xor(mine, k) * width, width)
        out_ref[:, pl.ds(place, width)] = ref[...]


def far(value):
    return pltpu.with_memory_space_constraint(value, pltpu.HBM)


def other_core(value):
    return lax.ppermute(value, "c", [(0, 1), (1, 0)])


def local(projected, short_filter, residue, rate, out_weight):
    rows, channels = projected.shape[1], projected.shape[2]
    groups = rate.shape[0]
    width = out_weight.shape[1] // 4
    y, xh, core = lax.axis_index("y"), lax.axis_index("xh"), lax.axis_index("c")
    seq = lax.axis_index(("y", "xl"))
    halo = lax.ppermute(projected[:, rows - 8 :, :], ("y", "xl"), [(i, i + 1) for i in range(7)])

    size = channels // 2
    half = 2 * width
    parity = lax.rem(y, 2)
    mirror = [(0, 3), (3, 0), (1, 2), (2, 1)]
    fetched = lax.ppermute(
        lax.dynamic_slice(out_weight, (parity * size, (1 - xh) * half), (size, half)), ("xl", "xh"), mirror
    )

    flat = groups * MODES
    span = 256
    once = {"pipeline_mode": pl.Buffered(1)}

    def whole(shape):
        return pl.BlockSpec(shape, lambda i: (0,) * len(shape))

    def third(k):
        return pl.BlockSpec((None, span, channels), lambda i: (k, i, 0))

    signal, end, rt = pl.pallas_call(
        state_kernel,
        out_shape=(
            jax.ShapeDtypeStruct((rows, channels), BF),
            jax.ShapeDtypeStruct((8, MODES, channels), F32),
            jax.ShapeDtypeStruct((MODES, channels), F32),
        ),
        grid=(rows // span,),
        in_specs=[third(1), third(2), whole(halo.shape), whole(short_filter.shape), whole(rate.shape)],
        out_specs=(
            pl.BlockSpec((span, channels), lambda i: (i, 0)),
            whole((8, MODES, channels)),
            whole((MODES, channels)),
        ),
        scratch_shapes=[
            pltpu.VMEM((2, 8, channels), F32),
            pltpu.VMEM((MODES, 8, channels), F32),
            pltpu.VMEM((MODES, 8, channels), F32),
        ],
        compiler_params=pltpu.CompilerParams(vmem_limit_bytes=12 * 2**20),
        cost_estimate=pl.CostEstimate(flops=10**6, bytes_accessed=2**16, transcendentals=0),
        name="state",
    )(far(projected), far(projected), halo, far(short_filter), far(rate))
    end, xh_late, core_late, residue_late = lax.optimization_barrier((end, xh, core, residue))
    at = jnp.stack([seq, parity, xh_late * 2 + core_late, core_late]).astype(jnp.int32)
    weight = residue_late * jnp.sqrt(-jnp.expm1(-2.0 * rate))
    ends = lax.all_to_all(end, ("y", "xl"), 0, 0, tiled=True)
    conv, query, din = pl.pallas_call(
        conv_kernel,
        out_shape=(
            jax.ShapeDtypeStruct((rows, channels), BF),
            jax.ShapeDtypeStruct((rows, channels), BF),
            jax.ShapeDtypeStruct((CHUNK, flat), BF),
        ),
        grid=(1,),
        in_specs=[
            pl.BlockSpec((None, rows, channels), lambda i: (0, 0, 0)),
            whole((rows, channels)), whole(halo.shape), whole(short_filter.shape),
            whole(rate.shape), whole(rate.shape), whole(rt.shape),
        ],
        out_specs=(whole((rows, channels)), whole((rows, channels)), whole((CHUNK, flat))),
        scratch_shapes=[
            pltpu.VMEM((CHUNK + MODES, groups * CHUNK), BF),
            pltpu.VMEM((channels // LANES, LANES // GROUP * CHUNK, 2 * LANES), BF),
        ],
        compiler_params=pltpu.CompilerParams(vmem_limit_bytes=16 * 2**20),
        cost_estimate=pl.CostEstimate(flops=10**6, bytes_accessed=2**16, transcendentals=0),
        name="conv",
    )(far(projected), signal, halo, far(short_filter), far(rate), weight, rt)
    mixed = pl.pallas_call(
        mix_kernel,
        out_shape=jax.ShapeDtypeStruct((rows, channels), BF),
        in_specs=[SM] + [VM] * 5,
        out_specs=VM,
        compiler_params=pltpu.CompilerParams(vmem_limit_bytes=10 * 2**20),
        cost_estimate=pl.CostEstimate(flops=10**6, bytes_accessed=2**16, transcendentals=0),
        name="mix",
    )(at, ends, rt, din, conv, query)

    a_far = lax.ppermute(mixed, "xh", [(0, 1), (1, 0)])
    a_other = other_core(mixed)
    a_far_other = other_core(a_far)
    core_last, _ = lax.optimization_barrier((core, mixed))
    zero = jnp.minimum(core_last, 0)
    quarter = size // 2
    above, below = (lax.dynamic_slice(fetched, (zero + k * quarter, 0), (quarter, half)) for k in (0, 1))
    above = lax.ppermute(above, "y", [(i, (i + 1) % 4) for i in range(4)])
    below = lax.ppermute(below, "y", [(i, (i - 1) % 4) for i in range(4)])
    w_other = other_core(
        lax.dynamic_slice(out_weight, (0, (xh * 2 + 1 - core_last) * width), (channels, width))
    )
    g0, g1, g2 = (
        other_core(lax.dynamic_slice(v, (0, (1 - core) * width), (v.shape[0], width)))
        for v in (fetched, above, below)
    )

    tile = 512
    strips = width // tile

    def strip(shape):
        return pl.BlockSpec(shape[:-1] + (tile,), lambda i, at_ref: (0, i))

    def half_strip(shape):
        return pl.BlockSpec(shape[:-1] + (tile,), lambda i, at_ref: (0, at_ref[3] * strips + i))

    partial = pl.pallas_call(
        product_kernel,
        out_shape=pltpu.HBM((rows, width), BF),
        grid_spec=pltpu.PrefetchScalarGridSpec(
            num_scalar_prefetch=1,
            grid=(strips,),
            in_specs=[pl.BlockSpec((rows, channels), lambda i, at_ref: (0, 0), **once)] * 4
            + [pl.BlockSpec((channels, tile), lambda i, at_ref: (0, at_ref[2] * strips + i)), strip(w_other.shape)]
            + [half_strip(v.shape) for v in (fetched, above, below)]
            + [strip(v.shape) for v in (g0, g1, g2)],
            out_specs=strip((rows, width)),
            scratch_shapes=[pltpu.VMEM((rows, 4 * channels), BF), pltpu.VMEM((4 * channels, tile), BF)],
        ),
        compiler_params=pltpu.CompilerParams(vmem_limit_bytes=28 * 2**20),
        cost_estimate=pl.CostEstimate(flops=4 * 10**9, bytes_accessed=10 * 2**20, transcendentals=0),
        name="product",
    )(at, mixed, a_other, a_far, a_far_other, far(out_weight), w_other,
      fetched, above, below, g0, g1, g2)

    summed = lax.psum_scatter(partial, "z", scatter_dimension=0, tiled=True)
    size = summed.shape[0] // 4

    def traded(k):
        pairs = [(i, i ^ k) for i in range(4)]
        return lax.ppermute(summed[k * size : (k + 1) * size], ("xh", "c"), pairs)

    return pl.pallas_call(
        join_kernel,
        out_shape=jax.ShapeDtypeStruct((size, 4 * width), BF),
        in_specs=[SM] + [VM] * 4,
        out_specs=VM,
        compiler_params=pltpu.CompilerParams(vmem_limit_bytes=4 * 2**20),
        name="join",
    )(at, summed[:size], traded(1), traded(2), traded(3))


def solution(mesh):
    fine = Mesh(mesh.devices.reshape(4, 2, 8, 2, 2), ("y", "xl", "z", "xh", "c"))
    seq, tp = ("y", "xl"), ("z", "xh", "c")
    placed = (P(None, seq, tp), P(None, None, tp), P(tp, None), P(tp, None), P(tp, None))
    return jax.shard_map(local, mesh=fine, in_specs=placed, out_specs=P(seq + tp, None), check_vma=False)
```

```python
import jax
import jax.numpy as jnp
from jax import lax
from jax.experimental import pallas as pl
from jax.experimental.pallas import tpu as pltpu
from jax.sharding import Mesh, PartitionSpec as P

GROUP = 16
MODES = 16
CHUNK = 128
LANES = 128
BF = jnp.bfloat16
F32 = jnp.float32
VM = pl.BlockSpec(memory_space=pltpu.VMEM)
SM = pl.BlockSpec(memory_space=pltpu.SMEM)


def iota(shape, dim):
    return lax.broadcasted_iota(jnp.int32, shape, dim)


def spread(state):
    width = state.shape[1]
    groups = width // GROUP
    tall = jnp.concatenate([state] * groups, axis=0)
    shape = (groups * MODES, width)
    own = iota(shape, 0) // MODES == iota(shape, 1) // GROUP
    return jnp.where(own, tall, 0.0).astype(BF)


def one_hot(rows, columns, row_size, column_size):
    shape = (rows, columns)
    return (iota(shape, 0) // row_size == iota(shape, 1) // column_size).astype(F32)


def exact_dot(a, b, dims):
    return lax.dot_general(a, b, (dims, ((), ())), precision=lax.Precision.HIGHEST, preferred_element_type=F32)


def by_channel(table, channels):
    return exact_dot(table, one_hot(table.shape[0], channels, 1, GROUP), ((0,), (0,)))


def by_row(table):
    flat = table.shape[0] * MODES
    wide = exact_dot(one_hot(flat, table.shape[0], MODES, 1), table, ((1,), (0,)))
    keep = iota((flat, MODES), 0) % MODES == iota((flat, MODES), 1)
    return jnp.where(keep, wide, 0.0).sum(axis=1, keepdims=True)


def by_lane(table):
    flat = table.shape[0] * MODES
    wide = exact_dot(table, one_hot(table.shape[0], flat, 1, MODES), ((0,), (0,)))
    keep = iota((MODES, flat), 1) % MODES == iota((MODES, flat), 0)
    return jnp.where(keep, wide, 0.0).sum(axis=0, keepdims=True)


def tapped(taps, cur, before):
    ext = jnp.concatenate([before, cur], axis=0)
    skip = before.shape[0]
    one = pltpu.roll(ext, 1, 0)[skip:]
    two = pltpu.roll(ext, 2, 0)[skip:]
    return taps[0:1, :] * cur + taps[1:2, :] * one + taps[2:3, :] * two


def state_kernel(k_ref, v_ref, halo_ref, sf_ref, rate_ref, x_ref, end_ref, rt_ref, tail, total, power):
    step = pl.program_id(0)
    rows, channels = k_ref.shape

    @pl.when(step == 0)
    def _():
        rt = by_channel(rate_ref[...], channels)
        rt_ref[...] = rt
        total[...] = jnp.zeros_like(total)
        for n in range(MODES):
            power[n] = jnp.broadcast_to(jnp.exp(-8.0 * rt[n : n + 1, :]), (8, channels))
        for i in range(2):
            tail[i] = halo_ref[i + 1].astype(F32)

    featured = []
    for i, ref in enumerate((k_ref, v_ref)):
        cur = ref[...].astype(F32)
        featured.append(tapped(sf_ref[i + 1], cur, tail[i]))
        tail[i] = cur[rows - 8 :]
    signal = featured[0] * featured[1]
    x_ref[...] = signal.astype(BF)
    for h in range(channels // LANES):
        lanes = slice(h * LANES, (h + 1) * LANES)
        for first in range(0, MODES, 8):
            sums = [total[n, :, lanes] for n in range(first, first + 8)]
            powers = [power[n, :, lanes] for n in range(first, first + 8)]
            for b in range(rows // 8):
                block = signal[b * 8 : (b + 1) * 8, lanes]
                sums = [s * w + block for s, w in zip(sums, powers)]
            for n in range(8):
                total[first + n, :, lanes] = sums[n]

    @pl.when(step == pl.num_programs(0) - 1)
    def _():
        rt = rt_ref[...]
        ahead = (7 - iota((8, channels), 0)).astype(F32)
        end = jnp.concatenate(
            [
                (total[n] * jnp.exp(-ahead * rt[n : n + 1, :])).sum(axis=0, keepdims=True)
                for n in range(MODES)
            ],
            axis=0,
        )
        for j in range(end_ref.shape[0]):
            end_ref[j] = end


def conv_kernel(p_ref, x_ref, halo_ref, sf_ref, rate_ref, weight_ref, rt_ref,
                y_ref, q_ref, din_ref, table, masked):
    rows, channels = x_ref.shape
    halves = channels // LANES
    per_half = LANES // GROUP
    groups = channels // GROUP
    rate, weight = rate_ref[...], weight_ref[...]
    rcol = by_row(rate)
    wcol = by_row(weight)
    lane = iota((groups * MODES, CHUNK), 1)
    back = jnp.where(lane == 0, 0, CHUNK - lane).astype(F32)
    taps = (wcol * jnp.exp(-rcol * back)).reshape(groups, MODES, CHUNK).sum(axis=1)
    leave = jnp.exp(-rcol * (CHUNK - 1 - lane).astype(F32)).astype(BF)
    causal = iota((CHUNK, CHUNK), 0) >= iota((CHUNK, CHUNK), 1)
    for g in range(groups):
        wide = jnp.broadcast_to(taps[g : g + 1, :], (CHUNK, CHUNK))
        turned = pltpu.roll(wide, 0, 1, stride=1, stride_axis=0)
        table[0:CHUNK, g * CHUNK : (g + 1) * CHUNK] = jnp.where(causal, turned, 0.0).astype(BF)
        table[CHUNK : CHUNK + MODES, g * CHUNK : (g + 1) * CHUNK] = leave[g * MODES : (g + 1) * MODES]
    steps = (iota((CHUNK, groups * MODES), 0) + 1).astype(F32)
    din = (by_lane(weight) * jnp.exp(-by_lane(rate) * steps)).astype(BF)
    din_ref[...] = din
    power = jnp.exp(-rt_ref[...] * float(CHUNK))
    group_lane = iota((CHUNK, LANES), 1) // GROUP

    state = jnp.zeros((MODES, channels), F32)
    for pair in range(rows // (2 * CHUNK)):
        for j in range(2):
            q = 2 * pair + j
            span = slice(q * CHUNK, (q + 1) * CHUNK)
            before = halo_ref[0] if q == 0 else p_ref[q * CHUNK - 16 : q * CHUNK, :]
            q_ref[span, :] = tapped(sf_ref[0], p_ref[span, :].astype(F32), before.astype(F32)).astype(BF)
            for h in range(halves):
                part = x_ref[span, h * LANES : (h + 1) * LANES]
                for g in range(per_half):
                    masked[h, g * CHUNK : (g + 1) * CHUNK, j * LANES : (j + 1) * LANES] = jnp.where(
                        group_lane == g, part, jnp.zeros_like(part)
                    )
        depth = per_half * CHUNK
        made = [
            jnp.dot(table[:, h * depth : (h + 1) * depth], masked[h], preferred_element_type=F32)
            for h in range(halves)
        ]
        for j in range(2):
            q = 2 * pair + j
            full = jnp.concatenate([m[:, j * LANES : (j + 1) * LANES] for m in made], axis=1)
            within = full[:CHUNK]
            if q > 0:
                within = within + jnp.dot(din, spread(state), preferred_element_type=F32)
            y_ref[q * CHUNK : (q + 1) * CHUNK, :] = within.astype(BF)
            state = power * state + full[CHUNK:]


def mix_kernel(at_ref, ends_ref, rt_ref, din_ref, y_ref, q_ref, mixed_ref):
    rows = y_ref.shape[0]
    here = at_ref[0]
    rt = rt_ref[...]
    block_power = jnp.exp(-rt * float(rows))
    state = jnp.zeros(rt.shape, F32)
    for j in range(ends_ref.shape[0]):
        state = jnp.where(j < here, block_power * state + ends_ref[j], state)
    power = jnp.exp(-rt * float(CHUNK))
    din = din_ref[...]
    for q in range(rows // CHUNK):
        span = slice(q * CHUNK, (q + 1) * CHUNK)
        carried = jnp.dot(din, spread(state), preferred_element_type=F32)
        mixed_ref[span, :] = (q_ref[span, :].astype(F32) * (y_ref[span, :].astype(F32) + carried)).astype(BF)
        state = power * state


def side_by_side(left, refs):
    depth = refs[0].shape[1]

    @pl.when(pl.program_id(0) == 0)
    def _():
        for k, ref in enumerate(refs):
            left[:, k * depth : (k + 1) * depth] = ref[...]


def near_kernel(at_ref, a0, a1, w0, w1, c_ref, left, right):
    depth = w0.shape[0]
    side_by_side(left, (a0, a1))
    right[0:depth] = w0[...]
    right[depth : 2 * depth] = w1[...]
    block = 256
    for m in range(left.shape[0] // block):
        span = slice(m * block, (m + 1) * block)
        c_ref[span, :] = jnp.dot(left[span, :], right[...], preferred_element_type=F32).astype(BF)


def far_kernel(at_ref, a2, a3, f0, f1, f2, f3, g013, g2, near_ref, c_ref, left, right):
    y, mine = at_ref[1], at_ref[2]
    size = f0.shape[0]
    depth = right.shape[0] // 2
    tail = depth - 4 * size
    side_by_side(left, (a2, a3))
    for k, ref in enumerate((f0, f1, f2, f3)):
        owner = lax.rem(y - k + 4, 4) * size
        right[pl.ds(pl.multiple_of(owner, 16), size), :] = ref[0:size]
        passed = g2[0:size] if k == 2 else g013[(0, 1, 0, 2)[k] * size : ((0, 1, 0, 2)[k] + 1) * size]
        right[pl.ds(pl.multiple_of(depth + owner, 16), size), :] = passed
    right[4 * size : depth] = f2[size : size + tail]
    right[depth + 4 * size : 2 * depth] = g2[size : size + tail]
    block = 256
    for m in range(left.shape[0] // block):
        span = slice(m * block, (m + 1) * block)
        total = jnp.dot(left[span, :], right[...], preferred_element_type=F32)
        total = (total + near_ref[span, :].astype(F32)).astype(BF)
        for b in range(block // 32):
            high, low = m * (block // 128) + b // 4, b % 4
            place = pl.multiple_of((high * 4 + jnp.bitwise_xor(low, mine)) * 32, 32)
            c_ref[pl.ds(place, 32), :] = total[b * 32 : (b + 1) * 32]


def join_kernel(at_ref, p0, p1, p2, p3, out_ref):
    mine = at_ref[2]
    width = p0.shape[1]
    for k, ref in enumerate((p0, p1, p2, p3)):
        place = pl.multiple_of(jnp.bitwise_xor(mine, k) * width, width)
        out_ref[:, pl.ds(place, width)] = ref[...]


def far(value):
    return pltpu.with_memory_space_constraint(value, pltpu.HBM)


def other_core(value):
    return lax.ppermute(value, "c", [(0, 1), (1, 0)])


def local(projected, short_filter, residue, rate, out_weight):
    rows, channels = projected.shape[1], projected.shape[2]
    groups = rate.shape[0]
    width = out_weight.shape[1] // 4
    y, xh, core = lax.axis_index("y"), lax.axis_index("xh"), lax.axis_index("c")
    seq = lax.axis_index(("y", "xl"))
    edge = projected[:, rows - 8 :, :]
    edge, y_then = lax.optimization_barrier((edge, y))
    halo = lax.ppermute(edge, ("y", "xl"), [(i, i + 1) for i in range(7)])

    size = 48
    tail = channels - 4 * size
    half = 2 * width
    mirror = [(0, 3), (3, 0), (1, 2), (2, 1)]

    def there(source, start, count):
        return lax.dynamic_slice(source, (start, (1 - xh) * half), (count, half))

    f0 = lax.ppermute(there(out_weight, y_then * size, size), ("xl", "xh"), mirror)

    flat = groups * MODES
    span = 256
    once = {"pipeline_mode": pl.Buffered(1)}

    def whole(shape):
        return pl.BlockSpec(shape, lambda i: (0,) * len(shape))

    def third(k):
        return pl.BlockSpec((None, span, channels), lambda i: (k, i, 0))

    signal, end, rt = pl.pallas_call(
        state_kernel,
        out_shape=(
            pltpu.HBM((rows, channels), BF),
            jax.ShapeDtypeStruct((8, MODES, channels), F32),
            jax.ShapeDtypeStruct((MODES, channels), F32),
        ),
        grid=(rows // span,),
        in_specs=[third(1), third(2), whole(halo.shape), whole(short_filter.shape), whole(rate.shape)],
        out_specs=(
            pl.BlockSpec((span, channels), lambda i: (i, 0)),
            whole((8, MODES, channels)),
            whole((MODES, channels)),
        ),
        scratch_shapes=[
            pltpu.VMEM((2, 8, channels), F32),
            pltpu.VMEM((MODES, 8, channels), F32),
            pltpu.VMEM((MODES, 8, channels), F32),
        ],
        compiler_params=pltpu.CompilerParams(vmem_limit_bytes=12 * 2**20),
        cost_estimate=pl.CostEstimate(flops=10**6, bytes_accessed=2**16, transcendentals=0),
        name="state",
    )(far(projected), far(projected), halo, far(short_filter), far(rate))
    end, xh_late, core_late, residue_late, weight_late = lax.optimization_barrier((end, xh, core, residue, out_weight))
    f2 = jnp.concatenate(
        [there(weight_late, lax.rem(y + 2, 4) * size, size), there(weight_late, 4 * size, tail)], axis=0
    )
    f2 = lax.ppermute(f2, ("xl", "xh"), mirror)
    w_other = other_core(
        lax.dynamic_slice(weight_late, (0, (xh_late * 2 + 1 - core_late) * width), (channels, width))
    )
    at = jnp.stack([seq, y, xh_late * 2 + core_late, core_late]).astype(jnp.int32)
    weight = residue_late * jnp.sqrt(-jnp.expm1(-2.0 * rate))
    ends = lax.all_to_all(end, ("y", "xl"), 0, 0, tiled=True)
    conv, query, din = pl.pallas_call(
        conv_kernel,
        out_shape=(
            pltpu.HBM((rows, channels), BF),
            pltpu.HBM((rows, channels), BF),
            jax.ShapeDtypeStruct((CHUNK, flat), BF),
        ),
        grid=(1,),
        in_specs=[
            pl.BlockSpec((None, rows, channels), lambda i: (0, 0, 0)),
            whole((rows, channels)), whole(halo.shape), whole(short_filter.shape),
            whole(rate.shape), whole(rate.shape), whole(rt.shape),
        ],
        out_specs=(whole((rows, channels)), whole((rows, channels)), whole((CHUNK, flat))),
        scratch_shapes=[
            pltpu.VMEM((CHUNK + MODES, groups * CHUNK), BF),
            pltpu.VMEM((channels // LANES, LANES // GROUP * CHUNK, 2 * LANES), BF),
        ],
        compiler_params=pltpu.CompilerParams(vmem_limit_bytes=16 * 2**20),
        cost_estimate=pl.CostEstimate(flops=10**6, bytes_accessed=2**16, transcendentals=0),
        name="conv",
    )(far(projected), far(signal), halo, far(short_filter), far(rate), weight, rt)
    f1 = lax.ppermute(f0, "y", [(i, (i + 1) % 4) for i in range(4)])
    f3 = lax.ppermute(f0, "y", [(i, (i - 1) % 4) for i in range(4)])
    ends, f1, f3 = lax.optimization_barrier((ends, f1, f3))
    mixed = pl.pallas_call(
        mix_kernel,
        out_shape=jax.ShapeDtypeStruct((rows, channels), BF),
        in_specs=[SM] + [VM] * 5,
        out_specs=VM,
        compiler_params=pltpu.CompilerParams(vmem_limit_bytes=10 * 2**20),
        cost_estimate=pl.CostEstimate(flops=10**6, bytes_accessed=2**16, transcendentals=0),
        name="mix",
    )(at, ends, rt, din, far(conv), far(query))

    a_far = lax.ppermute(mixed, "xh", [(0, 1), (1, 0)])
    a_other = other_core(mixed)
    def given(parts):
        return other_core(
            jnp.concatenate([lax.dynamic_slice(v, (0, (1 - core) * width), (v.shape[0], width)) for v in parts], axis=0)
        )

    g013, g2 = given((f0, f1, f3)), given((f2,))

    tile = 512
    strips = width // tile

    def strip(shape):
        return pl.BlockSpec(shape[:-1] + (tile,), lambda i, at_ref: (0, i))

    def half_strip(shape):
        return pl.BlockSpec(shape[:-1] + (tile,), lambda i, at_ref: (0, at_ref[3] * strips + i))

    left_specs = [pl.BlockSpec((rows, channels), lambda i, at_ref: (0, 0), **once)] * 2
    near = pl.pallas_call(
        near_kernel,
        out_shape=jax.ShapeDtypeStruct((rows, width), BF),
        grid_spec=pltpu.PrefetchScalarGridSpec(
            num_scalar_prefetch=1,
            grid=(strips,),
            in_specs=left_specs
            + [pl.BlockSpec((channels, tile), lambda i, at_ref: (0, at_ref[2] * strips + i)), strip(w_other.shape)],
            out_specs=strip((rows, width)),
            scratch_shapes=[pltpu.VMEM((rows, 2 * channels), BF), pltpu.VMEM((2 * channels, tile), BF)],
        ),
        compiler_params=pltpu.CompilerParams(vmem_limit_bytes=16 * 2**20),
        cost_estimate=pl.CostEstimate(flops=2 * 10**9, bytes_accessed=6 * 2**20, transcendentals=0),
        name="near",
    )(at, mixed, a_other, far(out_weight), w_other)
    a_far, near = lax.optimization_barrier((a_far, near))
    a_far_other = other_core(a_far)
    partial = pl.pallas_call(
        far_kernel,
        out_shape=pltpu.HBM((rows, width), BF),
        grid_spec=pltpu.PrefetchScalarGridSpec(
            num_scalar_prefetch=1,
            grid=(strips,),
            in_specs=left_specs
            + [half_strip(v.shape) for v in (f0, f1, f2, f3)]
            + [strip(g013.shape), strip(g2.shape)]
            + [strip((rows, width))],
            out_specs=strip((rows, width)),
            scratch_shapes=[pltpu.VMEM((rows, 2 * channels), BF), pltpu.VMEM((2 * channels, tile), BF)],
        ),
        compiler_params=pltpu.CompilerParams(vmem_limit_bytes=20 * 2**20),
        cost_estimate=pl.CostEstimate(flops=2 * 10**9, bytes_accessed=10 * 2**20, transcendentals=0),
        name="far",
    )(at, a_far, a_far_other, f0, f1, f2, f3, g013, g2, near)

    summed = lax.psum_scatter(partial, "z", scatter_dimension=0, tiled=True)
    size = summed.shape[0] // 4

    def traded(k):
        pairs = [(i, i ^ k) for i in range(4)]
        return lax.ppermute(summed[k * size : (k + 1) * size], ("xh", "c"), pairs)

    return pl.pallas_call(
        join_kernel,
        out_shape=jax.ShapeDtypeStruct((size, 4 * width), BF),
        in_specs=[SM] + [VM] * 4,
        out_specs=VM,
        compiler_params=pltpu.CompilerParams(vmem_limit_bytes=4 * 2**20),
        name="join",
    )(at, summed[:size], traded(1), traded(2), traded(3))


def solution(mesh):
    fine = Mesh(mesh.devices.reshape(4, 2, 8, 2, 2), ("y", "xl", "z", "xh", "c"))
    seq, tp = ("y", "xl"), ("z", "xh", "c")
    placed = (P(None, seq, tp), P(None, None, tp), P(tp, None), P(tp, None), P(tp, None))
    return jax.shard_map(local, mesh=fine, in_specs=placed, out_specs=P(seq + tp, None), check_vma=False)
```

```python
import jax
import jax.numpy as jnp
from jax import lax
from jax.experimental import pallas as pl
from jax.experimental.pallas import tpu as pltpu
from jax.sharding import Mesh, PartitionSpec as P

GROUP = 16
MODES = 16
CHUNK = 128
LANES = 128
BF = jnp.bfloat16
F32 = jnp.float32
VM = pl.BlockSpec(memory_space=pltpu.VMEM)
SM = pl.BlockSpec(memory_space=pltpu.SMEM)


def iota(shape, dim):
    return lax.broadcasted_iota(jnp.int32, shape, dim)


def spread(state):
    width = state.shape[1]
    groups = width // GROUP
    tall = jnp.concatenate([state] * groups, axis=0)
    shape = (groups * MODES, width)
    own = iota(shape, 0) // MODES == iota(shape, 1) // GROUP
    return jnp.where(own, tall, 0.0).astype(BF)


def one_hot(rows, columns, row_size, column_size):
    shape = (rows, columns)
    return (iota(shape, 0) // row_size == iota(shape, 1) // column_size).astype(F32)


def exact_dot(a, b, dims):
    return lax.dot_general(a, b, (dims, ((), ())), precision=lax.Precision.HIGHEST, preferred_element_type=F32)


def by_channel(table, channels):
    return exact_dot(table, one_hot(table.shape[0], channels, 1, GROUP), ((0,), (0,)))


def by_row(table):
    flat = table.shape[0] * MODES
    wide = exact_dot(one_hot(flat, table.shape[0], MODES, 1), table, ((1,), (0,)))
    keep = iota((flat, MODES), 0) % MODES == iota((flat, MODES), 1)
    return jnp.where(keep, wide, 0.0).sum(axis=1, keepdims=True)


def by_lane(table):
    flat = table.shape[0] * MODES
    wide = exact_dot(table, one_hot(table.shape[0], flat, 1, MODES), ((0,), (0,)))
    keep = iota((MODES, flat), 1) % MODES == iota((MODES, flat), 0)
    return jnp.where(keep, wide, 0.0).sum(axis=0, keepdims=True)


def tapped(taps, cur, before):
    ext = jnp.concatenate([before, cur], axis=0)
    skip = before.shape[0]
    one = pltpu.roll(ext, 1, 0)[skip:]
    two = pltpu.roll(ext, 2, 0)[skip:]
    return taps[0:1, :] * cur + taps[1:2, :] * one + taps[2:3, :] * two


def state_kernel(k_ref, v_ref, halo_ref, sf_ref, rate_ref, x_ref, end_ref, rt_ref, tail, total, power):
    step = pl.program_id(0)
    rows, channels = k_ref.shape

    @pl.when(step == 0)
    def _():
        rt = by_channel(rate_ref[...], channels)
        rt_ref[...] = rt
        total[...] = jnp.zeros_like(total)
        for n in range(MODES):
            power[n] = jnp.broadcast_to(jnp.exp(-8.0 * rt[n : n + 1, :]), (8, channels))
        for i in range(2):
            tail[i] = halo_ref[i + 1].astype(F32)

    featured = []
    for i, ref in enumerate((k_ref, v_ref)):
        cur = ref[...].astype(F32)
        featured.append(tapped(sf_ref[i + 1], cur, tail[i]))
        tail[i] = cur[rows - 8 :]
    signal = featured[0] * featured[1]
    x_ref[...] = signal.astype(BF)
    for h in range(channels // LANES):
        lanes = slice(h * LANES, (h + 1) * LANES)
        for first in range(0, MODES, 8):
            sums = [total[n, :, lanes] for n in range(first, first + 8)]
            powers = [power[n, :, lanes] for n in range(first, first + 8)]
            for b in range(rows // 8):
                block = signal[b * 8 : (b + 1) * 8, lanes]
                sums = [s * w + block for s, w in zip(sums, powers)]
            for n in range(8):
                total[first + n, :, lanes] = sums[n]

    @pl.when(step == pl.num_programs(0) - 1)
    def _():
        rt = rt_ref[...]
        ahead = (7 - iota((8, channels), 0)).astype(F32)
        end = jnp.concatenate(
            [
                (total[n] * jnp.exp(-ahead * rt[n : n + 1, :])).sum(axis=0, keepdims=True)
                for n in range(MODES)
            ],
            axis=0,
        )
        for j in range(end_ref.shape[0]):
            end_ref[j] = end


def conv_kernel(p_ref, x_ref, halo_ref, sf_ref, rate_ref, weight_ref, rt_ref,
                y_ref, q_ref, din_ref, table, masked):
    rows, channels = x_ref.shape
    halves = channels // LANES
    per_half = LANES // GROUP
    groups = channels // GROUP
    rate, weight = rate_ref[...], weight_ref[...]
    rcol = by_row(rate)
    wcol = by_row(weight)
    lane = iota((groups * MODES, CHUNK), 1)
    back = jnp.where(lane == 0, 0, CHUNK - lane).astype(F32)
    taps = (wcol * jnp.exp(-rcol * back)).reshape(groups, MODES, CHUNK).sum(axis=1)
    leave = jnp.exp(-rcol * (CHUNK - 1 - lane).astype(F32)).astype(BF)
    causal = iota((CHUNK, CHUNK), 0) >= iota((CHUNK, CHUNK), 1)
    for g in range(groups):
        wide = jnp.broadcast_to(taps[g : g + 1, :], (CHUNK, CHUNK))
        turned = pltpu.roll(wide, 0, 1, stride=1, stride_axis=0)
        table[0:CHUNK, g * CHUNK : (g + 1) * CHUNK] = jnp.where(causal, turned, 0.0).astype(BF)
        table[CHUNK : CHUNK + MODES, g * CHUNK : (g + 1) * CHUNK] = leave[g * MODES : (g + 1) * MODES]
    steps = (iota((CHUNK, groups * MODES), 0) + 1).astype(F32)
    din = (by_lane(weight) * jnp.exp(-by_lane(rate) * steps)).astype(BF)
    din_ref[...] = din
    power = jnp.exp(-rt_ref[...] * float(CHUNK))
    group_lane = iota((CHUNK, LANES), 1) // GROUP

    state = jnp.zeros((MODES, channels), F32)
    for pair in range(rows // (2 * CHUNK)):
        for j in range(2):
            q = 2 * pair + j
            span = slice(q * CHUNK, (q + 1) * CHUNK)
            before = halo_ref[0] if q == 0 else p_ref[q * CHUNK - 16 : q * CHUNK, :]
            q_ref[span, :] = tapped(sf_ref[0], p_ref[span, :].astype(F32), before.astype(F32)).astype(BF)
            for h in range(halves):
                part = x_ref[span, h * LANES : (h + 1) * LANES]
                for g in range(per_half):
                    masked[h, g * CHUNK : (g + 1) * CHUNK, j * LANES : (j + 1) * LANES] = jnp.where(
                        group_lane == g, part, jnp.zeros_like(part)
                    )
        depth = per_half * CHUNK
        made = [
            jnp.dot(table[:, h * depth : (h + 1) * depth], masked[h], preferred_element_type=F32)
            for h in range(halves)
        ]
        for j in range(2):
            q = 2 * pair + j
            full = jnp.concatenate([m[:, j * LANES : (j + 1) * LANES] for m in made], axis=1)
            within = full[:CHUNK]
            if q > 0:
                within = within + jnp.dot(din, spread(state), preferred_element_type=F32)
            y_ref[q * CHUNK : (q + 1) * CHUNK, :] = within.astype(BF)
            state = power * state + full[CHUNK:]


def mix_kernel(at_ref, ends_ref, rt_ref, din_ref, y_ref, q_ref, mixed_ref):
    rows = y_ref.shape[0]
    here = at_ref[0]
    rt = rt_ref[...]
    block_power = jnp.exp(-rt * float(rows))
    state = jnp.zeros(rt.shape, F32)
    for j in range(ends_ref.shape[0]):
        state = jnp.where(j < here, block_power * state + ends_ref[j], state)
    power = jnp.exp(-rt * float(CHUNK))
    din = din_ref[...]
    for q in range(rows // CHUNK):
        span = slice(q * CHUNK, (q + 1) * CHUNK)
        carried = jnp.dot(din, spread(state), preferred_element_type=F32)
        mixed_ref[span, :] = (q_ref[span, :].astype(F32) * (y_ref[span, :].astype(F32) + carried)).astype(BF)
        state = power * state


def side_by_side(left, refs):
    depth = refs[0].shape[1]

    @pl.when(pl.program_id(0) == 0)
    def _():
        for k, ref in enumerate(refs):
            left[:, k * depth : (k + 1) * depth] = ref[...]


def near_kernel(at_ref, a0, a1, w0, w1, c_ref, left, right):
    depth = w0.shape[0]
    side_by_side(left, (a0, a1))
    right[0:depth] = w0[...]
    right[depth : 2 * depth] = w1[...]
    block = 256
    for m in range(left.shape[0] // block):
        span = slice(m * block, (m + 1) * block)
        c_ref[span, :] = jnp.dot(left[span, :], right[...], preferred_element_type=F32).astype(BF)


def far_kernel(at_ref, a2, a3, f0, f1, f2, f3, rest, g013, g2, near_ref, c_ref, left, right):
    y, mine = at_ref[1], at_ref[2]
    size = f0.shape[0]
    depth = right.shape[0] // 2
    tail = depth - 4 * size
    side_by_side(left, (a2, a3))
    for k, ref in enumerate((f0, f1, f2, f3)):
        owner = lax.rem(y - k + 4, 4) * size
        right[pl.ds(pl.multiple_of(owner, 16), size), :] = ref[0:size]
        passed = g2[0:size] if k == 2 else g013[(0, 1, 0, 2)[k] * size : ((0, 1, 0, 2)[k] + 1) * size]
        right[pl.ds(pl.multiple_of(depth + owner, 16), size), :] = passed
    right[4 * size : depth] = rest[...]
    right[depth + 4 * size : 2 * depth] = g013[3 * size : 3 * size + tail]
    block = 256
    for m in range(left.shape[0] // block):
        span = slice(m * block, (m + 1) * block)
        total = jnp.dot(left[span, :], right[...], preferred_element_type=F32)
        total = (total + near_ref[span, :].astype(F32)).astype(BF)
        for b in range(block // 32):
            high, low = m * (block // 128) + b // 4, b % 4
            place = pl.multiple_of((high * 4 + jnp.bitwise_xor(low, mine)) * 32, 32)
            c_ref[pl.ds(place, 32), :] = total[b * 32 : (b + 1) * 32]


def join_kernel(at_ref, p0, p1, p2, p3, out_ref):
    mine = at_ref[2]
    width = p0.shape[1]
    for k, ref in enumerate((p0, p1, p2, p3)):
        place = pl.multiple_of(jnp.bitwise_xor(mine, k) * width, width)
        out_ref[:, pl.ds(place, width)] = ref[...]


def far(value):
    return pltpu.with_memory_space_constraint(value, pltpu.HBM)


def other_core(value):
    return lax.ppermute(value, "c", [(0, 1), (1, 0)])


def local(projected, short_filter, residue, rate, out_weight):
    rows, channels = projected.shape[1], projected.shape[2]
    groups = rate.shape[0]
    width = out_weight.shape[1] // 4
    y, xh, core = lax.axis_index("y"), lax.axis_index("xh"), lax.axis_index("c")
    seq = lax.axis_index(("y", "xl"))
    edge = projected[:, rows - 8 :, :]
    edge, y_then = lax.optimization_barrier((edge, y))
    halo = lax.ppermute(edge, ("y", "xl"), [(i, i + 1) for i in range(7)])

    size = 48
    tail = channels - 4 * size
    half = 2 * width
    mirror = [(0, 3), (3, 0), (1, 2), (2, 1)]

    def there(source, start, count):
        return lax.dynamic_slice(source, (start, (1 - xh) * half), (count, half))

    f0 = lax.ppermute(there(out_weight, y_then * size, size), ("xl", "xh"), mirror)
    rest = lax.ppermute(there(out_weight, 4 * size, tail), ("xl", "xh"), mirror)

    flat = groups * MODES
    span = 256
    once = {"pipeline_mode": pl.Buffered(1)}

    def whole(shape):
        return pl.BlockSpec(shape, lambda i: (0,) * len(shape))

    def third(k):
        return pl.BlockSpec((None, span, channels), lambda i: (k, i, 0))

    signal, end, rt = pl.pallas_call(
        state_kernel,
        out_shape=(
            pltpu.HBM((rows, channels), BF),
            jax.ShapeDtypeStruct((8, MODES, channels), F32),
            jax.ShapeDtypeStruct((MODES, channels), F32),
        ),
        grid=(rows // span,),
        in_specs=[third(1), third(2), whole(halo.shape), whole(short_filter.shape), whole(rate.shape)],
        out_specs=(
            pl.BlockSpec((span, channels), lambda i: (i, 0)),
            whole((8, MODES, channels)),
            whole((MODES, channels)),
        ),
        scratch_shapes=[
            pltpu.VMEM((2, 8, channels), F32),
            pltpu.VMEM((MODES, 8, channels), F32),
            pltpu.VMEM((MODES, 8, channels), F32),
        ],
        compiler_params=pltpu.CompilerParams(vmem_limit_bytes=12 * 2**20),
        cost_estimate=pl.CostEstimate(flops=10**6, bytes_accessed=2**16, transcendentals=0),
        name="state",
    )(far(projected), far(projected), halo, far(short_filter), far(rate))
    end, residue_late, core_late = lax.optimization_barrier((end, residue, core))
    at = jnp.stack([seq, y, xh * 2 + core, core]).astype(jnp.int32)
    weight = residue_late * jnp.sqrt(-jnp.expm1(-2.0 * rate))
    ends = lax.all_to_all(end, ("y", "xl"), 0, 0, tiled=True)
    conv, query, din = pl.pallas_call(
        conv_kernel,
        out_shape=(
            pltpu.HBM((rows, channels), BF),
            pltpu.HBM((rows, channels), BF),
            jax.ShapeDtypeStruct((CHUNK, flat), BF),
        ),
        grid=(1,),
        in_specs=[
            pl.BlockSpec((None, rows, channels), lambda i: (0, 0, 0)),
            whole((rows, channels)), whole(halo.shape), whole(short_filter.shape),
            whole(rate.shape), whole(rate.shape), whole(rt.shape),
        ],
        out_specs=(whole((rows, channels)), whole((rows, channels)), whole((CHUNK, flat))),
        scratch_shapes=[
            pltpu.VMEM((CHUNK + MODES, groups * CHUNK), BF),
            pltpu.VMEM((channels // LANES, LANES // GROUP * CHUNK, 2 * LANES), BF),
        ],
        compiler_params=pltpu.CompilerParams(vmem_limit_bytes=16 * 2**20),
        cost_estimate=pl.CostEstimate(flops=6 * 10**9, bytes_accessed=2**16, transcendentals=0),
        name="conv",
    )(far(projected), far(signal), halo, far(short_filter), far(rate), weight, rt)
    f1 = lax.ppermute(f0, "y", [(i, (i + 1) % 4) for i in range(4)])
    f3 = lax.ppermute(f0, "y", [(i, (i - 1) % 4) for i in range(4)])
    ends, f1, f3, rest, f0_late = lax.optimization_barrier((ends, f1, f3, rest, f0))
    f2 = lax.ppermute(f0_late, "y", [(i, (i + 2) % 4) for i in range(4)])
    w_other = other_core(
        lax.dynamic_slice(out_weight, (0, (xh * 2 + 1 - core_late) * width), (channels, width))
    )
    mixed = pl.pallas_call(
        mix_kernel,
        out_shape=jax.ShapeDtypeStruct((rows, channels), BF),
        in_specs=[SM] + [VM] * 5,
        out_specs=VM,
        compiler_params=pltpu.CompilerParams(vmem_limit_bytes=10 * 2**20),
        cost_estimate=pl.CostEstimate(flops=10**6, bytes_accessed=2**16, transcendentals=0),
        name="mix",
    )(at, ends, rt, din, far(conv), far(query))

    a_far = lax.ppermute(mixed, "xh", [(0, 1), (1, 0)])
    a_other = other_core(mixed)
    def given(parts):
        return other_core(
            jnp.concatenate([lax.dynamic_slice(v, (0, (1 - core) * width), (v.shape[0], width)) for v in parts], axis=0)
        )

    g013, g2 = given((f0_late, f1, f3, rest)), given((f2,))

    tile = 512
    strips = width // tile

    def strip(shape):
        return pl.BlockSpec(shape[:-1] + (tile,), lambda i, at_ref: (0, i))

    def half_strip(shape):
        return pl.BlockSpec(shape[:-1] + (tile,), lambda i, at_ref: (0, at_ref[3] * strips + i))

    left_specs = [pl.BlockSpec((rows, channels), lambda i, at_ref: (0, 0), **once)] * 2
    near = pl.pallas_call(
        near_kernel,
        out_shape=jax.ShapeDtypeStruct((rows, width), BF),
        grid_spec=pltpu.PrefetchScalarGridSpec(
            num_scalar_prefetch=1,
            grid=(strips,),
            in_specs=left_specs
            + [pl.BlockSpec((channels, tile), lambda i, at_ref: (0, at_ref[2] * strips + i)), strip(w_other.shape)],
            out_specs=strip((rows, width)),
            scratch_shapes=[pltpu.VMEM((rows, 2 * channels), BF), pltpu.VMEM((2 * channels, tile), BF)],
        ),
        compiler_params=pltpu.CompilerParams(vmem_limit_bytes=16 * 2**20),
        cost_estimate=pl.CostEstimate(flops=2 * 10**9, bytes_accessed=6 * 2**20, transcendentals=0),
        name="near",
    )(at, mixed, a_other, far(out_weight), w_other)
    a_far, near = lax.optimization_barrier((a_far, near))
    a_far_other = other_core(a_far)
    partial = pl.pallas_call(
        far_kernel,
        out_shape=pltpu.HBM((rows, width), BF),
        grid_spec=pltpu.PrefetchScalarGridSpec(
            num_scalar_prefetch=1,
            grid=(strips,),
            in_specs=left_specs
            + [half_strip(v.shape) for v in (f0, f1, f2, f3, rest)]
            + [strip(g013.shape), strip(g2.shape)]
            + [strip((rows, width))],
            out_specs=strip((rows, width)),
            scratch_shapes=[pltpu.VMEM((rows, 2 * channels), BF), pltpu.VMEM((2 * channels, tile), BF)],
        ),
        compiler_params=pltpu.CompilerParams(vmem_limit_bytes=20 * 2**20),
        cost_estimate=pl.CostEstimate(flops=2 * 10**9, bytes_accessed=10 * 2**20, transcendentals=0),
        name="far",
    )(at, a_far, a_far_other, f0_late, f1, f2, f3, rest, g013, g2, near)

    summed = lax.psum_scatter(partial, "z", scatter_dimension=0, tiled=True)
    size = summed.shape[0] // 4

    def traded(k):
        pairs = [(i, i ^ k) for i in range(4)]
        return lax.ppermute(summed[k * size : (k + 1) * size], ("xh", "c"), pairs)

    return pl.pallas_call(
        join_kernel,
        out_shape=jax.ShapeDtypeStruct((size, 4 * width), BF),
        in_specs=[SM] + [VM] * 4,
        out_specs=VM,
        compiler_params=pltpu.CompilerParams(vmem_limit_bytes=4 * 2**20),
        name="join",
    )(at, summed[:size], traded(1), traded(2), traded(3))


def solution(mesh):
    fine = Mesh(mesh.devices.reshape(4, 2, 8, 2, 2), ("y", "xl", "z", "xh", "c"))
    seq, tp = ("y", "xl"), ("z", "xh", "c")
    placed = (P(None, seq, tp), P(None, None, tp), P(tp, None), P(tp, None), P(tp, None))
    return jax.shard_map(local, mesh=fine, in_specs=placed, out_specs=P(seq + tp, None), check_vma=False)
```

```python
import jax
import jax.numpy as jnp
from jax import lax
from jax.experimental import pallas as pl
from jax.experimental.pallas import tpu as pltpu
from jax.sharding import Mesh, PartitionSpec as P

GROUP = 16
MODES = 16
CHUNK = 128
LANES = 128
BF = jnp.bfloat16
F32 = jnp.float32
VM = pl.BlockSpec(memory_space=pltpu.VMEM)
SM = pl.BlockSpec(memory_space=pltpu.SMEM)


def iota(shape, dim):
    return lax.broadcasted_iota(jnp.int32, shape, dim)


def spread(state):
    width = state.shape[1]
    groups = width // GROUP
    tall = jnp.concatenate([state] * groups, axis=0)
    shape = (groups * MODES, width)
    own = iota(shape, 0) // MODES == iota(shape, 1) // GROUP
    return jnp.where(own, tall, 0.0).astype(BF)


def one_hot(rows, columns, row_size, column_size):
    shape = (rows, columns)
    return (iota(shape, 0) // row_size == iota(shape, 1) // column_size).astype(F32)


def exact_dot(a, b, dims):
    return lax.dot_general(a, b, (dims, ((), ())), precision=lax.Precision.HIGHEST, preferred_element_type=F32)


def by_channel(table, channels):
    return exact_dot(table, one_hot(table.shape[0], channels, 1, GROUP), ((0,), (0,)))


def by_row(table):
    flat = table.shape[0] * MODES
    wide = exact_dot(one_hot(flat, table.shape[0], MODES, 1), table, ((1,), (0,)))
    keep = iota((flat, MODES), 0) % MODES == iota((flat, MODES), 1)
    return jnp.where(keep, wide, 0.0).sum(axis=1, keepdims=True)


def by_lane(table):
    flat = table.shape[0] * MODES
    wide = exact_dot(table, one_hot(table.shape[0], flat, 1, MODES), ((0,), (0,)))
    keep = iota((MODES, flat), 1) % MODES == iota((MODES, flat), 0)
    return jnp.where(keep, wide, 0.0).sum(axis=0, keepdims=True)


def tapped(taps, cur, before):
    ext = jnp.concatenate([before, cur], axis=0)
    skip = before.shape[0]
    one = pltpu.roll(ext, 1, 0)[skip:]
    two = pltpu.roll(ext, 2, 0)[skip:]
    return taps[0:1, :] * cur + taps[1:2, :] * one + taps[2:3, :] * two


def state_kernel(k_ref, v_ref, halo_ref, sf_ref, rate_ref, x_ref, end_ref, rt_ref, tail, total, power):
    step = pl.program_id(0)
    rows, channels = k_ref.shape

    @pl.when(step == 0)
    def _():
        rt = by_channel(rate_ref[...], channels)
        rt_ref[...] = rt
        total[...] = jnp.zeros_like(total)
        for n in range(MODES):
            power[n] = jnp.broadcast_to(jnp.exp(-8.0 * rt[n : n + 1, :]), (8, channels))
        for i in range(2):
            tail[i] = halo_ref[i + 1].astype(F32)

    featured = []
    for i, ref in enumerate((k_ref, v_ref)):
        cur = ref[...].astype(F32)
        featured.append(tapped(sf_ref[i + 1], cur, tail[i]))
        tail[i] = cur[rows - 8 :]
    signal = featured[0] * featured[1]
    x_ref[...] = signal.astype(BF)
    for h in range(channels // LANES):
        lanes = slice(h * LANES, (h + 1) * LANES)
        for first in range(0, MODES, 8):
            sums = [total[n, :, lanes] for n in range(first, first + 8)]
            powers = [power[n, :, lanes] for n in range(first, first + 8)]
            for b in range(rows // 8):
                block = signal[b * 8 : (b + 1) * 8, lanes]
                sums = [s * w + block for s, w in zip(sums, powers)]
            for n in range(8):
                total[first + n, :, lanes] = sums[n]

    @pl.when(step == pl.num_programs(0) - 1)
    def _():
        rt = rt_ref[...]
        ahead = (7 - iota((8, channels), 0)).astype(F32)
        end = jnp.concatenate(
            [
                (total[n] * jnp.exp(-ahead * rt[n : n + 1, :])).sum(axis=0, keepdims=True)
                for n in range(MODES)
            ],
            axis=0,
        )
        for j in range(end_ref.shape[0]):
            end_ref[j] = end


def conv_kernel(p_ref, x_ref, halo_ref, sf_ref, rate_ref, weight_ref, rt_ref,
                y_ref, q_ref, din_ref, table, masked):
    rows, channels = x_ref.shape
    halves = channels // LANES
    per_half = LANES // GROUP
    groups = channels // GROUP
    rate, weight = rate_ref[...], weight_ref[...]
    rcol = by_row(rate)
    wcol = by_row(weight)
    lane = iota((groups * MODES, CHUNK), 1)
    back = jnp.where(lane == 0, 0, CHUNK - lane).astype(F32)
    taps = (wcol * jnp.exp(-rcol * back)).reshape(groups, MODES, CHUNK).sum(axis=1)
    leave = jnp.exp(-rcol * (CHUNK - 1 - lane).astype(F32)).astype(BF)
    causal = iota((CHUNK, CHUNK), 0) >= iota((CHUNK, CHUNK), 1)
    for g in range(groups):
        wide = jnp.broadcast_to(taps[g : g + 1, :], (CHUNK, CHUNK))
        turned = pltpu.roll(wide, 0, 1, stride=1, stride_axis=0)
        table[0:CHUNK, g * CHUNK : (g + 1) * CHUNK] = jnp.where(causal, turned, 0.0).astype(BF)
        table[CHUNK : CHUNK + MODES, g * CHUNK : (g + 1) * CHUNK] = leave[g * MODES : (g + 1) * MODES]
    steps = (iota((CHUNK, groups * MODES), 0) + 1).astype(F32)
    din = (by_lane(weight) * jnp.exp(-by_lane(rate) * steps)).astype(BF)
    din_ref[...] = din
    power = jnp.exp(-rt_ref[...] * float(CHUNK))
    group_lane = iota((CHUNK, LANES), 1) // GROUP

    state = jnp.zeros((MODES, channels), F32)
    for pair in range(rows // (2 * CHUNK)):
        for j in range(2):
            q = 2 * pair + j
            span = slice(q * CHUNK, (q + 1) * CHUNK)
            before = halo_ref[0] if q == 0 else p_ref[q * CHUNK - 16 : q * CHUNK, :]
            q_ref[span, :] = tapped(sf_ref[0], p_ref[span, :].astype(F32), before.astype(F32)).astype(BF)
            for h in range(halves):
                part = x_ref[span, h * LANES : (h + 1) * LANES]
                for g in range(per_half):
                    masked[h, g * CHUNK : (g + 1) * CHUNK, j * LANES : (j + 1) * LANES] = jnp.where(
                        group_lane == g, part, jnp.zeros_like(part)
                    )
        depth = per_half * CHUNK
        made = [
            jnp.dot(table[:, h * depth : (h + 1) * depth], masked[h], preferred_element_type=F32)
            for h in range(halves)
        ]
        for j in range(2):
            q = 2 * pair + j
            full = jnp.concatenate([m[:, j * LANES : (j + 1) * LANES] for m in made], axis=1)
            within = full[:CHUNK]
            if q > 0:
                within = within + jnp.dot(din, spread(state), preferred_element_type=F32)
            y_ref[q * CHUNK : (q + 1) * CHUNK, :] = within.astype(BF)
            state = power * state + full[CHUNK:]


def mix_kernel(at_ref, ends_ref, rt_ref, din_ref, y_ref, q_ref, mixed_ref):
    rows = y_ref.shape[0]
    here = at_ref[0]
    rt = rt_ref[...]
    block_power = jnp.exp(-rt * float(rows))
    state = jnp.zeros(rt.shape, F32)
    for j in range(ends_ref.shape[0]):
        state = jnp.where(j < here, block_power * state + ends_ref[j], state)
    power = jnp.exp(-rt * float(CHUNK))
    din = din_ref[...]
    for q in range(rows // CHUNK):
        span = slice(q * CHUNK, (q + 1) * CHUNK)
        carried = jnp.dot(din, spread(state), preferred_element_type=F32)
        mixed_ref[span, :] = (q_ref[span, :].astype(F32) * (y_ref[span, :].astype(F32) + carried)).astype(BF)
        state = power * state


def side_by_side(left, refs):
    depth = refs[0].shape[1]

    @pl.when(pl.program_id(0) == 0)
    def _():
        for k, ref in enumerate(refs):
            left[:, k * depth : (k + 1) * depth] = ref[...]


def near_kernel(at_ref, a0, a1, w0, w1, c_ref, left, right):
    depth = w0.shape[0]
    side_by_side(left, (a0, a1))
    right[0:depth] = w0[...]
    right[depth : 2 * depth] = w1[...]
    block = 256
    for m in range(left.shape[0] // block):
        span = slice(m * block, (m + 1) * block)
        c_ref[span, :] = jnp.dot(left[span, :], right[...], preferred_element_type=F32).astype(BF)


def far_kernel(at_ref, a2, a3, f0, f1, f2, f3, rest, g013, g2, near_ref, c_ref, left, right):
    y, mine = at_ref[1], at_ref[2]
    size = f0.shape[0]
    depth = right.shape[0] // 2
    tail = depth - 4 * size
    side_by_side(left, (a2, a3))
    for k, ref in enumerate((f0, f1, f2, f3)):
        owner = lax.rem(y - k + 4, 4) * size
        right[pl.ds(pl.multiple_of(owner, 16), size), :] = ref[0:size]
        passed = g2[0:size] if k == 2 else g013[(0, 1, 0, 2)[k] * size : ((0, 1, 0, 2)[k] + 1) * size]
        right[pl.ds(pl.multiple_of(depth + owner, 16), size), :] = passed
    right[4 * size : depth] = rest[...]
    right[depth + 4 * size : 2 * depth] = g013[3 * size : 3 * size + tail]
    block = 256
    for m in range(left.shape[0] // block):
        span = slice(m * block, (m + 1) * block)
        total = jnp.dot(left[span, :], right[...], preferred_element_type=F32)
        total = (total + near_ref[span, :].astype(F32)).astype(BF)
        for b in range(block // 32):
            high, low = m * (block // 128) + b // 4, b % 4
            place = pl.multiple_of((high * 4 + jnp.bitwise_xor(low, mine)) * 32, 32)
            c_ref[pl.ds(place, 32), :] = total[b * 32 : (b + 1) * 32]


def join_kernel(at_ref, p0, p1, p2, p3, out_ref):
    mine = at_ref[2]
    width = p0.shape[1]
    for k, ref in enumerate((p0, p1, p2, p3)):
        place = pl.multiple_of(jnp.bitwise_xor(mine, k) * width, width)
        out_ref[:, pl.ds(place, width)] = ref[...]


def far(value):
    return pltpu.with_memory_space_constraint(value, pltpu.HBM)


def other_core(value):
    return lax.ppermute(value, "c", [(0, 1), (1, 0)])


def local(projected, short_filter, residue, rate, out_weight):
    rows, channels = projected.shape[1], projected.shape[2]
    groups = rate.shape[0]
    width = out_weight.shape[1] // 4
    y, xh, core = lax.axis_index("y"), lax.axis_index("xh"), lax.axis_index("c")
    seq = lax.axis_index(("y", "xl"))
    edge = projected[:, rows - 8 :, :]
    edge, y_then = lax.optimization_barrier((edge, y))
    halo = lax.ppermute(edge, ("y", "xl"), [(i, i + 1) for i in range(7)])

    size = 48
    tail = channels - 4 * size
    half = 2 * width
    mirror = [(0, 3), (3, 0), (1, 2), (2, 1)]

    def there(source, start, count):
        return lax.dynamic_slice(source, (start, (1 - xh) * half), (count, half))

    f0 = lax.ppermute(there(out_weight, y_then * size, size), ("xl", "xh"), mirror)
    rest = lax.ppermute(there(out_weight, 4 * size, tail), ("xl", "xh"), mirror)

    flat = groups * MODES
    span = 256
    once = {"pipeline_mode": pl.Buffered(1)}

    def whole(shape):
        return pl.BlockSpec(shape, lambda i: (0,) * len(shape))

    def third(k):
        return pl.BlockSpec((None, span, channels), lambda i: (k, i, 0))

    signal, end, rt = pl.pallas_call(
        state_kernel,
        out_shape=(
            pltpu.HBM((rows, channels), BF),
            jax.ShapeDtypeStruct((8, MODES, channels), F32),
            jax.ShapeDtypeStruct((MODES, channels), F32),
        ),
        grid=(rows // span,),
        in_specs=[third(1), third(2), whole(halo.shape), whole(short_filter.shape), whole(rate.shape)],
        out_specs=(
            pl.BlockSpec((span, channels), lambda i: (i, 0)),
            whole((8, MODES, channels)),
            whole((MODES, channels)),
        ),
        scratch_shapes=[
            pltpu.VMEM((2, 8, channels), F32),
            pltpu.VMEM((MODES, 8, channels), F32),
            pltpu.VMEM((MODES, 8, channels), F32),
        ],
        compiler_params=pltpu.CompilerParams(vmem_limit_bytes=12 * 2**20),
        cost_estimate=pl.CostEstimate(flops=10**6, bytes_accessed=2**16, transcendentals=0),
        name="state",
    )(far(projected), far(projected), halo, far(short_filter), far(rate))
    end, residue_late = lax.optimization_barrier((end, residue))
    at = jnp.stack([seq, y, xh * 2 + core, core]).astype(jnp.int32)
    weight = residue_late * jnp.sqrt(-jnp.expm1(-2.0 * rate))
    ends = lax.all_to_all(end, ("y", "xl"), 0, 0, tiled=True)
    conv, query, din = pl.pallas_call(
        conv_kernel,
        out_shape=(
            pltpu.HBM((rows, channels), BF),
            pltpu.HBM((rows, channels), BF),
            jax.ShapeDtypeStruct((CHUNK, flat), BF),
        ),
        grid=(1,),
        in_specs=[
            pl.BlockSpec((None, rows, channels), lambda i: (0, 0, 0)),
            whole((rows, channels)), whole(halo.shape), whole(short_filter.shape),
            whole(rate.shape), whole(rate.shape), whole(rt.shape),
        ],
        out_specs=(whole((rows, channels)), whole((rows, channels)), whole((CHUNK, flat))),
        scratch_shapes=[
            pltpu.VMEM((CHUNK + MODES, groups * CHUNK), BF),
            pltpu.VMEM((channels // LANES, LANES // GROUP * CHUNK, 2 * LANES), BF),
        ],
        compiler_params=pltpu.CompilerParams(vmem_limit_bytes=16 * 2**20),
        cost_estimate=pl.CostEstimate(flops=6 * 10**9, bytes_accessed=2**16, transcendentals=0),
        name="conv",
    )(far(projected), far(signal), halo, far(short_filter), far(rate), weight, rt)
    f1 = lax.ppermute(f0, "y", [(i, (i + 1) % 4) for i in range(4)])
    f3 = lax.ppermute(f0, "y", [(i, (i - 1) % 4) for i in range(4)])
    ends, f1, f3, rest, f0_late = lax.optimization_barrier((ends, f1, f3, rest, f0))
    f2 = lax.ppermute(f0_late, "y", [(i, (i + 2) % 4) for i in range(4)])
    mixed = pl.pallas_call(
        mix_kernel,
        out_shape=jax.ShapeDtypeStruct((rows, channels), BF),
        in_specs=[SM] + [VM] * 5,
        out_specs=VM,
        compiler_params=pltpu.CompilerParams(vmem_limit_bytes=10 * 2**20),
        cost_estimate=pl.CostEstimate(flops=10**6, bytes_accessed=2**16, transcendentals=0),
        name="mix",
    )(at, ends, rt, din, far(conv), far(query))

    a_far = lax.ppermute(mixed, "xh", [(0, 1), (1, 0)])
    a_other = other_core(mixed)
    a_other, core_late = lax.optimization_barrier((a_other, core))
    w_other = other_core(
        lax.dynamic_slice(out_weight, (0, (xh * 2 + 1 - core_late) * width), (channels, width))
    )
    def given(parts):
        return other_core(
            jnp.concatenate([lax.dynamic_slice(v, (0, (1 - core) * width), (v.shape[0], width)) for v in parts], axis=0)
        )

    g013, g2 = given((f0_late, f1, f3, rest)), given((f2,))

    tile = 512
    strips = width // tile

    def strip(shape):
        return pl.BlockSpec(shape[:-1] + (tile,), lambda i, at_ref: (0, i))

    def half_strip(shape):
        return pl.BlockSpec(shape[:-1] + (tile,), lambda i, at_ref: (0, at_ref[3] * strips + i))

    left_specs = [pl.BlockSpec((rows, channels), lambda i, at_ref: (0, 0), **once)] * 2
    near = pl.pallas_call(
        near_kernel,
        out_shape=jax.ShapeDtypeStruct((rows, width), BF),
        grid_spec=pltpu.PrefetchScalarGridSpec(
            num_scalar_prefetch=1,
            grid=(strips,),
            in_specs=left_specs
            + [pl.BlockSpec((channels, tile), lambda i, at_ref: (0, at_ref[2] * strips + i)), strip(w_other.shape)],
            out_specs=strip((rows, width)),
            scratch_shapes=[pltpu.VMEM((rows, 2 * channels), BF), pltpu.VMEM((2 * channels, tile), BF)],
        ),
        compiler_params=pltpu.CompilerParams(vmem_limit_bytes=16 * 2**20),
        cost_estimate=pl.CostEstimate(flops=2 * 10**9, bytes_accessed=6 * 2**20, transcendentals=0),
        name="near",
    )(at, mixed, a_other, far(out_weight), w_other)
    a_far, near, g2 = lax.optimization_barrier((a_far, near, g2))
    a_far_other = other_core(a_far)
    partial = pl.pallas_call(
        far_kernel,
        out_shape=pltpu.HBM((rows, width), BF),
        grid_spec=pltpu.PrefetchScalarGridSpec(
            num_scalar_prefetch=1,
            grid=(strips,),
            in_specs=left_specs
            + [half_strip(v.shape) for v in (f0, f1, f2, f3, rest)]
            + [strip(g013.shape), strip(g2.shape)]
            + [strip((rows, width))],
            out_specs=strip((rows, width)),
            scratch_shapes=[pltpu.VMEM((rows, 2 * channels), BF), pltpu.VMEM((2 * channels, tile), BF)],
        ),
        compiler_params=pltpu.CompilerParams(vmem_limit_bytes=20 * 2**20),
        cost_estimate=pl.CostEstimate(flops=2 * 10**9, bytes_accessed=10 * 2**20, transcendentals=0),
        name="far",
    )(at, a_far, a_far_other, f0_late, f1, f2, f3, rest, g013, g2, near)

    summed = lax.psum_scatter(partial, "z", scatter_dimension=0, tiled=True)
    size = summed.shape[0] // 4

    def traded(k):
        pairs = [(i, i ^ k) for i in range(4)]
        return lax.ppermute(summed[k * size : (k + 1) * size], ("xh", "c"), pairs)

    return pl.pallas_call(
        join_kernel,
        out_shape=jax.ShapeDtypeStruct((size, 4 * width), BF),
        in_specs=[SM] + [VM] * 4,
        out_specs=VM,
        compiler_params=pltpu.CompilerParams(vmem_limit_bytes=4 * 2**20),
        name="join",
    )(at, summed[:size], traded(1), traded(2), traded(3))


def solution(mesh):
    fine = Mesh(mesh.devices.reshape(4, 2, 8, 2, 2), ("y", "xl", "z", "xh", "c"))
    seq, tp = ("y", "xl"), ("z", "xh", "c")
    placed = (P(None, seq, tp), P(None, None, tp), P(tp, None), P(tp, None), P(tp, None))
    return jax.shard_map(local, mesh=fine, in_specs=placed, out_specs=P(seq + tp, None), check_vma=False)
```

```python
import jax
import jax.numpy as jnp
from jax import lax
from jax.experimental import pallas as pl
from jax.experimental.pallas import tpu as pltpu
from jax.sharding import Mesh, PartitionSpec as P

GROUP = 16
MODES = 16
CHUNK = 128
LANES = 128
BF = jnp.bfloat16
F32 = jnp.float32
VM = pl.BlockSpec(memory_space=pltpu.VMEM)
SM = pl.BlockSpec(memory_space=pltpu.SMEM)


def iota(shape, dim):
    return lax.broadcasted_iota(jnp.int32, shape, dim)


def spread(state):
    width = state.shape[1]
    groups = width // GROUP
    tall = jnp.concatenate([state] * groups, axis=0)
    shape = (groups * MODES, width)
    own = iota(shape, 0) // MODES == iota(shape, 1) // GROUP
    return jnp.where(own, tall, 0.0).astype(BF)


def one_hot(rows, columns, row_size, column_size):
    shape = (rows, columns)
    return (iota(shape, 0) // row_size == iota(shape, 1) // column_size).astype(F32)


def exact_dot(a, b, dims):
    return lax.dot_general(a, b, (dims, ((), ())), precision=lax.Precision.HIGHEST, preferred_element_type=F32)


def by_channel(table, channels):
    return exact_dot(table, one_hot(table.shape[0], channels, 1, GROUP), ((0,), (0,)))


def by_row(table):
    flat = table.shape[0] * MODES
    wide = exact_dot(one_hot(flat, table.shape[0], MODES, 1), table, ((1,), (0,)))
    keep = iota((flat, MODES), 0) % MODES == iota((flat, MODES), 1)
    return jnp.where(keep, wide, 0.0).sum(axis=1, keepdims=True)


def by_lane(table):
    flat = table.shape[0] * MODES
    wide = exact_dot(table, one_hot(table.shape[0], flat, 1, MODES), ((0,), (0,)))
    keep = iota((MODES, flat), 1) % MODES == iota((MODES, flat), 0)
    return jnp.where(keep, wide, 0.0).sum(axis=0, keepdims=True)


def tapped(taps, cur, before):
    ext = jnp.concatenate([before, cur], axis=0)
    skip = before.shape[0]
    one = pltpu.roll(ext, 1, 0)[skip:]
    two = pltpu.roll(ext, 2, 0)[skip:]
    return taps[0:1, :] * cur + taps[1:2, :] * one + taps[2:3, :] * two


def state_kernel(k_ref, v_ref, halo_ref, sf_ref, rate_ref, x_ref, end_ref, rt_ref, tail, total, power):
    step = pl.program_id(0)
    rows, channels = k_ref.shape

    @pl.when(step == 0)
    def _():
        rt = by_channel(rate_ref[...], channels)
        rt_ref[...] = rt
        total[...] = jnp.zeros_like(total)
        for n in range(MODES):
            power[n] = jnp.broadcast_to(jnp.exp(-8.0 * rt[n : n + 1, :]), (8, channels))
        for i in range(2):
            tail[i] = halo_ref[i + 1].astype(F32)

    featured = []
    for i, ref in enumerate((k_ref, v_ref)):
        cur = ref[...].astype(F32)
        featured.append(tapped(sf_ref[i + 1], cur, tail[i]))
        tail[i] = cur[rows - 8 :]
    signal = featured[0] * featured[1]
    x_ref[...] = signal.astype(BF)
    for h in range(channels // LANES):
        lanes = slice(h * LANES, (h + 1) * LANES)
        for first in range(0, MODES, 8):
            sums = [total[n, :, lanes] for n in range(first, first + 8)]
            powers = [power[n, :, lanes] for n in range(first, first + 8)]
            for b in range(rows // 8):
                block = signal[b * 8 : (b + 1) * 8, lanes]
                sums = [s * w + block for s, w in zip(sums, powers)]
            for n in range(8):
                total[first + n, :, lanes] = sums[n]

    @pl.when(step == pl.num_programs(0) - 1)
    def _():
        rt = rt_ref[...]
        ahead = (7 - iota((8, channels), 0)).astype(F32)
        end = jnp.concatenate(
            [
                (total[n] * jnp.exp(-ahead * rt[n : n + 1, :])).sum(axis=0, keepdims=True)
                for n in range(MODES)
            ],
            axis=0,
        )
        for j in range(end_ref.shape[0]):
            end_ref[j] = end


def conv_kernel(p_ref, x_ref, halo_ref, sf_ref, rate_ref, weight_ref, rt_ref,
                y_ref, q_ref, din_ref, table, masked):
    rows, channels = x_ref.shape
    halves = channels // LANES
    per_half = LANES // GROUP
    groups = channels // GROUP
    rate, weight = rate_ref[...], weight_ref[...]
    rcol = by_row(rate)
    wcol = by_row(weight)
    lane = iota((groups * MODES, CHUNK), 1)
    back = jnp.where(lane == 0, 0, CHUNK - lane).astype(F32)
    taps = (wcol * jnp.exp(-rcol * back)).reshape(groups, MODES, CHUNK).sum(axis=1)
    leave = jnp.exp(-rcol * (CHUNK - 1 - lane).astype(F32)).astype(BF)
    causal = iota((CHUNK, CHUNK), 0) >= iota((CHUNK, CHUNK), 1)
    for g in range(groups):
        wide = jnp.broadcast_to(taps[g : g + 1, :], (CHUNK, CHUNK))
        turned = pltpu.roll(wide, 0, 1, stride=1, stride_axis=0)
        table[0:CHUNK, g * CHUNK : (g + 1) * CHUNK] = jnp.where(causal, turned, 0.0).astype(BF)
        table[CHUNK : CHUNK + MODES, g * CHUNK : (g + 1) * CHUNK] = leave[g * MODES : (g + 1) * MODES]
    steps = (iota((CHUNK, groups * MODES), 0) + 1).astype(F32)
    din = (by_lane(weight) * jnp.exp(-by_lane(rate) * steps)).astype(BF)
    din_ref[...] = din
    power = jnp.exp(-rt_ref[...] * float(CHUNK))
    group_lane = iota((CHUNK, LANES), 1) // GROUP

    state = jnp.zeros((MODES, channels), F32)
    for pair in range(rows // (2 * CHUNK)):
        for j in range(2):
            q = 2 * pair + j
            span = slice(q * CHUNK, (q + 1) * CHUNK)
            before = halo_ref[0] if q == 0 else p_ref[q * CHUNK - 16 : q * CHUNK, :]
            q_ref[span, :] = tapped(sf_ref[0], p_ref[span, :].astype(F32), before.astype(F32)).astype(BF)
            for h in range(halves):
                part = x_ref[span, h * LANES : (h + 1) * LANES]
                for g in range(per_half):
                    masked[h, g * CHUNK : (g + 1) * CHUNK, j * LANES : (j + 1) * LANES] = jnp.where(
                        group_lane == g, part, jnp.zeros_like(part)
                    )
        depth = per_half * CHUNK
        made = [
            jnp.dot(table[:, h * depth : (h + 1) * depth], masked[h], preferred_element_type=F32)
            for h in range(halves)
        ]
        for j in range(2):
            q = 2 * pair + j
            full = jnp.concatenate([m[:, j * LANES : (j + 1) * LANES] for m in made], axis=1)
            within = full[:CHUNK]
            if q > 0:
                within = within + jnp.dot(din, spread(state), preferred_element_type=F32)
            y_ref[q * CHUNK : (q + 1) * CHUNK, :] = within.astype(BF)
            state = power * state + full[CHUNK:]


def mix_kernel(at_ref, ends_ref, rt_ref, din_ref, y_ref, q_ref, mixed_ref):
    rows = y_ref.shape[0]
    here = at_ref[0]
    rt = rt_ref[...]
    block_power = jnp.exp(-rt * float(rows))
    state = jnp.zeros(rt.shape, F32)
    for j in range(ends_ref.shape[0]):
        state = jnp.where(j < here, block_power * state + ends_ref[j], state)
    power = jnp.exp(-rt * float(CHUNK))
    din = din_ref[...]
    for q in range(rows // CHUNK):
        span = slice(q * CHUNK, (q + 1) * CHUNK)
        carried = jnp.dot(din, spread(state), preferred_element_type=F32)
        mixed_ref[span, :] = (q_ref[span, :].astype(F32) * (y_ref[span, :].astype(F32) + carried)).astype(BF)
        state = power * state


def side_by_side(left, refs):
    depth = refs[0].shape[1]

    @pl.when(pl.program_id(0) == 0)
    def _():
        for k, ref in enumerate(refs):
            left[:, k * depth : (k + 1) * depth] = ref[...]


def near_kernel(at_ref, a0, a1, w0, w1, c_ref, left, right):
    depth = w0.shape[0]
    side_by_side(left, (a0, a1))
    right[0:depth] = w0[...]
    right[depth : 2 * depth] = w1[...]
    block = 256
    for m in range(left.shape[0] // block):
        span = slice(m * block, (m + 1) * block)
        c_ref[span, :] = jnp.dot(left[span, :], right[...], preferred_element_type=F32).astype(BF)


def far_kernel(at_ref, a2, a3, f0, f1, f2, f3, rest, g013, g2, near_ref, c_ref, left, right):
    y, mine = at_ref[1], at_ref[2]
    size = f0.shape[0]
    depth = right.shape[0] // 2
    tail = depth - 4 * size
    side_by_side(left, (a2, a3))
    for k, ref in enumerate((f0, f1, f2, f3)):
        owner = lax.rem(y - k + 4, 4) * size
        right[pl.ds(pl.multiple_of(owner, 16), size), :] = ref[0:size]
        passed = g2[0:size] if k == 2 else g013[(0, 1, 0, 2)[k] * size : ((0, 1, 0, 2)[k] + 1) * size]
        right[pl.ds(pl.multiple_of(depth + owner, 16), size), :] = passed
    right[4 * size : depth] = rest[...]
    right[depth + 4 * size : 2 * depth] = g013[3 * size : 3 * size + tail]
    block = 256
    for m in range(left.shape[0] // block):
        span = slice(m * block, (m + 1) * block)
        total = jnp.dot(left[span, :], right[...], preferred_element_type=F32)
        total = (total + near_ref[span, :].astype(F32)).astype(BF)
        for b in range(block // 32):
            high, low = m * (block // 128) + b // 4, b % 4
            place = pl.multiple_of((high * 4 + jnp.bitwise_xor(low, mine)) * 32, 32)
            c_ref[pl.ds(place, 32), :] = total[b * 32 : (b + 1) * 32]


def join_kernel(at_ref, p0, p1, p2, p3, out_ref):
    mine = at_ref[2]
    width = p0.shape[1]
    for k, ref in enumerate((p0, p1, p2, p3)):
        place = pl.multiple_of(jnp.bitwise_xor(mine, k) * width, width)
        out_ref[:, pl.ds(place, width)] = ref[...]


def far(value):
    return pltpu.with_memory_space_constraint(value, pltpu.HBM)


def other_core(value):
    return lax.ppermute(value, "c", [(0, 1), (1, 0)])


def local(projected, short_filter, residue, rate, out_weight):
    rows, channels = projected.shape[1], projected.shape[2]
    groups = rate.shape[0]
    width = out_weight.shape[1] // 4
    y, xh, core = lax.axis_index("y"), lax.axis_index("xh"), lax.axis_index("c")
    seq = lax.axis_index(("y", "xl"))
    edge = projected[:, rows - 8 :, :]
    edge, y_then = lax.optimization_barrier((edge, y))
    halo = lax.ppermute(edge, ("y", "xl"), [(i, i + 1) for i in range(7)])

    size = 48
    tail = channels - 4 * size
    half = 2 * width
    mirror = [(0, 3), (3, 0), (1, 2), (2, 1)]

    def there(source, start, count):
        return lax.dynamic_slice(source, (start, (1 - xh) * half), (count, half))

    f0 = lax.ppermute(there(out_weight, y_then * size, size), ("xl", "xh"), mirror)
    rest = lax.ppermute(there(out_weight, 4 * size, tail), ("xl", "xh"), mirror)

    flat = groups * MODES
    span = 256
    once = {"pipeline_mode": pl.Buffered(1)}

    def whole(shape):
        return pl.BlockSpec(shape, lambda i: (0,) * len(shape))

    def third(k):
        return pl.BlockSpec((None, span, channels), lambda i: (k, i, 0))

    signal, end, rt = pl.pallas_call(
        state_kernel,
        out_shape=(
            pltpu.HBM((rows, channels), BF),
            jax.ShapeDtypeStruct((8, MODES, channels), F32),
            jax.ShapeDtypeStruct((MODES, channels), F32),
        ),
        grid=(rows // span,),
        in_specs=[third(1), third(2), whole(halo.shape), whole(short_filter.shape), whole(rate.shape)],
        out_specs=(
            pl.BlockSpec((span, channels), lambda i: (i, 0)),
            whole((8, MODES, channels)),
            whole((MODES, channels)),
        ),
        scratch_shapes=[
            pltpu.VMEM((2, 8, channels), F32),
            pltpu.VMEM((MODES, 8, channels), F32),
            pltpu.VMEM((MODES, 8, channels), F32),
        ],
        compiler_params=pltpu.CompilerParams(vmem_limit_bytes=12 * 2**20),
        cost_estimate=pl.CostEstimate(flops=10**6, bytes_accessed=2**16, transcendentals=0),
        name="state",
    )(far(projected), far(projected), halo, far(short_filter), far(rate))
    end, residue_late = lax.optimization_barrier((end, residue))
    at = jnp.stack([seq, y, xh * 2 + core, core]).astype(jnp.int32)
    weight = residue_late * jnp.sqrt(-jnp.expm1(-2.0 * rate))
    ends = lax.all_to_all(end, ("y", "xl"), 0, 0, tiled=True)
    conv, query, din = pl.pallas_call(
        conv_kernel,
        out_shape=(
            pltpu.HBM((rows, channels), BF),
            pltpu.HBM((rows, channels), BF),
            jax.ShapeDtypeStruct((CHUNK, flat), BF),
        ),
        grid=(1,),
        in_specs=[
            pl.BlockSpec((None, rows, channels), lambda i: (0, 0, 0)),
            whole((rows, channels)), whole(halo.shape), whole(short_filter.shape),
            whole(rate.shape), whole(rate.shape), whole(rt.shape),
        ],
        out_specs=(whole((rows, channels)), whole((rows, channels)), whole((CHUNK, flat))),
        scratch_shapes=[
            pltpu.VMEM((CHUNK + MODES, groups * CHUNK), BF),
            pltpu.VMEM((channels // LANES, LANES // GROUP * CHUNK, 2 * LANES), BF),
        ],
        compiler_params=pltpu.CompilerParams(vmem_limit_bytes=16 * 2**20),
        cost_estimate=pl.CostEstimate(flops=6 * 10**9, bytes_accessed=2**16, transcendentals=0),
        name="conv",
    )(far(projected), far(signal), halo, far(short_filter), far(rate), weight, rt)
    f1 = lax.ppermute(f0, "y", [(i, (i + 1) % 4) for i in range(4)])
    f3 = lax.ppermute(f0, "y", [(i, (i - 1) % 4) for i in range(4)])
    ends, f1, f3, rest, f0_late = lax.optimization_barrier((ends, f1, f3, rest, f0))
    f2 = lax.ppermute(f0_late, "y", [(i, (i + 2) % 4) for i in range(4)])
    mixed = pl.pallas_call(
        mix_kernel,
        out_shape=jax.ShapeDtypeStruct((rows, channels), BF),
        in_specs=[SM] + [VM] * 5,
        out_specs=VM,
        compiler_params=pltpu.CompilerParams(vmem_limit_bytes=10 * 2**20),
        cost_estimate=pl.CostEstimate(flops=10**6, bytes_accessed=2**16, transcendentals=0),
        name="mix",
    )(at, ends, rt, din, far(conv), far(query))

    a_far = lax.ppermute(mixed, "xh", [(0, 1), (1, 0)])
    a_other = other_core(mixed)
    a_other, core_late = lax.optimization_barrier((a_other, core))
    w_other = other_core(
        lax.dynamic_slice(out_weight, (0, (xh * 2 + 1 - core_late) * width), (channels, width))
    )
    def given(parts):
        return other_core(
            jnp.concatenate([lax.dynamic_slice(v, (0, (1 - core) * width), (v.shape[0], width)) for v in parts], axis=0)
        )

    g013 = given((f0_late, f1, f3, rest))

    tile = 512
    strips = width // tile

    def strip(shape):
        return pl.BlockSpec(shape[:-1] + (tile,), lambda i, at_ref: (0, i))

    def half_strip(shape):
        return pl.BlockSpec(shape[:-1] + (tile,), lambda i, at_ref: (0, at_ref[3] * strips + i))

    left_specs = [pl.BlockSpec((rows, channels), lambda i, at_ref: (0, 0), **once)] * 2
    near = pl.pallas_call(
        near_kernel,
        out_shape=jax.ShapeDtypeStruct((rows, width), BF),
        grid_spec=pltpu.PrefetchScalarGridSpec(
            num_scalar_prefetch=1,
            grid=(strips,),
            in_specs=left_specs
            + [pl.BlockSpec((channels, tile), lambda i, at_ref: (0, at_ref[2] * strips + i)), strip(w_other.shape)],
            out_specs=strip((rows, width)),
            scratch_shapes=[pltpu.VMEM((rows, 2 * channels), BF), pltpu.VMEM((2 * channels, tile), BF)],
        ),
        compiler_params=pltpu.CompilerParams(vmem_limit_bytes=16 * 2**20),
        cost_estimate=pl.CostEstimate(flops=2 * 10**9, bytes_accessed=6 * 2**20, transcendentals=0),
        name="near",
    )(at, mixed, a_other, far(out_weight), w_other)
    a_far, near, f2 = lax.optimization_barrier((a_far, near, f2))
    g2 = given((f2,))
    a_far_other = other_core(a_far)
    partial = pl.pallas_call(
        far_kernel,
        out_shape=pltpu.HBM((rows, width), BF),
        grid_spec=pltpu.PrefetchScalarGridSpec(
            num_scalar_prefetch=1,
            grid=(strips,),
            in_specs=left_specs
            + [half_strip(v.shape) for v in (f0, f1, f2, f3, rest)]
            + [strip(g013.shape), strip(g2.shape)]
            + [strip((rows, width))],
            out_specs=strip((rows, width)),
            scratch_shapes=[pltpu.VMEM((rows, 2 * channels), BF), pltpu.VMEM((2 * channels, tile), BF)],
        ),
        compiler_params=pltpu.CompilerParams(vmem_limit_bytes=20 * 2**20),
        cost_estimate=pl.CostEstimate(flops=2 * 10**9, bytes_accessed=10 * 2**20, transcendentals=0),
        name="far",
    )(at, a_far, a_far_other, f0_late, f1, f2, f3, rest, g013, g2, near)

    summed = lax.psum_scatter(partial, "z", scatter_dimension=0, tiled=True)
    size = summed.shape[0] // 4

    def traded(k):
        pairs = [(i, i ^ k) for i in range(4)]
        return lax.ppermute(summed[k * size : (k + 1) * size], ("xh", "c"), pairs)

    return pl.pallas_call(
        join_kernel,
        out_shape=jax.ShapeDtypeStruct((size, 4 * width), BF),
        in_specs=[SM] + [VM] * 4,
        out_specs=VM,
        compiler_params=pltpu.CompilerParams(vmem_limit_bytes=4 * 2**20),
        name="join",
    )(at, summed[:size], traded(1), traded(2), traded(3))


def solution(mesh):
    fine = Mesh(mesh.devices.reshape(4, 2, 8, 2, 2), ("y", "xl", "z", "xh", "c"))
    seq, tp = ("y", "xl"), ("z", "xh", "c")
    placed = (P(None, seq, tp), P(None, None, tp), P(tp, None), P(tp, None), P(tp, None))
    return jax.shard_map(local, mesh=fine, in_specs=placed, out_specs=P(seq + tp, None), check_vma=False)
```

```python
import jax
import jax.numpy as jnp
from jax import lax
from jax.experimental import pallas as pl
from jax.experimental.pallas import tpu as pltpu
from jax.sharding import Mesh, PartitionSpec as P

GROUP = 16
MODES = 16
CHUNK = 128
LANES = 128
BF = jnp.bfloat16
F32 = jnp.float32
VM = pl.BlockSpec(memory_space=pltpu.VMEM)
SM = pl.BlockSpec(memory_space=pltpu.SMEM)


def iota(shape, dim):
    return lax.broadcasted_iota(jnp.int32, shape, dim)


def spread(state):
    width = state.shape[1]
    groups = width // GROUP
    tall = jnp.concatenate([state] * groups, axis=0)
    shape = (groups * MODES, width)
    own = iota(shape, 0) // MODES == iota(shape, 1) // GROUP
    return jnp.where(own, tall, 0.0).astype(BF)


def one_hot(rows, columns, row_size, column_size):
    shape = (rows, columns)
    return (iota(shape, 0) // row_size == iota(shape, 1) // column_size).astype(F32)


def exact_dot(a, b, dims):
    return lax.dot_general(a, b, (dims, ((), ())), precision=lax.Precision.HIGHEST, preferred_element_type=F32)


def by_channel(table, channels):
    return exact_dot(table, one_hot(table.shape[0], channels, 1, GROUP), ((0,), (0,)))


def by_row(table):
    flat = table.shape[0] * MODES
    wide = exact_dot(one_hot(flat, table.shape[0], MODES, 1), table, ((1,), (0,)))
    keep = iota((flat, MODES), 0) % MODES == iota((flat, MODES), 1)
    return jnp.where(keep, wide, 0.0).sum(axis=1, keepdims=True)


def by_lane(table):
    flat = table.shape[0] * MODES
    wide = exact_dot(table, one_hot(table.shape[0], flat, 1, MODES), ((0,), (0,)))
    keep = iota((MODES, flat), 1) % MODES == iota((MODES, flat), 0)
    return jnp.where(keep, wide, 0.0).sum(axis=0, keepdims=True)


def tapped(taps, cur, before):
    ext = jnp.concatenate([before, cur], axis=0)
    skip = before.shape[0]
    one = pltpu.roll(ext, 1, 0)[skip:]
    two = pltpu.roll(ext, 2, 0)[skip:]
    return taps[0:1, :] * cur + taps[1:2, :] * one + taps[2:3, :] * two


def state_kernel(k_ref, v_ref, halo_ref, sf_ref, rate_ref, x_ref, end_ref, rt_ref, tail, total, power):
    step = pl.program_id(0)
    rows, channels = k_ref.shape

    @pl.when(step == 0)
    def _():
        rt = by_channel(rate_ref[...], channels)
        rt_ref[...] = rt
        total[...] = jnp.zeros_like(total)
        for n in range(MODES):
            power[n] = jnp.broadcast_to(jnp.exp(-8.0 * rt[n : n + 1, :]), (8, channels))
        for i in range(2):
            tail[i] = halo_ref[i + 1].astype(F32)

    featured = []
    for i, ref in enumerate((k_ref, v_ref)):
        cur = ref[...].astype(F32)
        featured.append(tapped(sf_ref[i + 1], cur, tail[i]))
        tail[i] = cur[rows - 8 :]
    signal = featured[0] * featured[1]
    x_ref[...] = signal.astype(BF)
    for h in range(channels // LANES):
        lanes = slice(h * LANES, (h + 1) * LANES)
        for first in range(0, MODES, 8):
            sums = [total[n, :, lanes] for n in range(first, first + 8)]
            powers = [power[n, :, lanes] for n in range(first, first + 8)]
            for b in range(rows // 8):
                block = signal[b * 8 : (b + 1) * 8, lanes]
                sums = [s * w + block for s, w in zip(sums, powers)]
            for n in range(8):
                total[first + n, :, lanes] = sums[n]

    @pl.when(step == pl.num_programs(0) - 1)
    def _():
        rt = rt_ref[...]
        ahead = (7 - iota((8, channels), 0)).astype(F32)
        end = jnp.concatenate(
            [
                (total[n] * jnp.exp(-ahead * rt[n : n + 1, :])).sum(axis=0, keepdims=True)
                for n in range(MODES)
            ],
            axis=0,
        )
        for j in range(end_ref.shape[0]):
            end_ref[j] = end


def conv_kernel(p_ref, x_ref, halo_ref, sf_ref, rate_ref, weight_ref, rt_ref,
                y_ref, q_ref, din_ref, table, masked):
    rows, channels = x_ref.shape
    halves = channels // LANES
    per_half = LANES // GROUP
    groups = channels // GROUP
    rate, weight = rate_ref[...], weight_ref[...]
    rcol = by_row(rate)
    wcol = by_row(weight)
    lane = iota((groups * MODES, CHUNK), 1)
    back = jnp.where(lane == 0, 0, CHUNK - lane).astype(F32)
    taps = (wcol * jnp.exp(-rcol * back)).reshape(groups, MODES, CHUNK).sum(axis=1)
    leave = jnp.exp(-rcol * (CHUNK - 1 - lane).astype(F32)).astype(BF)
    causal = iota((CHUNK, CHUNK), 0) >= iota((CHUNK, CHUNK), 1)
    for g in range(groups):
        wide = jnp.broadcast_to(taps[g : g + 1, :], (CHUNK, CHUNK))
        turned = pltpu.roll(wide, 0, 1, stride=1, stride_axis=0)
        table[0:CHUNK, g * CHUNK : (g + 1) * CHUNK] = jnp.where(causal, turned, 0.0).astype(BF)
        table[CHUNK : CHUNK + MODES, g * CHUNK : (g + 1) * CHUNK] = leave[g * MODES : (g + 1) * MODES]
    steps = (iota((CHUNK, groups * MODES), 0) + 1).astype(F32)
    din = (by_lane(weight) * jnp.exp(-by_lane(rate) * steps)).astype(BF)
    din_ref[...] = din
    power = jnp.exp(-rt_ref[...] * float(CHUNK))
    group_lane = iota((CHUNK, LANES), 1) // GROUP

    state = jnp.zeros((MODES, channels), F32)
    for pair in range(rows // (2 * CHUNK)):
        for j in range(2):
            q = 2 * pair + j
            span = slice(q * CHUNK, (q + 1) * CHUNK)
            before = halo_ref[0] if q == 0 else p_ref[q * CHUNK - 16 : q * CHUNK, :]
            q_ref[span, :] = tapped(sf_ref[0], p_ref[span, :].astype(F32), before.astype(F32)).astype(BF)
            for h in range(halves):
                part = x_ref[span, h * LANES : (h + 1) * LANES]
                for g in range(per_half):
                    masked[h, g * CHUNK : (g + 1) * CHUNK, j * LANES : (j + 1) * LANES] = jnp.where(
                        group_lane == g, part, jnp.zeros_like(part)
                    )
        depth = per_half * CHUNK
        made = [
            jnp.dot(table[:, h * depth : (h + 1) * depth], masked[h], preferred_element_type=F32)
            for h in range(halves)
        ]
        for j in range(2):
            q = 2 * pair + j
            full = jnp.concatenate([m[:, j * LANES : (j + 1) * LANES] for m in made], axis=1)
            within = full[:CHUNK]
            if q > 0:
                within = within + jnp.dot(din, spread(state), preferred_element_type=F32)
            y_ref[q * CHUNK : (q + 1) * CHUNK, :] = within.astype(BF)
            state = power * state + full[CHUNK:]


def mix_kernel(at_ref, ends_ref, rt_ref, din_ref, y_ref, q_ref, mixed_ref):
    rows = y_ref.shape[0]
    here = at_ref[0]
    rt = rt_ref[...]
    block_power = jnp.exp(-rt * float(rows))
    state = jnp.zeros(rt.shape, F32)
    for j in range(ends_ref.shape[0]):
        state = jnp.where(j < here, block_power * state + ends_ref[j], state)
    power = jnp.exp(-rt * float(CHUNK))
    din = din_ref[...]
    for q in range(rows // CHUNK):
        span = slice(q * CHUNK, (q + 1) * CHUNK)
        carried = jnp.dot(din, spread(state), preferred_element_type=F32)
        mixed_ref[span, :] = (q_ref[span, :].astype(F32) * (y_ref[span, :].astype(F32) + carried)).astype(BF)
        state = power * state


def side_by_side(left, refs):
    depth = refs[0].shape[1]

    @pl.when(pl.program_id(0) == 0)
    def _():
        for k, ref in enumerate(refs):
            left[:, k * depth : (k + 1) * depth] = ref[...]


def near_kernel(at_ref, a0, a1, w0, w1, c_ref, left, right):
    depth = w0.shape[0]
    side_by_side(left, (a0, a1))
    right[0:depth] = w0[...]
    right[depth : 2 * depth] = w1[...]
    block = 256
    for m in range(left.shape[0] // block):
        span = slice(m * block, (m + 1) * block)
        c_ref[span, :] = jnp.dot(left[span, :], right[...], preferred_element_type=F32).astype(BF)


def far_kernel(at_ref, a2, a3, f0, f1, f2, f3, rest, g013, g2, near_ref, c_ref, left, right):
    y, mine = at_ref[1], at_ref[2]
    size = f0.shape[0]
    depth = right.shape[0] // 2
    tail = depth - 4 * size
    side_by_side(left, (a2, a3))
    for k, ref in enumerate((f0, f1, f2, f3)):
        owner = lax.rem(y - k + 4, 4) * size
        right[pl.ds(pl.multiple_of(owner, 16), size), :] = ref[0:size]
        passed = g2[0:size] if k == 2 else g013[(0, 1, 0, 2)[k] * size : ((0, 1, 0, 2)[k] + 1) * size]
        right[pl.ds(pl.multiple_of(depth + owner, 16), size), :] = passed
    right[4 * size : depth] = rest[...]
    right[depth + 4 * size : 2 * depth] = g013[3 * size : 3 * size + tail]
    block = 256
    for m in range(left.shape[0] // block):
        span = slice(m * block, (m + 1) * block)
        total = jnp.dot(left[span, :], right[...], preferred_element_type=F32)
        total = (total + near_ref[span, :].astype(F32)).astype(BF)
        for b in range(block // 32):
            high, low = m * (block // 128) + b // 4, b % 4
            place = pl.multiple_of((high * 4 + jnp.bitwise_xor(low, mine)) * 32, 32)
            c_ref[pl.ds(place, 32), :] = total[b * 32 : (b + 1) * 32]


def join_kernel(at_ref, p0, p1, p2, p3, out_ref):
    mine = at_ref[2]
    width = p0.shape[1]
    for k, ref in enumerate((p0, p1, p2, p3)):
        place = pl.multiple_of(jnp.bitwise_xor(mine, k) * width, width)
        out_ref[:, pl.ds(place, width)] = ref[...]


def far(value):
    return pltpu.with_memory_space_constraint(value, pltpu.HBM)


def other_core(value):
    return lax.ppermute(value, "c", [(0, 1), (1, 0)])


def local(projected, short_filter, residue, rate, out_weight):
    rows, channels = projected.shape[1], projected.shape[2]
    groups = rate.shape[0]
    width = out_weight.shape[1] // 4
    y, xh, core = lax.axis_index("y"), lax.axis_index("xh"), lax.axis_index("c")
    seq = lax.axis_index(("y", "xl"))
    edge = projected[:, rows - 8 :, :]
    edge, y_then = lax.optimization_barrier((edge, y))
    halo = lax.ppermute(edge, ("y", "xl"), [(i, i + 1) for i in range(7)])

    size = 48
    tail = channels - 4 * size
    half = 2 * width
    mirror = [(0, 3), (3, 0), (1, 2), (2, 1)]

    def there(source, start, count):
        return lax.dynamic_slice(source, (start, (1 - xh) * half), (count, half))

    f0 = lax.ppermute(there(out_weight, y_then * size, size), ("xl", "xh"), mirror)
    rest = lax.ppermute(there(out_weight, 4 * size, tail), ("xl", "xh"), mirror)

    flat = groups * MODES
    span = 256
    once = {"pipeline_mode": pl.Buffered(1)}

    def whole(shape):
        return pl.BlockSpec(shape, lambda i: (0,) * len(shape))

    def third(k):
        return pl.BlockSpec((None, span, channels), lambda i: (k, i, 0))

    signal, end, rt = pl.pallas_call(
        state_kernel,
        out_shape=(
            pltpu.HBM((rows, channels), BF),
            jax.ShapeDtypeStruct((8, MODES, channels), F32),
            jax.ShapeDtypeStruct((MODES, channels), F32),
        ),
        grid=(rows // span,),
        in_specs=[third(1), third(2), whole(halo.shape), whole(short_filter.shape), whole(rate.shape)],
        out_specs=(
            pl.BlockSpec((span, channels), lambda i: (i, 0)),
            whole((8, MODES, channels)),
            whole((MODES, channels)),
        ),
        scratch_shapes=[
            pltpu.VMEM((2, 8, channels), F32),
            pltpu.VMEM((MODES, 8, channels), F32),
            pltpu.VMEM((MODES, 8, channels), F32),
        ],
        compiler_params=pltpu.CompilerParams(vmem_limit_bytes=12 * 2**20),
        cost_estimate=pl.CostEstimate(flops=10**6, bytes_accessed=2**16, transcendentals=0),
        name="state",
    )(far(projected), far(projected), halo, far(short_filter), far(rate))
    end, residue_late = lax.optimization_barrier((end, residue))
    at = jnp.stack([seq, y, xh * 2 + core, core]).astype(jnp.int32)
    weight = residue_late * jnp.sqrt(-jnp.expm1(-2.0 * rate))
    ends = lax.all_to_all(end, ("y", "xl"), 0, 0, tiled=True)
    conv, query, din = pl.pallas_call(
        conv_kernel,
        out_shape=(
            pltpu.HBM((rows, channels), BF),
            pltpu.HBM((rows, channels), BF),
            jax.ShapeDtypeStruct((CHUNK, flat), BF),
        ),
        grid=(1,),
        in_specs=[
            pl.BlockSpec((None, rows, channels), lambda i: (0, 0, 0)),
            whole((rows, channels)), whole(halo.shape), whole(short_filter.shape),
            whole(rate.shape), whole(rate.shape), whole(rt.shape),
        ],
        out_specs=(whole((rows, channels)), whole((rows, channels)), whole((CHUNK, flat))),
        scratch_shapes=[
            pltpu.VMEM((CHUNK + MODES, groups * CHUNK), BF),
            pltpu.VMEM((channels // LANES, LANES // GROUP * CHUNK, 2 * LANES), BF),
        ],
        compiler_params=pltpu.CompilerParams(vmem_limit_bytes=16 * 2**20),
        cost_estimate=pl.CostEstimate(flops=6 * 10**9, bytes_accessed=2**16, transcendentals=0),
        name="conv",
    )(far(projected), far(signal), halo, far(short_filter), far(rate), weight, rt)
    f1 = lax.ppermute(f0, "y", [(i, (i + 1) % 4) for i in range(4)])
    f3 = lax.ppermute(f0, "y", [(i, (i - 1) % 4) for i in range(4)])
    ends, f1, f3, rest, f0_late = lax.optimization_barrier((ends, f1, f3, rest, f0))
    f2 = lax.ppermute(f0_late, "y", [(i, (i + 2) % 4) for i in range(4)])
    mixed = pl.pallas_call(
        mix_kernel,
        out_shape=jax.ShapeDtypeStruct((rows, channels), BF),
        in_specs=[SM] + [VM] * 5,
        out_specs=VM,
        compiler_params=pltpu.CompilerParams(vmem_limit_bytes=10 * 2**20),
        cost_estimate=pl.CostEstimate(flops=10**6, bytes_accessed=2**16, transcendentals=0),
        name="mix",
    )(at, ends, rt, din, far(conv), far(query))

    a_far = lax.ppermute(mixed, "xh", [(0, 1), (1, 0)])
    def given(parts):
        return jnp.concatenate(
            [lax.dynamic_slice(v, (0, (1 - core) * width), (v.shape[0], width)) for v in parts], axis=0
        )

    _, core_late = lax.optimization_barrier((mixed, core))
    w_given = lax.dynamic_slice(out_weight, (0, (xh * 2 + 1 - core_late) * width), (channels, width))
    w_given, mixed_late = lax.optimization_barrier((w_given, mixed))
    a_other = other_core(mixed_late)
    w_other = other_core(w_given)
    g013 = other_core(given((f0_late, f1, f3, rest)))

    tile = 512
    strips = width // tile

    def strip(shape):
        return pl.BlockSpec(shape[:-1] + (tile,), lambda i, at_ref: (0, i))

    def half_strip(shape):
        return pl.BlockSpec(shape[:-1] + (tile,), lambda i, at_ref: (0, at_ref[3] * strips + i))

    left_specs = [pl.BlockSpec((rows, channels), lambda i, at_ref: (0, 0), **once)] * 2
    near = pl.pallas_call(
        near_kernel,
        out_shape=jax.ShapeDtypeStruct((rows, width), BF),
        grid_spec=pltpu.PrefetchScalarGridSpec(
            num_scalar_prefetch=1,
            grid=(strips,),
            in_specs=left_specs
            + [pl.BlockSpec((channels, tile), lambda i, at_ref: (0, at_ref[2] * strips + i)), strip(w_other.shape)],
            out_specs=strip((rows, width)),
            scratch_shapes=[pltpu.VMEM((rows, 2 * channels), BF), pltpu.VMEM((2 * channels, tile), BF)],
        ),
        compiler_params=pltpu.CompilerParams(vmem_limit_bytes=16 * 2**20),
        cost_estimate=pl.CostEstimate(flops=2 * 10**9, bytes_accessed=6 * 2**20, transcendentals=0),
        name="near",
    )(at, mixed, a_other, far(out_weight), w_other)
    a_far, near, f2 = lax.optimization_barrier((a_far, near, f2))
    g2 = other_core(given((f2,)))
    a_far_other = other_core(a_far)
    partial = pl.pallas_call(
        far_kernel,
        out_shape=pltpu.HBM((rows, width), BF),
        grid_spec=pltpu.PrefetchScalarGridSpec(
            num_scalar_prefetch=1,
            grid=(strips,),
            in_specs=left_specs
            + [half_strip(v.shape) for v in (f0, f1, f2, f3, rest)]
            + [strip(g013.shape), strip(g2.shape)]
            + [strip((rows, width))],
            out_specs=strip((rows, width)),
            scratch_shapes=[pltpu.VMEM((rows, 2 * channels), BF), pltpu.VMEM((2 * channels, tile), BF)],
        ),
        compiler_params=pltpu.CompilerParams(vmem_limit_bytes=20 * 2**20),
        cost_estimate=pl.CostEstimate(flops=2 * 10**9, bytes_accessed=10 * 2**20, transcendentals=0),
        name="far",
    )(at, a_far, a_far_other, f0_late, f1, f2, f3, rest, g013, g2, near)

    summed = lax.psum_scatter(partial, "z", scatter_dimension=0, tiled=True)
    size = summed.shape[0] // 4

    def traded(k):
        pairs = [(i, i ^ k) for i in range(4)]
        return lax.ppermute(summed[k * size : (k + 1) * size], ("xh", "c"), pairs)

    return pl.pallas_call(
        join_kernel,
        out_shape=jax.ShapeDtypeStruct((size, 4 * width), BF),
        in_specs=[SM] + [VM] * 4,
        out_specs=VM,
        compiler_params=pltpu.CompilerParams(vmem_limit_bytes=4 * 2**20),
        name="join",
    )(at, summed[:size], traded(1), traded(2), traded(3))


def solution(mesh):
    fine = Mesh(mesh.devices.reshape(4, 2, 8, 2, 2), ("y", "xl", "z", "xh", "c"))
    seq, tp = ("y", "xl"), ("z", "xh", "c")
    placed = (P(None, seq, tp), P(None, None, tp), P(tp, None), P(tp, None), P(tp, None))
    return jax.shard_map(local, mesh=fine, in_specs=placed, out_specs=P(seq + tp, None), check_vma=False)
```

```python
import jax
import jax.numpy as jnp
from jax import lax
from jax.experimental import pallas as pl
from jax.experimental.pallas import tpu as pltpu
from jax.sharding import Mesh, PartitionSpec as P

GROUP = 16
MODES = 16
CHUNK = 128
LANES = 128
BF = jnp.bfloat16
F32 = jnp.float32
VM = pl.BlockSpec(memory_space=pltpu.VMEM)
SM = pl.BlockSpec(memory_space=pltpu.SMEM)


def iota(shape, dim):
    return lax.broadcasted_iota(jnp.int32, shape, dim)


def spread(state):
    width = state.shape[1]
    groups = width // GROUP
    tall = jnp.concatenate([state] * groups, axis=0)
    shape = (groups * MODES, width)
    own = iota(shape, 0) // MODES == iota(shape, 1) // GROUP
    return jnp.where(own, tall, 0.0).astype(BF)


def one_hot(rows, columns, row_size, column_size):
    shape = (rows, columns)
    return (iota(shape, 0) // row_size == iota(shape, 1) // column_size).astype(F32)


def exact_dot(a, b, dims):
    return lax.dot_general(a, b, (dims, ((), ())), precision=lax.Precision.HIGHEST, preferred_element_type=F32)


def by_channel(table, channels):
    return exact_dot(table, one_hot(table.shape[0], channels, 1, GROUP), ((0,), (0,)))


def by_row(table):
    flat = table.shape[0] * MODES
    wide = exact_dot(one_hot(flat, table.shape[0], MODES, 1), table, ((1,), (0,)))
    keep = iota((flat, MODES), 0) % MODES == iota((flat, MODES), 1)
    return jnp.where(keep, wide, 0.0).sum(axis=1, keepdims=True)


def by_lane(table):
    flat = table.shape[0] * MODES
    wide = exact_dot(table, one_hot(table.shape[0], flat, 1, MODES), ((0,), (0,)))
    keep = iota((MODES, flat), 1) % MODES == iota((MODES, flat), 0)
    return jnp.where(keep, wide, 0.0).sum(axis=0, keepdims=True)


def tapped(taps, cur, before):
    ext = jnp.concatenate([before, cur], axis=0)
    skip = before.shape[0]
    one = pltpu.roll(ext, 1, 0)[skip:]
    two = pltpu.roll(ext, 2, 0)[skip:]
    return taps[0:1, :] * cur + taps[1:2, :] * one + taps[2:3, :] * two


def state_kernel(k_ref, v_ref, halo_ref, sf_ref, rate_ref, x_ref, end_ref, rt_ref, tail, total, power):
    step = pl.program_id(0)
    rows, channels = k_ref.shape

    @pl.when(step == 0)
    def _():
        rt = by_channel(rate_ref[...], channels)
        rt_ref[...] = rt
        total[...] = jnp.zeros_like(total)
        for n in range(MODES):
            power[n] = jnp.broadcast_to(jnp.exp(-8.0 * rt[n : n + 1, :]), (8, channels))
        for i in range(2):
            tail[i] = halo_ref[i + 1].astype(F32)

    featured = []
    for i, ref in enumerate((k_ref, v_ref)):
        cur = ref[...].astype(F32)
        featured.append(tapped(sf_ref[i + 1], cur, tail[i]))
        tail[i] = cur[rows - 8 :]
    signal = featured[0] * featured[1]
    x_ref[...] = signal.astype(BF)
    for h in range(channels // LANES):
        lanes = slice(h * LANES, (h + 1) * LANES)
        for first in range(0, MODES, 8):
            sums = [total[n, :, lanes] for n in range(first, first + 8)]
            powers = [power[n, :, lanes] for n in range(first, first + 8)]
            for b in range(rows // 8):
                block = signal[b * 8 : (b + 1) * 8, lanes]
                sums = [s * w + block for s, w in zip(sums, powers)]
            for n in range(8):
                total[first + n, :, lanes] = sums[n]

    @pl.when(step == pl.num_programs(0) - 1)
    def _():
        rt = rt_ref[...]
        ahead = (7 - iota((8, channels), 0)).astype(F32)
        end = jnp.concatenate(
            [
                (total[n] * jnp.exp(-ahead * rt[n : n + 1, :])).sum(axis=0, keepdims=True)
                for n in range(MODES)
            ],
            axis=0,
        )
        for j in range(end_ref.shape[0]):
            end_ref[j] = end


def conv_kernel(p_ref, x_ref, halo_ref, sf_ref, rate_ref, weight_ref, rt_ref,
                y_ref, q_ref, din_ref, table, masked):
    rows, channels = x_ref.shape
    halves = channels // LANES
    per_half = LANES // GROUP
    groups = channels // GROUP
    rate, weight = rate_ref[...], weight_ref[...]
    rcol = by_row(rate)
    wcol = by_row(weight)
    lane = iota((groups * MODES, CHUNK), 1)
    back = jnp.where(lane == 0, 0, CHUNK - lane).astype(F32)
    taps = (wcol * jnp.exp(-rcol * back)).reshape(groups, MODES, CHUNK).sum(axis=1)
    leave = jnp.exp(-rcol * (CHUNK - 1 - lane).astype(F32)).astype(BF)
    causal = iota((CHUNK, CHUNK), 0) >= iota((CHUNK, CHUNK), 1)
    for g in range(groups):
        wide = jnp.broadcast_to(taps[g : g + 1, :], (CHUNK, CHUNK))
        turned = pltpu.roll(wide, 0, 1, stride=1, stride_axis=0)
        table[0:CHUNK, g * CHUNK : (g + 1) * CHUNK] = jnp.where(causal, turned, 0.0).astype(BF)
        table[CHUNK : CHUNK + MODES, g * CHUNK : (g + 1) * CHUNK] = leave[g * MODES : (g + 1) * MODES]
    steps = (iota((CHUNK, groups * MODES), 0) + 1).astype(F32)
    din = (by_lane(weight) * jnp.exp(-by_lane(rate) * steps)).astype(BF)
    din_ref[...] = din
    power = jnp.exp(-rt_ref[...] * float(CHUNK))
    group_lane = iota((CHUNK, LANES), 1) // GROUP

    state = jnp.zeros((MODES, channels), F32)
    for pair in range(rows // (2 * CHUNK)):
        for j in range(2):
            q = 2 * pair + j
            span = slice(q * CHUNK, (q + 1) * CHUNK)
            before = halo_ref[0] if q == 0 else p_ref[q * CHUNK - 16 : q * CHUNK, :]
            q_ref[span, :] = tapped(sf_ref[0], p_ref[span, :].astype(F32), before.astype(F32)).astype(BF)
            for h in range(halves):
                part = x_ref[span, h * LANES : (h + 1) * LANES]
                for g in range(per_half):
                    masked[h, g * CHUNK : (g + 1) * CHUNK, j * LANES : (j + 1) * LANES] = jnp.where(
                        group_lane == g, part, jnp.zeros_like(part)
                    )
        depth = per_half * CHUNK
        made = [
            jnp.dot(table[:, h * depth : (h + 1) * depth], masked[h], preferred_element_type=F32)
            for h in range(halves)
        ]
        for j in range(2):
            q = 2 * pair + j
            full = jnp.concatenate([m[:, j * LANES : (j + 1) * LANES] for m in made], axis=1)
            within = full[:CHUNK]
            if q > 0:
                within = within + jnp.dot(din, spread(state), preferred_element_type=F32)
            y_ref[q * CHUNK : (q + 1) * CHUNK, :] = within.astype(BF)
            state = power * state + full[CHUNK:]


def mix_kernel(at_ref, ends_ref, rt_ref, din_ref, y_ref, q_ref, mixed_ref):
    rows = y_ref.shape[0]
    here = at_ref[0]
    rt = rt_ref[...]
    block_power = jnp.exp(-rt * float(rows))
    state = jnp.zeros(rt.shape, F32)
    for j in range(ends_ref.shape[0]):
        state = jnp.where(j < here, block_power * state + ends_ref[j], state)
    power = jnp.exp(-rt * float(CHUNK))
    din = din_ref[...]
    for q in range(rows // CHUNK):
        span = slice(q * CHUNK, (q + 1) * CHUNK)
        carried = jnp.dot(din, spread(state), preferred_element_type=F32)
        mixed_ref[span, :] = (q_ref[span, :].astype(F32) * (y_ref[span, :].astype(F32) + carried)).astype(BF)
        state = power * state


def side_by_side(left, refs):
    depth = refs[0].shape[1]

    @pl.when(pl.program_id(0) == 0)
    def _():
        for k, ref in enumerate(refs):
            left[:, k * depth : (k + 1) * depth] = ref[...]


def near_kernel(at_ref, a0, a1, w0, w1, c_ref, left, right):
    depth = w0.shape[0]
    side_by_side(left, (a0, a1))
    right[0:depth] = w0[...]
    right[depth : 2 * depth] = w1[...]
    block = 256
    for m in range(left.shape[0] // block):
        span = slice(m * block, (m + 1) * block)
        c_ref[span, :] = jnp.dot(left[span, :], right[...], preferred_element_type=F32).astype(BF)


def far_kernel(at_ref, a2, a3, f0, f1, f2, f3, rest, g013, g2, near_ref, c_ref, left, right):
    y, mine = at_ref[1], at_ref[2]
    size = f0.shape[0]
    depth = right.shape[0] // 2
    tail = depth - 4 * size
    side_by_side(left, (a2, a3))
    for k, ref in enumerate((f0, f1, f2, f3)):
        owner = lax.rem(y - k + 4, 4) * size
        right[pl.ds(pl.multiple_of(owner, 16), size), :] = ref[0:size]
        passed = g2[0:size] if k == 2 else g013[(0, 1, 0, 2)[k] * size : ((0, 1, 0, 2)[k] + 1) * size]
        right[pl.ds(pl.multiple_of(depth + owner, 16), size), :] = passed
    right[4 * size : depth] = rest[...]
    right[depth + 4 * size : 2 * depth] = g013[3 * size : 3 * size + tail]
    block = 256
    for m in range(left.shape[0] // block):
        span = slice(m * block, (m + 1) * block)
        total = jnp.dot(left[span, :], right[...], preferred_element_type=F32)
        total = (total + near_ref[span, :].astype(F32)).astype(BF)
        for b in range(block // 32):
            high, low = m * (block // 128) + b // 4, b % 4
            place = pl.multiple_of((high * 4 + jnp.bitwise_xor(low, mine)) * 32, 32)
            c_ref[pl.ds(place, 32), :] = total[b * 32 : (b + 1) * 32]


def join_kernel(at_ref, p0, p1, p2, p3, out_ref):
    mine = at_ref[2]
    width = p0.shape[1]
    for k, ref in enumerate((p0, p1, p2, p3)):
        place = pl.multiple_of(jnp.bitwise_xor(mine, k) * width, width)
        out_ref[:, pl.ds(place, width)] = ref[...]


def far(value):
    return pltpu.with_memory_space_constraint(value, pltpu.HBM)


def other_core(value):
    return lax.ppermute(value, "c", [(0, 1), (1, 0)])


def local(projected, short_filter, residue, rate, out_weight):
    rows, channels = projected.shape[1], projected.shape[2]
    groups = rate.shape[0]
    width = out_weight.shape[1] // 4
    y, xh, core = lax.axis_index("y"), lax.axis_index("xh"), lax.axis_index("c")
    seq = lax.axis_index(("y", "xl"))
    edge = projected[:, rows - 8 :, :]
    edge, y_then = lax.optimization_barrier((edge, y))
    halo = lax.ppermute(edge, ("y", "xl"), [(i, i + 1) for i in range(7)])

    size = 48
    tail = channels - 4 * size
    half = 2 * width
    mirror = [(0, 3), (3, 0), (1, 2), (2, 1)]

    def there(source, start, count):
        return lax.dynamic_slice(source, (start, (1 - xh) * half), (count, half))

    f0 = lax.ppermute(there(out_weight, y_then * size, size), ("xl", "xh"), mirror)
    rest = lax.ppermute(there(out_weight, 4 * size, tail), ("xl", "xh"), mirror)

    flat = groups * MODES
    span = 256
    once = {"pipeline_mode": pl.Buffered(1)}

    def whole(shape):
        return pl.BlockSpec(shape, lambda i: (0,) * len(shape))

    def third(k):
        return pl.BlockSpec((None, span, channels), lambda i: (k, i, 0))

    signal, end, rt = pl.pallas_call(
        state_kernel,
        out_shape=(
            pltpu.HBM((rows, channels), BF),
            jax.ShapeDtypeStruct((8, MODES, channels), F32),
            jax.ShapeDtypeStruct((MODES, channels), F32),
        ),
        grid=(rows // span,),
        in_specs=[third(1), third(2), whole(halo.shape), whole(short_filter.shape), whole(rate.shape)],
        out_specs=(
            pl.BlockSpec((span, channels), lambda i: (i, 0)),
            whole((8, MODES, channels)),
            whole((MODES, channels)),
        ),
        scratch_shapes=[
            pltpu.VMEM((2, 8, channels), F32),
            pltpu.VMEM((MODES, 8, channels), F32),
            pltpu.VMEM((MODES, 8, channels), F32),
        ],
        compiler_params=pltpu.CompilerParams(vmem_limit_bytes=12 * 2**20),
        cost_estimate=pl.CostEstimate(flops=10**6, bytes_accessed=2**16, transcendentals=0),
        name="state",
    )(far(projected), far(projected), halo, far(short_filter), far(rate))
    end, residue_late = lax.optimization_barrier((end, residue))
    at = jnp.stack([seq, y, xh * 2 + core, core]).astype(jnp.int32)
    weight = residue_late * jnp.sqrt(-jnp.expm1(-2.0 * rate))
    ends = lax.all_to_all(end, ("y", "xl"), 0, 0, tiled=True)
    conv, query, din = pl.pallas_call(
        conv_kernel,
        out_shape=(
            pltpu.HBM((rows, channels), BF),
            pltpu.HBM((rows, channels), BF),
            jax.ShapeDtypeStruct((CHUNK, flat), BF),
        ),
        grid=(1,),
        in_specs=[
            pl.BlockSpec((None, rows, channels), lambda i: (0, 0, 0)),
            whole((rows, channels)), whole(halo.shape), whole(short_filter.shape),
            whole(rate.shape), whole(rate.shape), whole(rt.shape),
        ],
        out_specs=(whole((rows, channels)), whole((rows, channels)), whole((CHUNK, flat))),
        scratch_shapes=[
            pltpu.VMEM((CHUNK + MODES, groups * CHUNK), BF),
            pltpu.VMEM((channels // LANES, LANES // GROUP * CHUNK, 2 * LANES), BF),
        ],
        compiler_params=pltpu.CompilerParams(vmem_limit_bytes=16 * 2**20),
        cost_estimate=pl.CostEstimate(flops=6 * 10**9, bytes_accessed=2**16, transcendentals=0),
        name="conv",
    )(far(projected), far(signal), halo, far(short_filter), far(rate), weight, rt)
    f1 = lax.ppermute(f0, "y", [(i, (i + 1) % 4) for i in range(4)])
    f3 = lax.ppermute(f0, "y", [(i, (i - 1) % 4) for i in range(4)])
    ends, f1, f3, rest, f0_late = lax.optimization_barrier((ends, f1, f3, rest, f0))
    f2 = lax.ppermute(f0_late, "y", [(i, (i + 2) % 4) for i in range(4)])
    mixed = pl.pallas_call(
        mix_kernel,
        out_shape=jax.ShapeDtypeStruct((rows, channels), BF),
        in_specs=[SM] + [VM] * 5,
        out_specs=VM,
        compiler_params=pltpu.CompilerParams(vmem_limit_bytes=10 * 2**20),
        cost_estimate=pl.CostEstimate(flops=10**6, bytes_accessed=2**16, transcendentals=0),
        name="mix",
    )(at, ends, rt, din, far(conv), far(query))

    a_far = lax.ppermute(mixed, "xh", [(0, 1), (1, 0)])
    def given(parts):
        return jnp.concatenate(
            [lax.dynamic_slice(v, (0, (1 - core) * width), (v.shape[0], width)) for v in parts], axis=0
        )

    _, core_late = lax.optimization_barrier((mixed, core))
    w_given = lax.dynamic_slice(out_weight, (0, (xh * 2 + 1 - core_late) * width), (channels, width))
    w_given, mixed_late = lax.optimization_barrier((w_given, mixed))
    a_other = other_core(mixed_late)
    w_other = other_core(w_given)
    g013 = other_core(given((f0_late, f1, f3, rest)))

    tile = 1024
    strips = width // tile

    def strip(shape):
        return pl.BlockSpec(shape[:-1] + (tile,), lambda i, at_ref: (0, i))

    def half_strip(shape):
        return pl.BlockSpec(shape[:-1] + (tile,), lambda i, at_ref: (0, at_ref[3] * strips + i))

    left_specs = [pl.BlockSpec((rows, channels), lambda i, at_ref: (0, 0), **once)] * 2
    near = pl.pallas_call(
        near_kernel,
        out_shape=jax.ShapeDtypeStruct((rows, width), BF),
        grid_spec=pltpu.PrefetchScalarGridSpec(
            num_scalar_prefetch=1,
            grid=(strips,),
            in_specs=left_specs
            + [pl.BlockSpec((channels, tile), lambda i, at_ref: (0, at_ref[2] * strips + i)), strip(w_other.shape)],
            out_specs=strip((rows, width)),
            scratch_shapes=[pltpu.VMEM((rows, 2 * channels), BF), pltpu.VMEM((2 * channels, tile), BF)],
        ),
        compiler_params=pltpu.CompilerParams(vmem_limit_bytes=24 * 2**20),
        cost_estimate=pl.CostEstimate(flops=2 * 10**9, bytes_accessed=6 * 2**20, transcendentals=0),
        name="near",
    )(at, mixed, a_other, far(out_weight), w_other)
    a_far, near, f2 = lax.optimization_barrier((a_far, near, f2))
    g2 = other_core(given((f2,)))
    a_far_other = other_core(a_far)
    partial = pl.pallas_call(
        far_kernel,
        out_shape=pltpu.HBM((rows, width), BF),
        grid_spec=pltpu.PrefetchScalarGridSpec(
            num_scalar_prefetch=1,
            grid=(strips,),
            in_specs=left_specs
            + [half_strip(v.shape) for v in (f0, f1, f2, f3, rest)]
            + [strip(g013.shape), strip(g2.shape)]
            + [strip((rows, width))],
            out_specs=strip((rows, width)),
            scratch_shapes=[pltpu.VMEM((rows, 2 * channels), BF), pltpu.VMEM((2 * channels, tile), BF)],
        ),
        compiler_params=pltpu.CompilerParams(vmem_limit_bytes=30 * 2**20),
        cost_estimate=pl.CostEstimate(flops=2 * 10**9, bytes_accessed=10 * 2**20, transcendentals=0),
        name="far",
    )(at, a_far, a_far_other, f0_late, f1, f2, f3, rest, g013, g2, near)

    summed = lax.psum_scatter(partial, "z", scatter_dimension=0, tiled=True)
    size = summed.shape[0] // 4

    def traded(k):
        pairs = [(i, i ^ k) for i in range(4)]
        return lax.ppermute(summed[k * size : (k + 1) * size], ("xh", "c"), pairs)

    return pl.pallas_call(
        join_kernel,
        out_shape=jax.ShapeDtypeStruct((size, 4 * width), BF),
        in_specs=[SM] + [VM] * 4,
        out_specs=VM,
        compiler_params=pltpu.CompilerParams(vmem_limit_bytes=4 * 2**20),
        name="join",
    )(at, summed[:size], traded(1), traded(2), traded(3))


def solution(mesh):
    fine = Mesh(mesh.devices.reshape(4, 2, 8, 2, 2), ("y", "xl", "z", "xh", "c"))
    seq, tp = ("y", "xl"), ("z", "xh", "c")
    placed = (P(None, seq, tp), P(None, None, tp), P(tp, None), P(tp, None), P(tp, None))
    return jax.shard_map(local, mesh=fine, in_specs=placed, out_specs=P(seq + tp, None), check_vma=False)
```

```python
import jax
import jax.numpy as jnp
from jax import lax
from jax.experimental import pallas as pl
from jax.experimental.pallas import tpu as pltpu
from jax.sharding import Mesh, PartitionSpec as P

GROUP = 16
MODES = 16
CHUNK = 128
LANES = 128
BF = jnp.bfloat16
F32 = jnp.float32
VM = pl.BlockSpec(memory_space=pltpu.VMEM)
SM = pl.BlockSpec(memory_space=pltpu.SMEM)


def iota(shape, dim):
    return lax.broadcasted_iota(jnp.int32, shape, dim)


def spread(state):
    width = state.shape[1]
    groups = width // GROUP
    tall = jnp.concatenate([state] * groups, axis=0)
    shape = (groups * MODES, width)
    own = iota(shape, 0) // MODES == iota(shape, 1) // GROUP
    return jnp.where(own, tall, 0.0).astype(BF)


def one_hot(rows, columns, row_size, column_size):
    shape = (rows, columns)
    return (iota(shape, 0) // row_size == iota(shape, 1) // column_size).astype(F32)


def exact_dot(a, b, dims):
    return lax.dot_general(a, b, (dims, ((), ())), precision=lax.Precision.HIGHEST, preferred_element_type=F32)


def by_channel(table, channels):
    return exact_dot(table, one_hot(table.shape[0], channels, 1, GROUP), ((0,), (0,)))


def by_row(table):
    flat = table.shape[0] * MODES
    wide = exact_dot(one_hot(flat, table.shape[0], MODES, 1), table, ((1,), (0,)))
    keep = iota((flat, MODES), 0) % MODES == iota((flat, MODES), 1)
    return jnp.where(keep, wide, 0.0).sum(axis=1, keepdims=True)


def by_lane(table):
    flat = table.shape[0] * MODES
    wide = exact_dot(table, one_hot(table.shape[0], flat, 1, MODES), ((0,), (0,)))
    keep = iota((MODES, flat), 1) % MODES == iota((MODES, flat), 0)
    return jnp.where(keep, wide, 0.0).sum(axis=0, keepdims=True)


def tapped(taps, cur, before):
    ext = jnp.concatenate([before, cur], axis=0)
    skip = before.shape[0]
    one = pltpu.roll(ext, 1, 0)[skip:]
    two = pltpu.roll(ext, 2, 0)[skip:]
    return taps[0:1, :] * cur + taps[1:2, :] * one + taps[2:3, :] * two


def state_kernel(k_ref, v_ref, halo_ref, sf_ref, rate_ref, x_ref, end_ref, rt_ref, tail, total, power):
    step = pl.program_id(0)
    rows, channels = k_ref.shape

    @pl.when(step == 0)
    def _():
        rt = by_channel(rate_ref[...], channels)
        rt_ref[...] = rt
        total[...] = jnp.zeros_like(total)
        for n in range(MODES):
            power[n] = jnp.broadcast_to(jnp.exp(-8.0 * rt[n : n + 1, :]), (8, channels))
        for i in range(2):
            tail[i] = halo_ref[i + 1].astype(F32)

    featured = []
    for i, ref in enumerate((k_ref, v_ref)):
        cur = ref[...].astype(F32)
        featured.append(tapped(sf_ref[i + 1], cur, tail[i]))
        tail[i] = cur[rows - 8 :]
    signal = featured[0] * featured[1]
    x_ref[...] = signal.astype(BF)
    for h in range(channels // LANES):
        lanes = slice(h * LANES, (h + 1) * LANES)
        for first in range(0, MODES, 8):
            sums = [total[n, :, lanes] for n in range(first, first + 8)]
            powers = [power[n, :, lanes] for n in range(first, first + 8)]
            for b in range(rows // 8):
                block = signal[b * 8 : (b + 1) * 8, lanes]
                sums = [s * w + block for s, w in zip(sums, powers)]
            for n in range(8):
                total[first + n, :, lanes] = sums[n]

    @pl.when(step == pl.num_programs(0) - 1)
    def _():
        rt = rt_ref[...]
        ahead = (7 - iota((8, channels), 0)).astype(F32)
        end = jnp.concatenate(
            [
                (total[n] * jnp.exp(-ahead * rt[n : n + 1, :])).sum(axis=0, keepdims=True)
                for n in range(MODES)
            ],
            axis=0,
        )
        for j in range(end_ref.shape[0]):
            end_ref[j] = end


def conv_kernel(p_ref, x_ref, halo_ref, sf_ref, rate_ref, weight_ref, rt_ref,
                y_ref, q_ref, din_ref, table, masked):
    rows, channels = x_ref.shape
    halves = channels // LANES
    per_half = LANES // GROUP
    groups = channels // GROUP
    rate, weight = rate_ref[...], weight_ref[...]
    rcol = by_row(rate)
    wcol = by_row(weight)
    lane = iota((groups * MODES, CHUNK), 1)
    back = jnp.where(lane == 0, 0, CHUNK - lane).astype(F32)
    taps = (wcol * jnp.exp(-rcol * back)).reshape(groups, MODES, CHUNK).sum(axis=1)
    leave = jnp.exp(-rcol * (CHUNK - 1 - lane).astype(F32)).astype(BF)
    causal = iota((CHUNK, CHUNK), 0) >= iota((CHUNK, CHUNK), 1)
    for g in range(groups):
        wide = jnp.broadcast_to(taps[g : g + 1, :], (CHUNK, CHUNK))
        turned = pltpu.roll(wide, 0, 1, stride=1, stride_axis=0)
        table[0:CHUNK, g * CHUNK : (g + 1) * CHUNK] = jnp.where(causal, turned, 0.0).astype(BF)
        table[CHUNK : CHUNK + MODES, g * CHUNK : (g + 1) * CHUNK] = leave[g * MODES : (g + 1) * MODES]
    steps = (iota((CHUNK, groups * MODES), 0) + 1).astype(F32)
    din = (by_lane(weight) * jnp.exp(-by_lane(rate) * steps)).astype(BF)
    din_ref[...] = din
    power = jnp.exp(-rt_ref[...] * float(CHUNK))
    group_lane = iota((CHUNK, LANES), 1) // GROUP

    state = jnp.zeros((MODES, channels), F32)
    for pair in range(rows // (2 * CHUNK)):
        for j in range(2):
            q = 2 * pair + j
            span = slice(q * CHUNK, (q + 1) * CHUNK)
            before = halo_ref[0] if q == 0 else p_ref[q * CHUNK - 16 : q * CHUNK, :]
            q_ref[span, :] = tapped(sf_ref[0], p_ref[span, :].astype(F32), before.astype(F32)).astype(BF)
            for h in range(halves):
                part = x_ref[span, h * LANES : (h + 1) * LANES]
                for g in range(per_half):
                    masked[h, g * CHUNK : (g + 1) * CHUNK, j * LANES : (j + 1) * LANES] = jnp.where(
                        group_lane == g, part, jnp.zeros_like(part)
                    )
        depth = per_half * CHUNK
        made = [
            jnp.dot(table[:, h * depth : (h + 1) * depth], masked[h], preferred_element_type=F32)
            for h in range(halves)
        ]
        for j in range(2):
            q = 2 * pair + j
            full = jnp.concatenate([m[:, j * LANES : (j + 1) * LANES] for m in made], axis=1)
            within = full[:CHUNK]
            if q > 0:
                within = within + jnp.dot(din, spread(state), preferred_element_type=F32)
            y_ref[q * CHUNK : (q + 1) * CHUNK, :] = within.astype(BF)
            state = power * state + full[CHUNK:]


def mix_kernel(at_ref, ends_ref, rt_ref, din_ref, y_ref, q_ref, mixed_ref):
    rows = y_ref.shape[0]
    here = at_ref[0]
    rt = rt_ref[...]
    block_power = jnp.exp(-rt * float(rows))
    state = jnp.zeros(rt.shape, F32)
    for j in range(ends_ref.shape[0]):
        state = jnp.where(j < here, block_power * state + ends_ref[j], state)
    power = jnp.exp(-rt * float(CHUNK))
    din = din_ref[...]
    for q in range(rows // CHUNK):
        span = slice(q * CHUNK, (q + 1) * CHUNK)
        carried = jnp.dot(din, spread(state), preferred_element_type=F32)
        mixed_ref[span, :] = (q_ref[span, :].astype(F32) * (y_ref[span, :].astype(F32) + carried)).astype(BF)
        state = power * state


def side_by_side(left, refs):
    depth = refs[0].shape[1]

    @pl.when(pl.program_id(0) == 0)
    def _():
        for k, ref in enumerate(refs):
            left[:, k * depth : (k + 1) * depth] = ref[...]


def near_kernel(at_ref, a0, a1, w0, w1, c_ref, left, right):
    depth = w0.shape[0]
    side_by_side(left, (a0, a1))
    right[0:depth] = w0[...]
    right[depth : 2 * depth] = w1[...]
    block = 256
    for m in range(left.shape[0] // block):
        span = slice(m * block, (m + 1) * block)
        c_ref[span, :] = jnp.dot(left[span, :], right[...], preferred_element_type=F32).astype(BF)


def far_kernel(at_ref, a2, a3, f0, f1, f2, f3, rest, g013, g2, near_ref, c_ref, left, right):
    y, mine = at_ref[1], at_ref[2]
    size = f0.shape[0]
    depth = right.shape[0] // 2
    tail = depth - 4 * size
    side_by_side(left, (a2, a3))
    for k, ref in enumerate((f0, f1, f2, f3)):
        owner = lax.rem(y - k + 4, 4) * size
        right[pl.ds(pl.multiple_of(owner, 16), size), :] = ref[0:size]
        passed = g2[0:size] if k == 2 else g013[(0, 1, 0, 2)[k] * size : ((0, 1, 0, 2)[k] + 1) * size]
        right[pl.ds(pl.multiple_of(depth + owner, 16), size), :] = passed
    right[4 * size : depth] = rest[...]
    right[depth + 4 * size : 2 * depth] = g013[3 * size : 3 * size + tail]
    block = 256
    for m in range(left.shape[0] // block):
        span = slice(m * block, (m + 1) * block)
        total = jnp.dot(left[span, :], right[...], preferred_element_type=F32)
        total = (total + near_ref[span, :].astype(F32)).astype(BF)
        for b in range(block // 32):
            high, low = m * (block // 128) + b // 4, b % 4
            place = pl.multiple_of((high * 4 + jnp.bitwise_xor(low, mine)) * 32, 32)
            c_ref[pl.ds(place, 32), :] = total[b * 32 : (b + 1) * 32]


def join_kernel(at_ref, p0, p1, p2, p3, out_ref):
    mine = at_ref[2]
    width = p0.shape[1]
    for k, ref in enumerate((p0, p1, p2, p3)):
        place = pl.multiple_of(jnp.bitwise_xor(mine, k) * width, width)
        out_ref[:, pl.ds(place, width)] = ref[...]


def far(value):
    return pltpu.with_memory_space_constraint(value, pltpu.HBM)


def other_core(value):
    return lax.ppermute(value, "c", [(0, 1), (1, 0)])


def local(projected, short_filter, residue, rate, out_weight):
    rows, channels = projected.shape[1], projected.shape[2]
    groups = rate.shape[0]
    width = out_weight.shape[1] // 4
    y, xh, core = lax.axis_index("y"), lax.axis_index("xh"), lax.axis_index("c")
    seq = lax.axis_index(("y", "xl"))
    edge = projected[:, rows - 8 :, :]
    edge, y_then = lax.optimization_barrier((edge, y))
    halo = lax.ppermute(edge, ("y", "xl"), [(i, i + 1) for i in range(7)])

    size = 48
    tail = channels - 4 * size
    half = 2 * width
    mirror = [(0, 3), (3, 0), (1, 2), (2, 1)]

    def there(source, start, count):
        return lax.dynamic_slice(source, (start, (1 - xh) * half), (count, half))

    f0 = lax.ppermute(there(out_weight, y_then * size, size), ("xl", "xh"), mirror)
    rest = lax.ppermute(there(out_weight, 4 * size, tail), ("xl", "xh"), mirror)

    flat = groups * MODES
    span = 512
    once = {"pipeline_mode": pl.Buffered(1)}

    def whole(shape):
        return pl.BlockSpec(shape, lambda i: (0,) * len(shape))

    def third(k):
        return pl.BlockSpec((None, span, channels), lambda i: (k, i, 0))

    signal, end, rt = pl.pallas_call(
        state_kernel,
        out_shape=(
            pltpu.HBM((rows, channels), BF),
            jax.ShapeDtypeStruct((8, MODES, channels), F32),
            jax.ShapeDtypeStruct((MODES, channels), F32),
        ),
        grid=(rows // span,),
        in_specs=[third(1), third(2), whole(halo.shape), whole(short_filter.shape), whole(rate.shape)],
        out_specs=(
            pl.BlockSpec((span, channels), lambda i: (i, 0)),
            whole((8, MODES, channels)),
            whole((MODES, channels)),
        ),
        scratch_shapes=[
            pltpu.VMEM((2, 8, channels), F32),
            pltpu.VMEM((MODES, 8, channels), F32),
            pltpu.VMEM((MODES, 8, channels), F32),
        ],
        compiler_params=pltpu.CompilerParams(vmem_limit_bytes=12 * 2**20),
        cost_estimate=pl.CostEstimate(flops=10**6, bytes_accessed=2**16, transcendentals=0),
        name="state",
    )(far(projected), far(projected), halo, far(short_filter), far(rate))
    end, residue_late = lax.optimization_barrier((end, residue))
    at = jnp.stack([seq, y, xh * 2 + core, core]).astype(jnp.int32)
    weight = residue_late * jnp.sqrt(-jnp.expm1(-2.0 * rate))
    ends = lax.all_to_all(end, ("y", "xl"), 0, 0, tiled=True)
    conv, query, din = pl.pallas_call(
        conv_kernel,
        out_shape=(
            pltpu.HBM((rows, channels), BF),
            pltpu.HBM((rows, channels), BF),
            jax.ShapeDtypeStruct((CHUNK, flat), BF),
        ),
        grid=(1,),
        in_specs=[
            pl.BlockSpec((None, rows, channels), lambda i: (0, 0, 0)),
            whole((rows, channels)), whole(halo.shape), whole(short_filter.shape),
            whole(rate.shape), whole(rate.shape), whole(rt.shape),
        ],
        out_specs=(whole((rows, channels)), whole((rows, channels)), whole((CHUNK, flat))),
        scratch_shapes=[
            pltpu.VMEM((CHUNK + MODES, groups * CHUNK), BF),
            pltpu.VMEM((channels // LANES, LANES // GROUP * CHUNK, 2 * LANES), BF),
        ],
        compiler_params=pltpu.CompilerParams(vmem_limit_bytes=16 * 2**20),
        cost_estimate=pl.CostEstimate(flops=6 * 10**9, bytes_accessed=2**16, transcendentals=0),
        name="conv",
    )(far(projected), far(signal), halo, far(short_filter), far(rate), weight, rt)
    f1 = lax.ppermute(f0, "y", [(i, (i + 1) % 4) for i in range(4)])
    f3 = lax.ppermute(f0, "y", [(i, (i - 1) % 4) for i in range(4)])
    ends, f1, f3, rest, f0_late = lax.optimization_barrier((ends, f1, f3, rest, f0))
    f2 = lax.ppermute(f0_late, "y", [(i, (i + 2) % 4) for i in range(4)])
    mixed = pl.pallas_call(
        mix_kernel,
        out_shape=jax.ShapeDtypeStruct((rows, channels), BF),
        in_specs=[SM] + [VM] * 5,
        out_specs=VM,
        compiler_params=pltpu.CompilerParams(vmem_limit_bytes=10 * 2**20),
        cost_estimate=pl.CostEstimate(flops=10**6, bytes_accessed=2**16, transcendentals=0),
        name="mix",
    )(at, ends, rt, din, far(conv), far(query))

    a_far = lax.ppermute(mixed, "xh", [(0, 1), (1, 0)])
    def given(parts):
        return jnp.concatenate(
            [lax.dynamic_slice(v, (0, (1 - core) * width), (v.shape[0], width)) for v in parts], axis=0
        )

    _, core_late = lax.optimization_barrier((mixed, core))
    w_given = lax.dynamic_slice(out_weight, (0, (xh * 2 + 1 - core_late) * width), (channels, width))
    w_given, mixed_late = lax.optimization_barrier((w_given, mixed))
    a_other = other_core(mixed_late)
    w_other = other_core(w_given)
    g013 = other_core(given((f0_late, f1, f3, rest)))

    tile = 1024
    strips = width // tile

    def strip(shape):
        return pl.BlockSpec(shape[:-1] + (tile,), lambda i, at_ref: (0, i))

    def half_strip(shape):
        return pl.BlockSpec(shape[:-1] + (tile,), lambda i, at_ref: (0, at_ref[3] * strips + i))

    left_specs = [pl.BlockSpec((rows, channels), lambda i, at_ref: (0, 0), **once)] * 2
    near = pl.pallas_call(
        near_kernel,
        out_shape=jax.ShapeDtypeStruct((rows, width), BF),
        grid_spec=pltpu.PrefetchScalarGridSpec(
            num_scalar_prefetch=1,
            grid=(strips,),
            in_specs=left_specs
            + [pl.BlockSpec((channels, tile), lambda i, at_ref: (0, at_ref[2] * strips + i)), strip(w_other.shape)],
            out_specs=strip((rows, width)),
            scratch_shapes=[pltpu.VMEM((rows, 2 * channels), BF), pltpu.VMEM((2 * channels, tile), BF)],
        ),
        compiler_params=pltpu.CompilerParams(vmem_limit_bytes=24 * 2**20),
        cost_estimate=pl.CostEstimate(flops=2 * 10**9, bytes_accessed=6 * 2**20, transcendentals=0),
        name="near",
    )(at, mixed, a_other, far(out_weight), w_other)
    a_far, near, f2 = lax.optimization_barrier((a_far, near, f2))
    g2 = other_core(given((f2,)))
    a_far_other = other_core(a_far)
    partial = pl.pallas_call(
        far_kernel,
        out_shape=pltpu.HBM((rows, width), BF),
        grid_spec=pltpu.PrefetchScalarGridSpec(
            num_scalar_prefetch=1,
            grid=(strips,),
            in_specs=left_specs
            + [half_strip(v.shape) for v in (f0, f1, f2, f3, rest)]
            + [strip(g013.shape), strip(g2.shape)]
            + [strip((rows, width))],
            out_specs=strip((rows, width)),
            scratch_shapes=[pltpu.VMEM((rows, 2 * channels), BF), pltpu.VMEM((2 * channels, tile), BF)],
        ),
        compiler_params=pltpu.CompilerParams(vmem_limit_bytes=30 * 2**20),
        cost_estimate=pl.CostEstimate(flops=2 * 10**9, bytes_accessed=10 * 2**20, transcendentals=0),
        name="far",
    )(at, a_far, a_far_other, f0_late, f1, f2, f3, rest, g013, g2, near)

    summed = lax.psum_scatter(partial, "z", scatter_dimension=0, tiled=True)
    size = summed.shape[0] // 4

    def traded(k):
        pairs = [(i, i ^ k) for i in range(4)]
        return lax.ppermute(summed[k * size : (k + 1) * size], ("xh", "c"), pairs)

    return pl.pallas_call(
        join_kernel,
        out_shape=jax.ShapeDtypeStruct((size, 4 * width), BF),
        in_specs=[SM] + [VM] * 4,
        out_specs=VM,
        compiler_params=pltpu.CompilerParams(vmem_limit_bytes=4 * 2**20),
        name="join",
    )(at, summed[:size], traded(1), traded(2), traded(3))


def solution(mesh):
    fine = Mesh(mesh.devices.reshape(4, 2, 8, 2, 2), ("y", "xl", "z", "xh", "c"))
    seq, tp = ("y", "xl"), ("z", "xh", "c")
    placed = (P(None, seq, tp), P(None, None, tp), P(tp, None), P(tp, None), P(tp, None))
    return jax.shard_map(local, mesh=fine, in_specs=placed, out_specs=P(seq + tp, None), check_vma=False)
```

```python
import jax
import jax.numpy as jnp
from jax import lax
from jax.experimental import pallas as pl
from jax.experimental.pallas import tpu as pltpu
from jax.sharding import Mesh, PartitionSpec as P

GROUP = 16
MODES = 16
CHUNK = 128
LANES = 128
BF = jnp.bfloat16
F32 = jnp.float32
VM = pl.BlockSpec(memory_space=pltpu.VMEM)
SM = pl.BlockSpec(memory_space=pltpu.SMEM)


def iota(shape, dim):
    return lax.broadcasted_iota(jnp.int32, shape, dim)


def spread(state):
    width = state.shape[1]
    groups = width // GROUP
    tall = jnp.concatenate([state] * groups, axis=0)
    shape = (groups * MODES, width)
    own = iota(shape, 0) // MODES == iota(shape, 1) // GROUP
    return jnp.where(own, tall, 0.0).astype(BF)


def one_hot(rows, columns, row_size, column_size):
    shape = (rows, columns)
    return (iota(shape, 0) // row_size == iota(shape, 1) // column_size).astype(F32)


def exact_dot(a, b, dims):
    return lax.dot_general(a, b, (dims, ((), ())), precision=lax.Precision.HIGHEST, preferred_element_type=F32)


def by_channel(table, channels):
    return exact_dot(table, one_hot(table.shape[0], channels, 1, GROUP), ((0,), (0,)))


def by_row(table):
    flat = table.shape[0] * MODES
    wide = exact_dot(one_hot(flat, table.shape[0], MODES, 1), table, ((1,), (0,)))
    keep = iota((flat, MODES), 0) % MODES == iota((flat, MODES), 1)
    return jnp.where(keep, wide, 0.0).sum(axis=1, keepdims=True)


def by_lane(table):
    flat = table.shape[0] * MODES
    wide = exact_dot(table, one_hot(table.shape[0], flat, 1, MODES), ((0,), (0,)))
    keep = iota((MODES, flat), 1) % MODES == iota((MODES, flat), 0)
    return jnp.where(keep, wide, 0.0).sum(axis=0, keepdims=True)


def tapped(taps, cur, before):
    ext = jnp.concatenate([before, cur], axis=0)
    skip = before.shape[0]
    one = pltpu.roll(ext, 1, 0)[skip:]
    two = pltpu.roll(ext, 2, 0)[skip:]
    return taps[0:1, :] * cur + taps[1:2, :] * one + taps[2:3, :] * two


def state_kernel(k_ref, v_ref, halo_ref, sf_ref, rate_ref, x_ref, end_ref, rt_ref, tail, total, power):
    step = pl.program_id(0)
    rows, channels = k_ref.shape

    @pl.when(step == 0)
    def _():
        rt = by_channel(rate_ref[...], channels)
        rt_ref[...] = rt
        total[...] = jnp.zeros_like(total)
        for n in range(MODES):
            power[n] = jnp.broadcast_to(jnp.exp(-8.0 * rt[n : n + 1, :]), (8, channels))
        for i in range(2):
            tail[i] = halo_ref[i + 1].astype(F32)

    featured = []
    for i, ref in enumerate((k_ref, v_ref)):
        cur = ref[...].astype(F32)
        featured.append(tapped(sf_ref[i + 1], cur, tail[i]))
        tail[i] = cur[rows - 8 :]
    signal = featured[0] * featured[1]
    x_ref[...] = signal.astype(BF)
    for h in range(channels // LANES):
        lanes = slice(h * LANES, (h + 1) * LANES)
        for first in range(0, MODES, 8):
            sums = [total[n, :, lanes] for n in range(first, first + 8)]
            powers = [power[n, :, lanes] for n in range(first, first + 8)]
            for b in range(rows // 8):
                block = signal[b * 8 : (b + 1) * 8, lanes]
                sums = [s * w + block for s, w in zip(sums, powers)]
            for n in range(8):
                total[first + n, :, lanes] = sums[n]

    @pl.when(step == pl.num_programs(0) - 1)
    def _():
        rt = rt_ref[...]
        ahead = (7 - iota((8, channels), 0)).astype(F32)
        end = jnp.concatenate(
            [
                (total[n] * jnp.exp(-ahead * rt[n : n + 1, :])).sum(axis=0, keepdims=True)
                for n in range(MODES)
            ],
            axis=0,
        )
        for j in range(end_ref.shape[0]):
            end_ref[j] = end


def conv_kernel(p_ref, x_ref, halo_ref, sf_ref, rate_ref, weight_ref, rt_ref,
                y_ref, q_ref, din_ref, table, masked):
    rows, channels = x_ref.shape
    halves = channels // LANES
    per_half = LANES // GROUP
    groups = channels // GROUP
    rate, weight = rate_ref[...], weight_ref[...]
    rcol = by_row(rate)
    wcol = by_row(weight)
    lane = iota((groups * MODES, CHUNK), 1)
    back = jnp.where(lane == 0, 0, CHUNK - lane).astype(F32)
    taps = (wcol * jnp.exp(-rcol * back)).reshape(groups, MODES, CHUNK).sum(axis=1)
    leave = jnp.exp(-rcol * (CHUNK - 1 - lane).astype(F32)).astype(BF)
    causal = iota((CHUNK, CHUNK), 0) >= iota((CHUNK, CHUNK), 1)
    for g in range(groups):
        wide = jnp.broadcast_to(taps[g : g + 1, :], (CHUNK, CHUNK))
        turned = pltpu.roll(wide, 0, 1, stride=1, stride_axis=0)
        table[0:CHUNK, g * CHUNK : (g + 1) * CHUNK] = jnp.where(causal, turned, 0.0).astype(BF)
        table[CHUNK : CHUNK + MODES, g * CHUNK : (g + 1) * CHUNK] = leave[g * MODES : (g + 1) * MODES]
    steps = (iota((CHUNK, groups * MODES), 0) + 1).astype(F32)
    din = (by_lane(weight) * jnp.exp(-by_lane(rate) * steps)).astype(BF)
    din_ref[...] = din
    power = jnp.exp(-rt_ref[...] * float(CHUNK))
    group_lane = iota((CHUNK, LANES), 1) // GROUP

    state = jnp.zeros((MODES, channels), F32)
    for pair in range(rows // (2 * CHUNK)):
        for j in range(2):
            q = 2 * pair + j
            span = slice(q * CHUNK, (q + 1) * CHUNK)
            before = halo_ref[0] if q == 0 else p_ref[q * CHUNK - 16 : q * CHUNK, :]
            q_ref[span, :] = tapped(sf_ref[0], p_ref[span, :].astype(F32), before.astype(F32)).astype(BF)
            for h in range(halves):
                part = x_ref[span, h * LANES : (h + 1) * LANES]
                for g in range(per_half):
                    masked[h, g * CHUNK : (g + 1) * CHUNK, j * LANES : (j + 1) * LANES] = jnp.where(
                        group_lane == g, part, jnp.zeros_like(part)
                    )
        depth = per_half * CHUNK
        made = [
            jnp.dot(table[:, h * depth : (h + 1) * depth], masked[h], preferred_element_type=F32)
            for h in range(halves)
        ]
        for j in range(2):
            q = 2 * pair + j
            full = jnp.concatenate([m[:, j * LANES : (j + 1) * LANES] for m in made], axis=1)
            within = full[:CHUNK]
            if q > 0:
                within = within + jnp.dot(din, spread(state), preferred_element_type=F32)
            y_ref[q * CHUNK : (q + 1) * CHUNK, :] = within.astype(BF)
            state = power * state + full[CHUNK:]


def mix_kernel(at_ref, ends_ref, rt_ref, din_ref, y_ref, q_ref, mixed_ref):
    rows = y_ref.shape[0]
    here = at_ref[0]
    rt = rt_ref[...]
    block_power = jnp.exp(-rt * float(rows))
    state = jnp.zeros(rt.shape, F32)
    for j in range(ends_ref.shape[0]):
        state = jnp.where(j < here, block_power * state + ends_ref[j], state)
    power = jnp.exp(-rt * float(CHUNK))
    din = din_ref[...]
    for q in range(rows // CHUNK):
        span = slice(q * CHUNK, (q + 1) * CHUNK)
        carried = jnp.dot(din, spread(state), preferred_element_type=F32)
        mixed_ref[span, :] = (q_ref[span, :].astype(F32) * (y_ref[span, :].astype(F32) + carried)).astype(BF)
        state = power * state


def near_kernel(at_ref, a0, a1, w0, w1, c_ref):
    block = 256
    for m in range(a0.shape[0] // block):
        span = slice(m * block, (m + 1) * block)
        total = jnp.dot(a0[span, :], w0[...], preferred_element_type=F32)
        total += jnp.dot(a1[span, :], w1[...], preferred_element_type=F32)
        c_ref[span, :] = total.astype(BF)


def far_kernel(at_ref, a2, a3, f0, f1, f2, f3, rest, g013, g2, near_ref, c_ref, right):
    y, mine = at_ref[1], at_ref[2]
    size = f0.shape[0]
    depth = right.shape[0] // 2
    tail = depth - 4 * size
    for k, ref in enumerate((f0, f1, f2, f3)):
        owner = lax.rem(y - k + 4, 4) * size
        right[pl.ds(pl.multiple_of(owner, 16), size), :] = ref[0:size]
        passed = g2[0:size] if k == 2 else g013[(0, 1, 0, 2)[k] * size : ((0, 1, 0, 2)[k] + 1) * size]
        right[pl.ds(pl.multiple_of(depth + owner, 16), size), :] = passed
    right[4 * size : depth] = rest[...]
    right[depth + 4 * size : 2 * depth] = g013[3 * size : 3 * size + tail]
    block = 256
    for m in range(a2.shape[0] // block):
        span = slice(m * block, (m + 1) * block)
        total = jnp.dot(a2[span, :], right[0:depth], preferred_element_type=F32)
        total += jnp.dot(a3[span, :], right[depth : 2 * depth], preferred_element_type=F32)
        total = (total + near_ref[span, :].astype(F32)).astype(BF)
        for b in range(block // 32):
            high, low = m * (block // 128) + b // 4, b % 4
            place = pl.multiple_of((high * 4 + jnp.bitwise_xor(low, mine)) * 32, 32)
            c_ref[pl.ds(place, 32), :] = total[b * 32 : (b + 1) * 32]


def join_kernel(at_ref, p0, p1, p2, p3, out_ref):
    mine = at_ref[2]
    width = p0.shape[1]
    for k, ref in enumerate((p0, p1, p2, p3)):
        place = pl.multiple_of(jnp.bitwise_xor(mine, k) * width, width)
        out_ref[:, pl.ds(place, width)] = ref[...]


def far(value):
    return pltpu.with_memory_space_constraint(value, pltpu.HBM)


def other_core(value):
    return lax.ppermute(value, "c", [(0, 1), (1, 0)])


def local(projected, short_filter, residue, rate, out_weight):
    rows, channels = projected.shape[1], projected.shape[2]
    groups = rate.shape[0]
    width = out_weight.shape[1] // 4
    y, xh, core = lax.axis_index("y"), lax.axis_index("xh"), lax.axis_index("c")
    seq = lax.axis_index(("y", "xl"))
    edge = projected[:, rows - 8 :, :]
    edge, y_then = lax.optimization_barrier((edge, y))
    halo = lax.ppermute(edge, ("y", "xl"), [(i, i + 1) for i in range(7)])

    size = 48
    tail = channels - 4 * size
    half = 2 * width
    mirror = [(0, 3), (3, 0), (1, 2), (2, 1)]

    def there(source, start, count):
        return lax.dynamic_slice(source, (start, (1 - xh) * half), (count, half))

    f0 = lax.ppermute(there(out_weight, y_then * size, size), ("xl", "xh"), mirror)
    rest = lax.ppermute(there(out_weight, 4 * size, tail), ("xl", "xh"), mirror)

    flat = groups * MODES
    span = 256
    once = {"pipeline_mode": pl.Buffered(1)}

    def whole(shape):
        return pl.BlockSpec(shape, lambda i: (0,) * len(shape))

    def third(k):
        return pl.BlockSpec((None, span, channels), lambda i: (k, i, 0))

    signal, end, rt = pl.pallas_call(
        state_kernel,
        out_shape=(
            pltpu.HBM((rows, channels), BF),
            jax.ShapeDtypeStruct((8, MODES, channels), F32),
            jax.ShapeDtypeStruct((MODES, channels), F32),
        ),
        grid=(rows // span,),
        in_specs=[third(1), third(2), whole(halo.shape), whole(short_filter.shape), whole(rate.shape)],
        out_specs=(
            pl.BlockSpec((span, channels), lambda i: (i, 0)),
            whole((8, MODES, channels)),
            whole((MODES, channels)),
        ),
        scratch_shapes=[
            pltpu.VMEM((2, 8, channels), F32),
            pltpu.VMEM((MODES, 8, channels), F32),
            pltpu.VMEM((MODES, 8, channels), F32),
        ],
        compiler_params=pltpu.CompilerParams(vmem_limit_bytes=12 * 2**20),
        cost_estimate=pl.CostEstimate(flops=10**6, bytes_accessed=2**16, transcendentals=0),
        name="state",
    )(far(projected), far(projected), halo, far(short_filter), far(rate))
    end, residue_late = lax.optimization_barrier((end, residue))
    at = jnp.stack([seq, y, xh * 2 + core, core]).astype(jnp.int32)
    weight = residue_late * jnp.sqrt(-jnp.expm1(-2.0 * rate))
    ends = lax.all_to_all(end, ("y", "xl"), 0, 0, tiled=True)
    conv, query, din = pl.pallas_call(
        conv_kernel,
        out_shape=(
            pltpu.HBM((rows, channels), BF),
            pltpu.HBM((rows, channels), BF),
            jax.ShapeDtypeStruct((CHUNK, flat), BF),
        ),
        grid=(1,),
        in_specs=[
            pl.BlockSpec((None, rows, channels), lambda i: (0, 0, 0)),
            whole((rows, channels)), whole(halo.shape), whole(short_filter.shape),
            whole(rate.shape), whole(rate.shape), whole(rt.shape),
        ],
        out_specs=(whole((rows, channels)), whole((rows, channels)), whole((CHUNK, flat))),
        scratch_shapes=[
            pltpu.VMEM((CHUNK + MODES, groups * CHUNK), BF),
            pltpu.VMEM((channels // LANES, LANES // GROUP * CHUNK, 2 * LANES), BF),
        ],
        compiler_params=pltpu.CompilerParams(vmem_limit_bytes=16 * 2**20),
        cost_estimate=pl.CostEstimate(flops=6 * 10**9, bytes_accessed=2**16, transcendentals=0),
        name="conv",
    )(far(projected), far(signal), halo, far(short_filter), far(rate), weight, rt)
    f1 = lax.ppermute(f0, "y", [(i, (i + 1) % 4) for i in range(4)])
    f3 = lax.ppermute(f0, "y", [(i, (i - 1) % 4) for i in range(4)])
    ends, f1, f3, rest, f0_late = lax.optimization_barrier((ends, f1, f3, rest, f0))
    f2 = lax.ppermute(f0_late, "y", [(i, (i + 2) % 4) for i in range(4)])
    mixed = pl.pallas_call(
        mix_kernel,
        out_shape=jax.ShapeDtypeStruct((rows, channels), BF),
        in_specs=[SM] + [VM] * 5,
        out_specs=VM,
        compiler_params=pltpu.CompilerParams(vmem_limit_bytes=10 * 2**20),
        cost_estimate=pl.CostEstimate(flops=10**6, bytes_accessed=2**16, transcendentals=0),
        name="mix",
    )(at, ends, rt, din, far(conv), far(query))

    a_far = lax.ppermute(mixed, "xh", [(0, 1), (1, 0)])
    def given(parts):
        return jnp.concatenate(
            [lax.dynamic_slice(v, (0, (1 - core) * width), (v.shape[0], width)) for v in parts], axis=0
        )

    _, core_late = lax.optimization_barrier((mixed, core))
    w_given = lax.dynamic_slice(out_weight, (0, (xh * 2 + 1 - core_late) * width), (channels, width))
    w_given, mixed_late = lax.optimization_barrier((w_given, mixed))
    a_other = other_core(mixed_late)
    w_other = other_core(w_given)
    g013 = other_core(given((f0_late, f1, f3, rest)))

    tile = 1024
    strips = width // tile

    def strip(shape):
        return pl.BlockSpec(shape[:-1] + (tile,), lambda i, at_ref: (0, i))

    def half_strip(shape):
        return pl.BlockSpec(shape[:-1] + (tile,), lambda i, at_ref: (0, at_ref[3] * strips + i))

    left_specs = [pl.BlockSpec((rows, channels), lambda i, at_ref: (0, 0), **once)] * 2
    near = pl.pallas_call(
        near_kernel,
        out_shape=jax.ShapeDtypeStruct((rows, width), BF),
        grid_spec=pltpu.PrefetchScalarGridSpec(
            num_scalar_prefetch=1,
            grid=(strips,),
            in_specs=left_specs
            + [pl.BlockSpec((channels, tile), lambda i, at_ref: (0, at_ref[2] * strips + i)), strip(w_other.shape)],
            out_specs=strip((rows, width)),
        ),
        compiler_params=pltpu.CompilerParams(vmem_limit_bytes=24 * 2**20),
        cost_estimate=pl.CostEstimate(flops=2 * 10**9, bytes_accessed=6 * 2**20, transcendentals=0),
        name="near",
    )(at, mixed, a_other, far(out_weight), w_other)
    a_far, near, f2 = lax.optimization_barrier((a_far, near, f2))
    g2 = other_core(given((f2,)))
    a_far_other = other_core(a_far)
    partial = pl.pallas_call(
        far_kernel,
        out_shape=pltpu.HBM((rows, width), BF),
        grid_spec=pltpu.PrefetchScalarGridSpec(
            num_scalar_prefetch=1,
            grid=(strips,),
            in_specs=left_specs
            + [half_strip(v.shape) for v in (f0, f1, f2, f3, rest)]
            + [strip(g013.shape), strip(g2.shape)]
            + [strip((rows, width))],
            out_specs=strip((rows, width)),
            scratch_shapes=[pltpu.VMEM((2 * channels, tile), BF)],
        ),
        compiler_params=pltpu.CompilerParams(vmem_limit_bytes=30 * 2**20),
        cost_estimate=pl.CostEstimate(flops=2 * 10**9, bytes_accessed=10 * 2**20, transcendentals=0),
        name="far",
    )(at, a_far, a_far_other, f0_late, f1, f2, f3, rest, g013, g2, near)

    summed = lax.psum_scatter(partial, "z", scatter_dimension=0, tiled=True)
    size = summed.shape[0] // 4

    def traded(k):
        pairs = [(i, i ^ k) for i in range(4)]
        return lax.ppermute(summed[k * size : (k + 1) * size], ("xh", "c"), pairs)

    return pl.pallas_call(
        join_kernel,
        out_shape=jax.ShapeDtypeStruct((size, 4 * width), BF),
        in_specs=[SM] + [VM] * 4,
        out_specs=VM,
        compiler_params=pltpu.CompilerParams(vmem_limit_bytes=4 * 2**20),
        name="join",
    )(at, summed[:size], traded(1), traded(2), traded(3))


def solution(mesh):
    fine = Mesh(mesh.devices.reshape(4, 2, 8, 2, 2), ("y", "xl", "z", "xh", "c"))
    seq, tp = ("y", "xl"), ("z", "xh", "c")
    placed = (P(None, seq, tp), P(None, None, tp), P(tp, None), P(tp, None), P(tp, None))
    return jax.shard_map(local, mesh=fine, in_specs=placed, out_specs=P(seq + tp, None), check_vma=False)
```
